256 devices in a mesh: nbhd: 16 (over y_lo, x, core), sub: 16 (over z, y_hi).
Axes of the slice: x: 4, y: 4 (y_hi: 2, y_lo: 2; y = y_hi * 2 + y_lo), z: 8, core: 2. Of those that a mesh axis runs over, the one named last changes fastest.
Arguments:
- snap_init: bfloat16 [16, 64, 16, 96, 128], P('nbhd', 'sub'), may hold values from -8 to 8
- channel_map: int32 [16, 64, 16, 96], P('nbhd', 'sub'), may hold values from 0 to 3
- yface_vals: bfloat16 [16, 96, 128], P('nbhd'), may hold values from -6 to 6
- zface_vals: bfloat16 [16, 16, 128], P('nbhd'), may hold values from -6 to 6
- face_of: int32 [16, 128], P('nbhd'), may hold values from 0 to 3
- start_block: float32 [16, 128, 32], P('nbhd'), may hold values from -6 to 6
- correlation: int32 [16, 16], replicated, may hold values 0 or 1
Outputs:
- owner_basis: bfloat16 [16, 16, 16, 32, 384], P('nbhd', 'sub')
The draws below stay inside these ranges and needn't reach their ends.
All inputs are finite; a program needn't handle non-finite values.
Results may differ from the reference program's by a relative error of at most 0.0072.
Values may be sent and summed in bfloat16 or wider, within the bound.
A program may use at most 128 MiB of HBM per device.

```python
import math
import jax
import jax.numpy as jnp
from jax import lax

NY = 16
NZ = 96
NSNAP = 128
MODES = 32
SWEEPS = 3
ITERS = 4
NBHDS = 16
NXR = 64
PIECE = 384


def sine_profile(count, waves):
    position = jnp.arange(1, count + 1, dtype=jnp.float32) / (count + 1.0)
    return jnp.sin(math.pi * position[None, :, None] * waves[:, None, :])


def draw_snap_init(key, part):
    shape = (NBHDS, NXR, NY, NZ, NSNAP)
    keys = jax.random.split(key, 6)
    wave_x = jax.random.randint(keys[0], (NBHDS, NSNAP), 1, 7).astype(jnp.float32)
    wave_y = jax.random.randint(keys[1], (NBHDS, NSNAP), 1, 6).astype(jnp.float32)
    wave_z = jax.random.randint(keys[2], (NBHDS, NSNAP), 1, 7).astype(jnp.float32)
    along_x = sine_profile(NXR, wave_x)[:, :, None, None, :]
    along_y = sine_profile(NY, wave_y)[:, None, :, None, :]
    along_z = sine_profile(NZ, wave_z)[:, None, None, :, :]
    smooth = along_x * along_y * along_z
    rough_share = jnp.exp(jax.random.uniform(keys[3], (NBHDS, 1, 1, 1, NSNAP), jnp.float32, math.log(0.1), math.log(0.7)))
    scales = jnp.exp(jax.random.uniform(keys[4], (NBHDS, 1, 1, 1, NSNAP), jnp.float32, math.log(0.3), math.log(3.0)))
    local = jax.random.normal(keys[5], shape, jnp.float32)
    field = smooth + rough_share * local
    return jnp.clip(field * scales, -8.0, 8.0).astype(jnp.bfloat16)


def plant(values, stream_key, least, high):
    place = [jax.random.randint(jax.random.fold_in(stream_key, axis), (), 0, length) for axis, length in enumerate(values.shape)]
    widest = values.shape.index(max(values.shape))
    beside = place[:widest] + [(place[widest] + 1) % values.shape[widest]] + place[widest + 1:]
    return values.at[tuple(place)].set(least).at[tuple(beside)].set(high)


def shard_levels(rng, shape, cuts, smallest, high):
    def one(axis_at, blocks):
        heights = jax.random.uniform(jax.random.fold_in(jax.random.fold_in(rng, 6), axis_at), (blocks,), jnp.float32, smallest / len(cuts), high / len(cuts))
        return jnp.repeat(jnp.exp(heights), shape[axis_at] // blocks).reshape((-1,) + (1,) * (len(shape) - axis_at - 1))

    gain = one(*cuts[0])
    for cut in cuts[1:]:
        gain = gain * one(*cut)
    return gain


def scatter_about(own_key, shape, scale, bound, shards=(), kind=jnp.bfloat16):
    level = shard_levels(own_key, shape, shards, -0.22, 0.18) if shards else 1.0
    result = jax.random.normal(own_key, shape, jnp.float32) * scale * level
    return jnp.minimum(jnp.maximum(result, -bound), bound).astype(kind)


def setup_inputs(seed: int = 0) -> dict:
    seeds = jax.random.split(jax.random.key(seed), 8)
    snap_init = draw_snap_init(jax.random.fold_in(seeds[7], 71), 0)
    channel_map = plant(jax.random.randint(seeds[1], (NBHDS, NXR, NY, NZ), 0, 4), jax.random.fold_in(seeds[1], 1), 0, 3).astype(jnp.int32)
    yface_vals = scatter_about(seeds[2], (NBHDS, NZ, NSNAP), 1.0, 6.0, ((0, 16),))
    zface_vals = scatter_about(seeds[3], (NBHDS, NY, NSNAP), 1.0, 6.0, ((0, 16),))
    face_of = plant(jax.random.randint(seeds[4], (NBHDS, NSNAP), 0, 4), jax.random.fold_in(seeds[4], 1), 0, 3).astype(jnp.int32)
    start_block = scatter_about(seeds[5], (NBHDS, NSNAP, MODES), 1.0, 6.0, ((0, 16),), jnp.float32)
    correlation = plant((jax.random.randint(seeds[6], (NBHDS, NBHDS), 0, 2) < 1).astype(jnp.int32), jax.random.fold_in(seeds[6], 1), 0, 1)
    return {"snap_init": snap_init, "channel_map": channel_map, "yface_vals": yface_vals, "zface_vals": zface_vals, "face_of": face_of, "start_block": start_block, "correlation": correlation}


def harmonic(left_k, right_k):
    return 2.0 * left_k * right_k / (left_k + right_k)

def face_terms(field_ext, kappa_ext, first_plane, plane_count, ghosts):
    length = field_ext.shape[0]
    plane_ids = first_plane + jnp.arange(length, dtype=jnp.int32)
    inside = (plane_ids >= 0) & (plane_ids < plane_count)
    kappa = jnp.where(inside[:, None, None], kappa_ext, jnp.float32(1.0))
    centre = kappa[1:-1]
    x_lower = jnp.where(inside[:-2, None, None], harmonic(centre, kappa[:-2]), centre)
    x_upper = jnp.where(inside[2:, None, None], harmonic(centre, kappa[2:]), centre)
    y_inner = harmonic(centre[:, 1:], centre[:, :-1])
    y_lower = jnp.concatenate([centre[:, :1], y_inner], axis=1)
    y_upper = jnp.concatenate([y_inner, centre[:, -1:]], axis=1)
    z_inner = harmonic(centre[:, :, 1:], centre[:, :, :-1])
    z_lower = jnp.concatenate([centre[:, :, :1], z_inner], axis=2)
    z_upper = jnp.concatenate([z_inner, centre[:, :, -1:]], axis=2)
    middle = field_ext[1:-1].astype(jnp.float32)
    count, rows_y, rows_z, width = middle.shape
    ghost_ylo, ghost_yhi, ghost_zlo, ghost_zhi = ghosts
    below_y = jnp.concatenate([jnp.broadcast_to(ghost_ylo, (count, 1, rows_z, width)), middle[:, :-1]], axis=1)
    above_y = jnp.concatenate([middle[:, 1:], jnp.broadcast_to(ghost_yhi, (count, 1, rows_z, width))], axis=1)
    below_z = jnp.concatenate([jnp.broadcast_to(ghost_zlo[:, None, :], (count, rows_y, 1, width)), middle[:, :, :-1]], axis=2)
    above_z = jnp.concatenate([middle[:, :, 1:], jnp.broadcast_to(ghost_zhi[:, None, :], (count, rows_y, 1, width))], axis=2)
    numer = x_lower[..., None] * field_ext[:-2].astype(jnp.float32) + x_upper[..., None] * field_ext[2:].astype(jnp.float32) + y_lower[..., None] * below_y + y_upper[..., None] * above_y + z_lower[..., None] * below_z + z_upper[..., None] * above_z
    denom = x_lower + x_upper + y_lower + y_upper + z_lower + z_upper
    return (numer, denom, middle, inside[1:-1])

def relax(field_ext, kappa_ext, first_plane, plane_count, ghosts):
    numer, denom, middle, inside = face_terms(field_ext, kappa_ext, first_plane, plane_count, ghosts)
    updated = numer / denom[..., None]
    return jnp.where(inside[:, None, None, None], updated, jnp.float32(0.0)).astype(jnp.bfloat16)

def stiffness(field_ext, kappa_ext, first_plane, plane_count):
    rows_y, rows_z, width = (field_ext.shape[1], field_ext.shape[2], field_ext.shape[3])
    zero_y = jnp.zeros((rows_z, width), jnp.float32)
    zero_z = jnp.zeros((rows_y, width), jnp.float32)
    numer, denom, middle, inside = face_terms(field_ext, kappa_ext, first_plane, plane_count, (zero_y, zero_y, zero_z, zero_z))
    return (denom[..., None] * middle - numer).astype(jnp.bfloat16)

def make_ghosts(y_values, z_values, face_ids):
    y_float = y_values.astype(jnp.float32)
    z_float = z_values.astype(jnp.float32)
    picks = [(face_ids == side).astype(jnp.float32)[None, :] for side in range(4)]
    return (y_float * picks[0], y_float * picks[1], z_float * picks[2], z_float * picks[3])

def gram_terms(snapshots, kappa, stiff_apply):
    width = snapshots.shape[-1]
    flat = snapshots.reshape(-1, width)
    weighted = (flat * (kappa.reshape(-1, 1) / 16.0)).astype(jnp.bfloat16)
    stiff_flat = stiff_apply.reshape(-1, width)
    dims = (((0,), (0,)), ((), ()))
    mass_part = lax.dot_general(flat.astype(jnp.float32), weighted.astype(jnp.float32), dims, preferred_element_type=jnp.float32)
    stiff_part = lax.dot_general(flat.astype(jnp.float32), stiff_flat.astype(jnp.float32), dims, preferred_element_type=jnp.float32)
    return (mass_part, stiff_part)

def subspace(mass_sum, stiff_sum, start, cell_count):
    highest = lax.Precision.HIGHEST
    mass_gram = mass_sum / cell_count
    stiff_gram = (stiff_sum + stiff_sum.T) * (0.5 / cell_count)
    factor = jnp.linalg.cholesky(stiff_gram)
    mode_block = start
    for step in range(ITERS):
        right_side = jnp.dot(mass_gram, mode_block, precision=highest)
        solved = jax.scipy.linalg.cho_solve((factor, True), right_side)
        inner = jnp.dot(solved.T, jnp.dot(mass_gram, solved, precision=highest), precision=highest)
        inner = 0.5 * (inner + inner.T)
        lower = jnp.linalg.cholesky(inner)
        mode_block = jax.scipy.linalg.solve_triangular(lower, solved.T, lower=True).T
    return mode_block

def reference(snap_init, channel_map, yface_vals, zface_vals, face_of, start_block, correlation):

    def single(items):
        init, cmap, y_values, z_values, face_ids, start = items
        plane_count = init.shape[0]
        kappa = jnp.exp2(2.0 * cmap.astype(jnp.float32))
        ghosts = make_ghosts(y_values, z_values, face_ids)
        kappa_ext = jnp.pad(kappa, ((1, 1), (0, 0), (0, 0)))
        pad_spec = ((1, 1), (0, 0), (0, 0), (0, 0))
        state = init
        for sweep_no in range(SWEEPS):
            state = relax(jnp.pad(state, pad_spec), kappa_ext, -1, plane_count, ghosts)
        stiff_apply = stiffness(jnp.pad(state, pad_spec), kappa_ext, -1, plane_count)
        mass_part, stiff_part = gram_terms(state, kappa, stiff_apply)
        cell_count = float(plane_count * state.shape[1] * state.shape[2])
        mode_block = subspace(mass_part, stiff_part, start, cell_count)
        blocks = state.reshape(-1, NBHDS, PIECE, state.shape[-1]).astype(jnp.float32)
        modes_low = mode_block.astype(jnp.bfloat16).astype(jnp.float32)
        basis = jnp.einsum('gpcs,sm->gpmc', blocks, modes_low)
        return basis.astype(jnp.bfloat16)
    built = lax.map(single, (snap_init, channel_map, yface_vals, zface_vals, face_of, start_block))
    mask = correlation.T.astype(jnp.bfloat16)
    return jnp.transpose(built, (2, 1, 0, 3, 4)) * mask[:, None, :, None, None]
```

```python
import functools

import jax
import jax.numpy as jnp
from jax import lax
from jax.experimental import pallas as pl
from jax.experimental.pallas import tpu as pltpu
from jax.sharding import PartitionSpec as P

MESH = pl.DeviceIdType.MESH

SWEEPS = 3
ITERS = 4


def with_halo(cells, sides, width):
    for axis, dim in sides:
        count = lax.axis_size(axis)
        ends = count - 1
        head = lax.slice_in_dim(cells, 0, width, axis=dim)
        tail = lax.slice_in_dim(cells, cells.shape[dim] - width, cells.shape[dim], axis=dim)
        cells = jnp.concatenate(
            [
                lax.ppermute(tail, axis, [(i, (i + 1) % count) for i in range(ends)]),
                cells,
                lax.ppermute(head, axis, [((i + 1) % count, i) for i in range(ends)]),
            ],
            axis=dim,
        )
    return cells


def harmonic(left_k, right_k):
    return 2.0 * left_k * right_k / (left_k + right_k)


def face_terms(field_ext, kappa_ext, first_plane, plane_count, ghosts):
    length = field_ext.shape[0]
    plane_ids = first_plane + jnp.arange(length, dtype=jnp.int32)
    inside = (plane_ids >= 0) & (plane_ids < plane_count)
    kappa = jnp.where(inside[:, None, None], kappa_ext, jnp.float32(1.0))
    centre = kappa[1:-1]
    x_lower = jnp.where(inside[:-2, None, None], harmonic(centre, kappa[:-2]), centre)
    x_upper = jnp.where(inside[2:, None, None], harmonic(centre, kappa[2:]), centre)
    y_inner = harmonic(centre[:, 1:], centre[:, :-1])
    y_lower = jnp.concatenate([centre[:, :1], y_inner], axis=1)
    y_upper = jnp.concatenate([y_inner, centre[:, -1:]], axis=1)
    z_inner = harmonic(centre[:, :, 1:], centre[:, :, :-1])
    z_lower = jnp.concatenate([centre[:, :, :1], z_inner], axis=2)
    z_upper = jnp.concatenate([z_inner, centre[:, :, -1:]], axis=2)
    middle = field_ext[1:-1].astype(jnp.float32)
    count, rows_y, rows_z, width = middle.shape
    ghost_ylo, ghost_yhi, ghost_zlo, ghost_zhi = ghosts
    below_y = jnp.concatenate(
        [jnp.broadcast_to(ghost_ylo, (count, 1, rows_z, width)), middle[:, :-1]], axis=1
    )
    above_y = jnp.concatenate(
        [middle[:, 1:], jnp.broadcast_to(ghost_yhi, (count, 1, rows_z, width))], axis=1
    )
    below_z = jnp.concatenate(
        [jnp.broadcast_to(ghost_zlo[:, None, :], (count, rows_y, 1, width)), middle[:, :, :-1]],
        axis=2,
    )
    above_z = jnp.concatenate(
        [middle[:, :, 1:], jnp.broadcast_to(ghost_zhi[:, None, :], (count, rows_y, 1, width))],
        axis=2,
    )
    numer = (
        x_lower[..., None] * field_ext[:-2].astype(jnp.float32)
        + x_upper[..., None] * field_ext[2:].astype(jnp.float32)
        + y_lower[..., None] * below_y
        + y_upper[..., None] * above_y
        + z_lower[..., None] * below_z
        + z_upper[..., None] * above_z
    )
    denom = x_lower + x_upper + y_lower + y_upper + z_lower + z_upper
    return (numer, denom, middle, inside[1:-1])


def relax(field_ext, kappa_ext, first_plane, plane_count, ghosts):
    numer, denom, middle, inside = face_terms(
        field_ext, kappa_ext, first_plane, plane_count, ghosts
    )
    updated = numer / denom[..., None]
    return jnp.where(inside[:, None, None, None], updated, jnp.float32(0.0)).astype(jnp.bfloat16)


def stiffness(field_ext, kappa_ext, first_plane, plane_count):
    rows_y, rows_z, width = (field_ext.shape[1], field_ext.shape[2], field_ext.shape[3])
    zero_y = jnp.zeros((rows_z, width), jnp.float32)
    zero_z = jnp.zeros((rows_y, width), jnp.float32)
    numer, denom, middle, inside = face_terms(
        field_ext, kappa_ext, first_plane, plane_count, (zero_y, zero_y, zero_z, zero_z)
    )
    return (denom[..., None] * middle - numer).astype(jnp.bfloat16)


def make_ghosts(y_values, z_values, face_ids):
    y_float = y_values.astype(jnp.float32)
    z_float = z_values.astype(jnp.float32)
    picks = [(face_ids == side).astype(jnp.float32)[None, :] for side in range(4)]
    return (y_float * picks[0], y_float * picks[1], z_float * picks[2], z_float * picks[3])


def gram_terms(snapshots, kappa, stiff_apply):
    width = snapshots.shape[-1]
    flat = snapshots.reshape(-1, width)
    weighted = (flat * (kappa.reshape(-1, 1) / 16.0)).astype(jnp.bfloat16)
    stiff_flat = stiff_apply.reshape(-1, width)
    dims = (((0,), (0,)), ((), ()))
    mass_part = lax.dot_general(flat, weighted, dims, preferred_element_type=jnp.float32)
    stiff_part = lax.dot_general(flat, stiff_flat, dims, preferred_element_type=jnp.float32)
    return (mass_part, stiff_part)


def eliminate_spd(full, size, block):
    lanes = lax.broadcasted_iota(jnp.int32, (block, size), 1)
    rows = lax.broadcasted_iota(jnp.int32, (block, size), 0)
    wide = lax.broadcasted_iota(jnp.int32, (size, size), 1)
    for first in range(0, size, block):
        panel = full[first:first + block]
        signed = jnp.where(lanes < first, -panel, panel) if first else panel
        for i in range(block):
            col = first + i
            column = panel[:, col:col + 1]
            pivot = 1.0 / panel[i:i + 1, col:col + 1]
            row = jnp.where(lanes[:1] == col, 1.0, panel[i:i + 1]) * pivot
            cleared = jnp.where(lanes == col, 0.0, panel)
            panel = jnp.where(rows == i, row, cleared - column * row)
        inside = (wide >= first) & (wide < first + block)
        update = lax.dot_general(
            signed, panel, (((0,), (0,)), ((), ())),
            precision=lax.Precision.HIGHEST, preferred_element_type=jnp.float32,
        )
        rest = jnp.where(inside, 0.0, full) - update
        parts = []
        if first:
            parts.append(rest[:first])
        parts.append(panel)
        if first + block < size:
            parts.append(rest[first + block:])
        full = jnp.concatenate(parts, axis=0)
    return full


def normalize(inner, vectors):
    count = inner.shape[0]
    rows = lax.broadcasted_iota(jnp.int32, (count, 1), 0)
    eye = lax.broadcasted_iota(jnp.int32, (count, count), 0) == lax.broadcasted_iota(
        jnp.int32, (count, count), 1
    )
    for i in range(count - 1):
        factor = inner[:, i:i + 1] * (1.0 / inner[i:i + 1, i:i + 1])
        factor = jnp.where(rows > i, factor, 0.0)
        lead, mate = inner[i:i + 1], vectors[i:i + 1]
        inner = inner - factor * lead
        vectors = vectors - factor * mate
    diagonal = jnp.sum(jnp.where(eye, inner, 0.0), axis=1, keepdims=True)
    return vectors / jnp.sqrt(diagonal)


def modes_kernel(
    snaps_ref, gram_ref, start_ref, corr_ref, out_ref,
    slots, summed, total, stage, send_sem, recv_sem, send_two, recv_two, send_out, recv_out,
    *, members, owners, cell_count,
):
    me_sub = lax.axis_index("sub")
    me_nbhd = lax.axis_index("nbhd")
    size = gram_ref.shape[1]
    chunk = 2 * size // members

    def sub_at(step):
        return lax.rem(me_sub + step, members)

    def owner_at(step):
        return lax.rem(me_nbhd + step, owners)

    barrier = pltpu.get_barrier_semaphore()
    for step in range(1, members):
        pl.semaphore_signal(barrier, inc=1, device_id=(me_nbhd, sub_at(step)), device_id_type=MESH)
    for step in range(1, owners):
        pl.semaphore_signal(barrier, inc=1, device_id=(owner_at(step), me_sub), device_id_type=MESH)
    pl.semaphore_wait(barrier, members - 1 + owners - 1)

    def part(owner):
        return pl.ds(pl.multiple_of(owner * chunk, chunk), chunk)

    copies = []
    for step in range(1, members):
        peer = sub_at(step)
        copy = pltpu.make_async_remote_copy(
            src_ref=gram_ref.at[part(peer)],
            dst_ref=slots.at[step],
            send_sem=send_sem.at[step],
            recv_sem=recv_sem.at[step],
            device_id=(me_nbhd, peer),
            device_id_type=MESH,
        )
        copy.start()
        copies.append(copy)
    acc = gram_ref[part(me_sub)]
    for step in range(1, members):
        copies[step - 1].wait_recv()
        acc = acc + slots[step]
    summed[...] = acc
    total[part(me_sub)] = acc
    spread = []
    for step in range(1, members):
        copy = pltpu.make_async_remote_copy(
            src_ref=summed,
            dst_ref=total.at[part(me_sub)],
            send_sem=send_two.at[step],
            recv_sem=recv_two.at[step],
            device_id=(me_nbhd, sub_at(step)),
            device_id_type=MESH,
        )
        copy.start()
        spread.append(copy)
    for copy in spread:
        copy.wait_recv()

    dot = functools.partial(
        lax.dot_general, precision=lax.Precision.HIGHEST, preferred_element_type=jnp.float32
    )
    mass = total[:size] / cell_count
    stiff = total[size:]
    stiff = (stiff + stiff.T) * (0.5 / cell_count)
    inverse = eliminate_spd(stiff, size, 32)
    step_map = dot(mass, inverse, (((1,), (0,)), ((), ())))
    both = jnp.concatenate([step_map, dot(step_map, mass, (((1,), (0,)), ((), ())))], axis=1)
    rows = None
    for turn in range(ITERS):
        if turn == 0:
            pair = dot(start_ref[...], both, (((0,), (0,)), ((), ())))
        else:
            pair = dot(rows, both, (((1,), (0,)), ((), ())))
        solved, image = pair[:, :size], pair[:, size:]
        inner = dot(solved, image, (((1,), (1,)), ((), ())))
        inner = 0.5 * (inner + inner.T)
        rows = normalize(inner, solved)
    modes = rows.astype(jnp.bfloat16)

    def piece(owner):
        values = lax.dot_general(
            modes, snaps_ref[owner], (((1,), (1,)), ((), ())), preferred_element_type=jnp.float32
        )
        return (values * corr_ref[me_nbhd, owner].astype(jnp.float32)).astype(jnp.bfloat16)

    leaving = []
    for step in range(1, owners):
        owner = owner_at(step)
        stage[step] = piece(owner)
        copy = pltpu.make_async_remote_copy(
            src_ref=stage.at[step],
            dst_ref=out_ref.at[me_nbhd],
            send_sem=send_out.at[step],
            recv_sem=recv_out.at[step],
            device_id=(owner, me_sub),
            device_id_type=MESH,
        )
        copy.start()
        leaving.append(copy)
    out_ref[me_nbhd] = piece(me_nbhd)
    for copy in leaving:
        copy.wait_recv()
    for copy in copies + spread + leaving:
        copy.wait_send()


def modes_and_pieces(snaps, gram, start, corr, members, owners, cell_count):
    pieces, cells, size = snaps.shape
    modes = start.shape[1]
    vmem = pl.BlockSpec(memory_space=pltpu.VMEM)
    return pl.pallas_call(
        functools.partial(modes_kernel, members=members, owners=owners, cell_count=cell_count),
        out_shape=jax.ShapeDtypeStruct((owners, modes, cells), jnp.bfloat16),
        in_specs=[vmem, vmem, vmem, pl.BlockSpec(memory_space=pltpu.SMEM)],
        out_specs=vmem,
        scratch_shapes=[
            pltpu.VMEM((members, 2 * size // members, size), jnp.float32),
            pltpu.VMEM((2 * size // members, size), jnp.float32),
            pltpu.VMEM((2 * size, size), jnp.float32),
            pltpu.VMEM((owners, modes, cells), jnp.bfloat16),
            pltpu.SemaphoreType.DMA((members,)),
            pltpu.SemaphoreType.DMA((members,)),
            pltpu.SemaphoreType.DMA((members,)),
            pltpu.SemaphoreType.DMA((members,)),
            pltpu.SemaphoreType.DMA((owners,)),
            pltpu.SemaphoreType.DMA((owners,)),
        ],
        compiler_params=pltpu.CompilerParams(
            collective_id=1, has_side_effects=True, vmem_limit_bytes=32 << 20
        ),
    )(snaps, gram, start, corr)


def on_device(snap_init, channel_map, yface_vals, zface_vals, face_of, start_block, correlation):
    initial = snap_init[0]
    class_map = channel_map[0]
    planes = initial.shape[0]
    plane_count = planes * lax.axis_size("sub")
    base_plane = lax.axis_index("sub") * planes
    ghosts = make_ghosts(yface_vals[0], zface_vals[0], face_of[0])
    class_ext = with_halo(class_map, (("sub", 0),), 1)
    kappa_edge = jnp.exp2(2.0 * class_ext.astype(jnp.float32))
    state = initial
    for sweep_no in range(SWEEPS):
        padded = with_halo(state, (("sub", 0),), 1)
        state = relax(padded, kappa_edge, base_plane - 1, plane_count, ghosts)
    field_edge = with_halo(state, (("sub", 0),), 1)
    snapshots = field_edge[1:-1]
    kappa_local = kappa_edge[1:-1]
    stiff_apply = stiffness(field_edge, kappa_edge, base_plane - 1, plane_count)
    mass_part, stiff_part = gram_terms(snapshots, kappa_local, stiff_apply)
    cell_count = float(plane_count * snapshots.shape[1] * snapshots.shape[2])
    owner_count = lax.axis_size("nbhd")
    width = snapshots.shape[-1]
    piece_cells = snapshots.size // width // owner_count
    blocks = snapshots.reshape(owner_count, piece_cells, width)
    result = modes_and_pieces(
        blocks, jnp.concatenate([mass_part, stiff_part]), start_block[0], correlation,
        lax.axis_size("sub"), owner_count, cell_count,
    )
    return result[None, None]


def solution(mesh):
    return jax.shard_map(
        on_device,
        mesh=mesh,
        in_specs=(
            P("nbhd", "sub", None, None, None),
            P("nbhd", "sub", None, None),
            P("nbhd", None, None),
            P("nbhd", None, None),
            P("nbhd", None),
            P("nbhd", None, None),
            P(),
        ),
        out_specs=P("nbhd", "sub", None, None, None),
        check_vma=False,
    )
```

```python
import functools

import jax
import jax.numpy as jnp
from jax import lax
from jax.experimental import pallas as pl
from jax.experimental.pallas import tpu as pltpu
from jax.sharding import PartitionSpec as P

MESH = pl.DeviceIdType.MESH

SWEEPS = 3
ITERS = 4


def harmonic(left_k, right_k):
    return 2.0 * left_k * right_k / (left_k + right_k)


def relax_kernel(
    snap_ref, class_ref, yface_ref, zface_ref, face_ref, state_ref, gram_ref,
    field, coef, compact, kappa, ghost_z, early, swap, zland, yland, rhs,
    class_pair, class_low, class_high,
    swap_send, swap_recv, z_send, z_recv, y_send, y_recv, class_send, class_recv,
    *, members,
):
    me_nbhd = lax.axis_index("nbhd")
    me = lax.axis_index("sub")
    half = lax.rem(me, 2)
    tower = me // 2
    towers = members // 2
    own, rows_all, depth, width = snap_ref.shape
    both = 2 * own
    rows = rows_all // 2
    top = both + 1
    base = 8
    inner = pl.ds(base, depth)

    def at(sub):
        return (me_nbhd, lax.rem(sub + members, members))

    partner = at(me + 1 - 2 * half)
    cross = at(me - 1 + 2 * half)
    lower = at(me - 2)
    upper = at(me + 2)

    def remote(src, dst, send, recv, device):
        return pltpu.make_async_remote_copy(
            src_ref=src, dst_ref=dst, send_sem=send, recv_sem=recv,
            device_id=device, device_id_type=MESH,
        )

    barrier = pltpu.get_barrier_semaphore()
    for device in (partner, cross, lower, upper):
        pl.semaphore_signal(barrier, inc=1, device_id=device, device_id_type=MESH)
    pl.semaphore_wait(barrier, 4)

    class_copies = [
        remote(class_ref, class_pair, class_send.at[0], class_recv.at[0], partner),
    ]
    class_copies[0].start()
    class_other = []

    def class_sends(plane, land, slot, devices):
        made = []
        for place, device in enumerate(devices):
            made.append(remote(
                class_ref.at[plane], land, class_send.at[1 + place], class_recv.at[slot], device
            ))
        return made

    @pl.when(half == 0)
    def _():
        for copy in class_sends(0, class_high, 2, (lower, cross)):
            copy.start()

    @pl.when(half == 1)
    def _():
        for copy in class_sends(own - 1, class_low, 1, (upper, cross)):
            copy.start()

    order = [0] + list(range(own - 1, 0, -1))
    swaps = []
    for turn, q in enumerate(order):
        plane = q + half * (own - 1 - 2 * q)
        copy = remote(
            snap_ref.at[plane, pl.ds((rows - 1) * (1 - half), rows + 1)],
            swap.at[turn], swap_send.at[turn], swap_recv.at[turn], partner,
        )
        copy.start()
        swaps.append(copy)

    @pl.when(half == 0)
    def _():
        remote(
            snap_ref.at[0, pl.ds(0, rows)], zland.at[0, 1], z_send.at[0, 0], z_recv.at[0, 1], lower
        ).start()

    @pl.when(half == 1)
    def _():
        remote(
            snap_ref.at[own - 1, pl.ds(rows, rows)], zland.at[0, 0], z_send.at[0, 1],
            z_recv.at[0, 0], upper
        ).start()

    shift = 1 - half

    def fill_own(p, _):
        def fill(r, _):
            field[0, 1 + own * half + p, shift + r, inner, :] = snap_ref[
                p, (rows - 1) * half + r
            ].astype(jnp.float32)
            return 0
        return lax.fori_loop(0, rows + 1, fill, 0)

    lax.fori_loop(0, own, fill_own, 0)

    face = face_ref[...]

    def pick(side):
        return jnp.where(face == side, 1.0, 0.0)

    side_y = jnp.where(half == 0, pick(0), pick(1))
    ghost_y = yface_ref[...].astype(jnp.float32) * side_y
    zface = zface_ref[...].astype(jnp.float32)
    ghost_z[0] = zface * pick(2)
    ghost_z[1] = zface * pick(3)

    def set_ghosts(p, _):
        for buf in range(2):
            field[buf, p + 1, (rows + 1) * half, inner, :] = ghost_y

            def one(y, _):
                field[buf, p + 1, y + 1, pl.ds(base - 1, 1), :] = ghost_z[0, pl.ds(rows * half + y, 1), :]
                field[buf, p + 1, y + 1, pl.ds(base + depth, 1), :] = ghost_z[1, pl.ds(rows * half + y, 1), :]
                return 0

            lax.fori_loop(0, rows, one, 0)
        return 0

    lax.fori_loop(0, both, set_ghosts, 0)

    def to_kappa(classes):
        return jnp.left_shift(1, 2 * classes).astype(jnp.float32)

    def land(slot, ref):
        remote(ref, ref, class_send.at[0], class_recv.at[slot], partner).wait_recv()

    land(0, class_pair)
    land(1, class_low)
    land(2, class_high)
    kappa[0] = to_kappa(class_low[...])
    kappa[top] = to_kappa(class_high[...])
    for p in range(own):
        kappa[1 + own * half + p] = to_kappa(class_ref[p])
        kappa[1 + own * (1 - half) + p] = to_kappa(class_pair[p])

    def coefficients(p, _):
        centre = kappa[p + 1]
        has_low = jnp.logical_or(tower > 0, p > 0)
        has_high = jnp.logical_or(tower < towers - 1, p < both - 1)
        face_low = harmonic(centre, kappa[p])
        face_high = harmonic(centre, kappa[p + 2])
        x_lower = jnp.where(has_low, face_low, centre)
        x_upper = jnp.where(has_high, face_high, centre)
        y_inner = harmonic(centre[1:], centre[:-1])
        y_lower = jnp.concatenate([centre[:1], y_inner], axis=0)
        y_upper = jnp.concatenate([y_inner, centre[-1:]], axis=0)
        z_inner = harmonic(centre[:, 1:], centre[:, :-1])
        z_lower = jnp.concatenate([centre[:, :1], z_inner], axis=1)
        z_upper = jnp.concatenate([z_inner, centre[:, -1:]], axis=1)
        denom = x_lower + x_upper + y_lower + y_upper + z_lower + z_upper
        inverse = 1.0 / denom
        compact[0] = jnp.where(has_low, face_low, 0.0) * inverse
        compact[1] = jnp.where(has_high, face_high, 0.0) * inverse
        compact[2] = y_lower * inverse
        compact[3] = y_upper * inverse
        compact[4] = z_lower * inverse
        compact[5] = z_upper * inverse
        compact[6] = denom
        compact[7] = centre * (1.0 / 16.0)
        first = pl.multiple_of(rows * half, rows)
        for kind in range(8):
            turned = compact[kind, pl.ds(first, rows), :].T
            for y in range(rows):
                coef[kind, p, y] = jnp.broadcast_to(turned[:, y:y + 1], (depth, width))
        return 0

    lax.fori_loop(0, both, coefficients, 0)

    def row(sweep, p, y):
        src, dst = (sweep + 1) % 2, sweep % 2
        c = [coef.at[kind, p - 1, y - 1] for kind in range(6)]
        value = c[0][...] * field[src, p - 1, y, inner, :]
        value += c[1][...] * field[src, p + 1, y, inner, :]
        value += c[2][...] * field[src, p, y - 1, inner, :]
        value += c[3][...] * field[src, p, y + 1, inner, :]
        value += c[4][...] * field[src, p, y, pl.ds(base - 1, depth), :]
        value += c[5][...] * field[src, p, y, pl.ds(base + 1, depth), :]
        low = value.astype(jnp.bfloat16)
        field[dst, p, y, inner, :] = low.astype(jnp.float32)
        if sweep < SWEEPS:
            early[sweep - 1, p - 1, y - 1] = low
        else:
            state_ref[p - 1, y - 1] = low
            field[dst, p, y, pl.ds(base + depth, 1), :] = jnp.zeros((1, width), jnp.float32)

    def line(sweep, p, first, count):
        def body(i, _):
            row(sweep, p, first + i)
            return 0
        lax.fori_loop(0, count, body, 0)

    def fill_z(buf, round_no, side):
        remote(
            zland.at[round_no, side], zland.at[round_no, side], z_send.at[round_no, side],
            z_recv.at[round_no, side], lower,
        ).wait_recv()

        def fill(y, _):
            field[buf, top * side, y + 1, inner, :] = zland[round_no, side, y].astype(jnp.float32)
            return 0
        lax.fori_loop(0, rows, fill, 0)

    def plane_of(e):
        return e + (1 - half) * (top - 2 * e)

    for e in range(own + 2, both):
        line(1, plane_of(e), 1, rows)
    for turn, q in enumerate(order):
        swaps[turn].wait_recv()
        plane = q + (1 - half) * (own - 1 - 2 * q)
        if turn == 0:
            @pl.when(half == 0)
            def _():
                remote(
                    swap.at[0, pl.ds(0, rows)], zland.at[0, 0], z_send.at[0, 1], z_recv.at[0, 0], upper
                ).start()

            @pl.when(half == 1)
            def _():
                remote(
                    swap.at[0, pl.ds(1, rows)], zland.at[0, 1], z_send.at[0, 0], z_recv.at[0, 1], lower
                ).start()

        def fill(r, _):
            field[0, 1 + own * (1 - half) + plane, shift + r, inner, :] = swap[turn, r].astype(
                jnp.float32
            )
            return 0

        lax.fori_loop(0, rows + 1, fill, 0)
        if turn >= 1:
            line(1, plane_of(q + 2), 1, rows)
    line(1, plane_of(2), 1, rows)
    fill_z(0, 0, 0)
    line(1, 1, 1, rows)
    fill_z(0, 0, 1)
    line(1, both, 1, rows)

    edge = rows - (rows - 1) * half
    started = []

    def send_edges(sweep):
        held = early.at[sweep - 1] if sweep < SWEEPS else state_ref
        copies = [
            remote(held.at[0], zland.at[sweep, 1], z_send.at[sweep, 0], z_recv.at[sweep, 1], lower),
        ]
        if sweep < SWEEPS:
            copies.append(remote(
                held.at[both - 1], zland.at[sweep, 0], z_send.at[sweep, 1], z_recv.at[sweep, 0], upper
            ))
        ycopy = remote(
            held.at[pl.ds(0, both), edge - 1], yland.at[sweep - 1], y_send.at[sweep - 1],
            y_recv.at[sweep - 1], partner,
        )
        if sweep < SWEEPS:
            copies.append(ycopy)
        for copy in copies:
            copy.start()
        started.extend(copies)
        return ycopy

    def fill_y(buf, sweep, ycopy):
        ycopy.wait_recv()

        def fill(p, _):
            field[buf, p + 1, (rows + 1) * (1 - half), inner, :] = yland[sweep - 1, p].astype(jnp.float32)
            return 0
        lax.fori_loop(0, both, fill, 0)

    for sweep in range(2, SWEEPS + 1):
        ycopy = send_edges(sweep - 1)
        src = (sweep + 1) % 2

        def middle(i, _):
            line(sweep, i + 2, 1 + half, rows - 1)
            return 0
        lax.fori_loop(0, both - 2, middle, 0)
        fill_y(src, sweep - 1, ycopy)

        def border(i, _):
            row(sweep, i + 2, edge)
            return 0
        lax.fori_loop(0, both - 2, border, 0)
        fill_z(src, sweep - 1, 0)
        line(sweep, 1, 1, rows)
        fill_z(src, sweep - 1, 1)
        line(sweep, both, 1, rows)

    ycopy = send_edges(SWEEPS)

    @pl.when(half == 1)
    def _():
        ycopy.start()

    last = SWEEPS % 2

    def stiff_row(p, y, place):
        here = field[last, p, y, inner, :]
        ahead = coef[1, p - 1, y - 1] * field[last, p + 1, y, inner, :]
        ahead += coef[3, p - 1, y - 1] * field[last, p, y + 1, inner, :]
        ahead += coef[5, p - 1, y - 1] * field[last, p, y, pl.ds(base + 1, depth), :]
        value = coef[6, p - 1, y - 1] * (here - 2.0 * ahead)
        high = value.astype(jnp.bfloat16)
        rest = (value - high.astype(jnp.float32)).astype(jnp.bfloat16)
        rhs[place, :, pl.ds(0, width)] = (here * coef[7, p - 1, y - 1]).astype(jnp.bfloat16)
        rhs[place, :, pl.ds(width, width)] = high
        rhs[place, :, pl.ds(2 * width, width)] = rest

    def gram(left, count):
        right = rhs[pl.ds(0, count)].reshape(count * depth, 3 * width)
        part = lax.dot_general(
            left.reshape(count * depth, width), right, (((0,), (0,)), ((), ())),
            preferred_element_type=jnp.float32,
        )
        gram_ref[pl.ds(0, width), :] += part[:, :width]
        gram_ref[pl.ds(width, width), :] += part[:, width:2 * width] + part[:, 2 * width:]

    gram_ref[...] = jnp.zeros_like(gram_ref)

    def inside(i, _):
        def body(y, _):
            stiff_row(i + 1, y + 1, y)
            return 0
        lax.fori_loop(0, rows - 1, body, 0)
        gram(state_ref[i, pl.ds(0, rows - 1)], rows - 1)
        return 0
    lax.fori_loop(0, both - 1, inside, 0)

    @pl.when(half == 0)
    def _():
        fill_y(last, SWEEPS, ycopy)

    @pl.when(half == 1)
    def _():
        def clear(p, _):
            field[last, p + 1, rows + 1, inner, :] = jnp.zeros((depth, width), jnp.float32)
            return 0
        lax.fori_loop(0, both, clear, 0)

    def side(i, _):
        stiff_row(i + 1, rows, i)
        return 0
    lax.fori_loop(0, both - 1, side, 0)
    gram(state_ref[pl.ds(0, both - 1), rows - 1], both - 1)
    fill_z(last, SWEEPS, 1)

    def roof(y, _):
        stiff_row(both, y + 1, y)
        return 0
    lax.fori_loop(0, rows, roof, 0)
    gram(state_ref[both - 1], rows)

    class_copies[0].wait_send()
    for place in range(2):
        remote(
            class_ref.at[0], class_low, class_send.at[1 + place], class_recv.at[1], partner
        ).wait_send()
    for copy in swaps:
        copy.wait_send()
    for direction in range(2):
        remote(
            snap_ref.at[0, pl.ds(0, rows)], zland.at[0, 0], z_send.at[0, direction], z_recv.at[0, 0], lower
        ).wait_send()
    for copy in started:
        copy.wait_send()

    @pl.when(half == 1)
    def _():
        ycopy.wait_send()


def relax_and_gram(snap, classes, yface, zface, face, members):
    own, rows_all, depth, width = snap.shape
    both, rows = 2 * own, rows_all // 2
    vmem = pl.BlockSpec(memory_space=pltpu.VMEM)
    f32, bf16 = jnp.float32, jnp.bfloat16
    dma = pltpu.SemaphoreType.DMA
    return pl.pallas_call(
        functools.partial(relax_kernel, members=members),
        out_shape=(
            jax.ShapeDtypeStruct((both, rows, depth, width), bf16),
            jax.ShapeDtypeStruct((2 * width, width), f32),
        ),
        in_specs=[vmem] * 5,
        out_specs=(vmem, vmem),
        scratch_shapes=[
            pltpu.VMEM((2, both + 2, rows + 2, depth + 16, width), f32),
            pltpu.VMEM((8, both, rows, depth, width), f32),
            pltpu.VMEM((8, rows_all, depth), f32),
            pltpu.VMEM((both + 2, rows_all, depth), f32),
            pltpu.VMEM((2, rows_all, width), f32),
            pltpu.VMEM((SWEEPS - 1, both, rows, depth, width), bf16),
            pltpu.VMEM((own, rows + 1, depth, width), bf16),
            pltpu.VMEM((SWEEPS + 1, 2, rows, depth, width), bf16),
            pltpu.VMEM((SWEEPS, both, depth, width), bf16),
            pltpu.VMEM((max(both, rows), depth, 3 * width), bf16),
            pltpu.VMEM((own, rows_all, depth), jnp.int32),
            pltpu.VMEM((rows_all, depth), jnp.int32),
            pltpu.VMEM((rows_all, depth), jnp.int32),
            dma((own,)),
            dma((own,)),
            dma((SWEEPS + 1, 2)),
            dma((SWEEPS + 1, 2)),
            dma((SWEEPS,)),
            dma((SWEEPS,)),
            dma((3,)),
            dma((3,)),
        ],
        compiler_params=pltpu.CompilerParams(
            collective_id=0, has_side_effects=True, vmem_limit_bytes=60 << 20
        ),
    )(snap, classes, yface, zface, face)


def eliminate_spd(full, size, block):
    lanes = lax.broadcasted_iota(jnp.int32, (block, size), 1)
    rows = lax.broadcasted_iota(jnp.int32, (block, size), 0)
    wide = lax.broadcasted_iota(jnp.int32, (size, size), 1)
    for first in range(0, size, block):
        panel = full[first:first + block]
        signed = jnp.where(lanes < first, -panel, panel) if first else panel
        for i in range(block):
            col = first + i
            column = panel[:, col:col + 1]
            pivot = 1.0 / panel[i:i + 1, col:col + 1]
            row = jnp.where(lanes[:1] == col, 1.0, panel[i:i + 1]) * pivot
            cleared = jnp.where(lanes == col, 0.0, panel)
            panel = jnp.where(rows == i, row, cleared - column * row)
        inside = (wide >= first) & (wide < first + block)
        update = lax.dot_general(
            signed, panel, (((0,), (0,)), ((), ())),
            precision=lax.Precision.HIGHEST, preferred_element_type=jnp.float32,
        )
        rest = jnp.where(inside, 0.0, full) - update
        parts = []
        if first:
            parts.append(rest[:first])
        parts.append(panel)
        if first + block < size:
            parts.append(rest[first + block:])
        full = jnp.concatenate(parts, axis=0)
    return full


def normalize(inner, vectors):
    count = inner.shape[0]
    rows = lax.broadcasted_iota(jnp.int32, (count, 1), 0)
    eye = lax.broadcasted_iota(jnp.int32, (count, count), 0) == lax.broadcasted_iota(
        jnp.int32, (count, count), 1
    )
    for i in range(count - 1):
        factor = inner[:, i:i + 1] * (1.0 / inner[i:i + 1, i:i + 1])
        factor = jnp.where(rows > i, factor, 0.0)
        lead, mate = inner[i:i + 1], vectors[i:i + 1]
        inner = inner - factor * lead
        vectors = vectors - factor * mate
    diagonal = jnp.sum(jnp.where(eye, inner, 0.0), axis=1, keepdims=True)
    return vectors / jnp.sqrt(diagonal)


def modes_kernel(
    snaps_ref, gram_ref, start_ref, corr_ref, out_ref,
    slots, summed, total, stage, send_sem, recv_sem, send_two, recv_two, send_out, recv_out,
    *, members, owners, own, cell_count,
):
    me_sub = lax.axis_index("sub")
    me_nbhd = lax.axis_index("nbhd")
    size = gram_ref.shape[1]
    chunk = 2 * size // members

    def sub_at(step):
        return lax.rem(me_sub + step, members)

    half = lax.rem(me_sub, 2)
    tower = me_sub - half
    planes = own
    across = owners // planes
    mine = across // 2
    from_half = lax.rem(me_nbhd, across) // mine
    whole = jnp.where(from_half == half, 1, 0)

    barrier = pltpu.get_barrier_semaphore()
    for step in range(1, members):
        pl.semaphore_signal(barrier, inc=1, device_id=(me_nbhd, sub_at(step)), device_id_type=MESH)

    def is_me(nbhd):
        return jnp.logical_and(nbhd == me_nbhd, from_half == half)

    for nbhd in range(owners):
        @pl.when(jnp.logical_not(is_me(nbhd)))
        def _():
            pl.semaphore_signal(
                barrier, inc=1, device_id=(nbhd, tower + from_half), device_id_type=MESH
            )
    pl.semaphore_wait(barrier, members - 1 + owners - whole)

    def part(owner):
        return pl.ds(pl.multiple_of(owner * chunk, chunk), chunk)

    copies = []
    for step in range(1, members):
        peer = sub_at(step)
        copy = pltpu.make_async_remote_copy(
            src_ref=gram_ref.at[part(peer)],
            dst_ref=slots.at[step],
            send_sem=send_sem.at[step],
            recv_sem=recv_sem.at[step],
            device_id=(me_nbhd, peer),
            device_id_type=MESH,
        )
        copy.start()
        copies.append(copy)
    acc = gram_ref[part(me_sub)]
    for step in range(1, members):
        copies[step - 1].wait_recv()
        acc = acc + slots[step]
    summed[...] = acc
    total[part(me_sub)] = acc
    spread = []
    for step in range(1, members):
        copy = pltpu.make_async_remote_copy(
            src_ref=summed,
            dst_ref=total.at[part(me_sub)],
            send_sem=send_two.at[step],
            recv_sem=recv_two.at[step],
            device_id=(me_nbhd, sub_at(step)),
            device_id_type=MESH,
        )
        copy.start()
        spread.append(copy)
    for copy in spread:
        copy.wait_recv()

    dot = functools.partial(
        lax.dot_general, precision=lax.Precision.HIGHEST, preferred_element_type=jnp.float32
    )
    mass = total[:size] / cell_count
    stiff = total[size:]
    stiff = (stiff + stiff.T) * (0.5 / cell_count)
    inverse = eliminate_spd(stiff, size, 32)
    step_map = dot(mass, inverse, (((1,), (0,)), ((), ())))
    both = jnp.concatenate([step_map, dot(step_map, mass, (((1,), (0,)), ((), ())))], axis=1)
    rows = None
    for turn in range(ITERS):
        if turn == 0:
            pair = dot(start_ref[...], both, (((0,), (0,)), ((), ())))
        else:
            pair = dot(rows, both, (((1,), (0,)), ((), ())))
        solved, image = pair[:, :size], pair[:, size:]
        inner = dot(solved, image, (((1,), (1,)), ((), ())))
        inner = 0.5 * (inner + inner.T)
        rows = normalize(inner, solved)
    modes = rows.astype(jnp.bfloat16)

    def piece(index, owner):
        values = lax.dot_general(
            modes, snaps_ref[index], (((1,), (1,)), ((), ())), preferred_element_type=jnp.float32
        )
        return (values * corr_ref[me_nbhd, owner].astype(jnp.float32)).astype(jnp.bfloat16)

    def leave(step, owner, sub):
        return pltpu.make_async_remote_copy(
            src_ref=stage.at[step],
            dst_ref=out_ref.at[me_nbhd],
            send_sem=send_out.at[step],
            recv_sem=recv_out.at[me_nbhd],
            device_id=(owner, sub),
            device_id_type=MESH,
        )

    leaving = []
    for step in range(owners):
        index = lax.rem(step + me_nbhd, owners)
        level = index // mine
        owner = across * lax.rem(level, planes) + mine * half + lax.rem(index, mine)
        sub = tower + level // planes
        here = jnp.logical_and(owner == me_nbhd, sub == me_sub)
        stage[step] = piece(index, owner)

        @pl.when(jnp.logical_not(here))
        def _():
            leave(step, owner, sub).start()

        @pl.when(here)
        def _():
            out_ref[me_nbhd] = stage[step]

        leaving.append((step, owner, sub, here))
    for nbhd in range(owners):
        @pl.when(jnp.logical_not(is_me(nbhd)))
        def _():
            pltpu.make_async_remote_copy(
                src_ref=stage.at[0], dst_ref=out_ref.at[nbhd], send_sem=send_out.at[0],
                recv_sem=recv_out.at[nbhd], device_id=(nbhd, me_sub), device_id_type=MESH,
            ).wait_recv()
    for step, owner, sub, here in leaving:
        @pl.when(jnp.logical_not(here))
        def _():
            leave(step, owner, sub).wait_send()
    for copy in copies + spread:
        copy.wait_send()


def modes_and_pieces(snaps, gram, start, corr, members, owners, own, cell_count):
    pieces, cells, size = snaps.shape
    modes = start.shape[1]
    vmem = pl.BlockSpec(memory_space=pltpu.VMEM)
    return pl.pallas_call(
        functools.partial(
            modes_kernel, members=members, owners=owners, own=own, cell_count=cell_count
        ),
        out_shape=jax.ShapeDtypeStruct((owners, modes, cells), jnp.bfloat16),
        in_specs=[vmem, vmem, vmem, pl.BlockSpec(memory_space=pltpu.SMEM)],
        out_specs=vmem,
        scratch_shapes=[
            pltpu.VMEM((members, 2 * size // members, size), jnp.float32),
            pltpu.VMEM((2 * size // members, size), jnp.float32),
            pltpu.VMEM((2 * size, size), jnp.float32),
            pltpu.VMEM((owners, modes, cells), jnp.bfloat16),
            pltpu.SemaphoreType.DMA((members,)),
            pltpu.SemaphoreType.DMA((members,)),
            pltpu.SemaphoreType.DMA((members,)),
            pltpu.SemaphoreType.DMA((members,)),
            pltpu.SemaphoreType.DMA((owners,)),
            pltpu.SemaphoreType.DMA((owners,)),
        ],
        compiler_params=pltpu.CompilerParams(
            collective_id=1, has_side_effects=True, vmem_limit_bytes=32 << 20
        ),
    )(snaps, gram, start, corr)


def on_device(snap_init, channel_map, yface_vals, zface_vals, face_of, start_block, correlation):
    own, rows, depth, width = snap_init.shape[1:]
    members, owners = lax.axis_size("sub"), lax.axis_size("nbhd")
    state, gram = relax_and_gram(
        snap_init[0], channel_map[0], yface_vals[0], zface_vals[0], face_of, members
    )
    cells = own * rows * depth
    result = modes_and_pieces(
        state.reshape(owners, cells // owners, width), gram, start_block[0], correlation,
        members, owners, own, float(cells * members),
    )
    return result[None, None]


def solution(mesh):
    return jax.shard_map(
        on_device,
        mesh=mesh,
        in_specs=(
            P("nbhd", "sub", None, None, None),
            P("nbhd", "sub", None, None),
            P("nbhd", None, None),
            P("nbhd", None, None),
            P("nbhd", None),
            P("nbhd", None, None),
            P(),
        ),
        out_specs=P("nbhd", "sub", None, None, None),
        check_vma=False,
    )
```

```python
import functools

import jax
import jax.numpy as jnp
from jax import lax
from jax.experimental import pallas as pl
from jax.experimental.pallas import tpu as pltpu
from jax.sharding import PartitionSpec as P

MESH = pl.DeviceIdType.MESH

SWEEPS = 3
ITERS = 4


def harmonic(left_k, right_k):
    return 2.0 * left_k * right_k / (left_k + right_k)


def relax_kernel(
    snap_ref, class_ref, yface_ref, zface_ref, face_ref, state_ref, gram_ref,
    field, coef, compact, kappa, ghost_z, early, swap, zland, yland, rhs,
    class_pair, class_low, class_high,
    swap_send, swap_recv, z_send, z_recv, y_send, y_recv, class_send, class_recv,
    *, members,
):
    me_nbhd = lax.axis_index("nbhd")
    me = lax.axis_index("sub")
    half = lax.rem(me, 2)
    tower = me // 2
    towers = members // 2
    own, rows_all, depth, width = snap_ref.shape
    both = 2 * own
    rows = rows_all // 2
    top = both + 1
    base = 8
    inner = pl.ds(base, depth)

    def at(sub):
        return (me_nbhd, lax.rem(sub + members, members))

    partner = at(me + 1 - 2 * half)
    cross = at(me - 1 + 2 * half)
    lower = at(me - 2)
    upper = at(me + 2)

    def remote(src, dst, send, recv, device):
        return pltpu.make_async_remote_copy(
            src_ref=src, dst_ref=dst, send_sem=send, recv_sem=recv,
            device_id=device, device_id_type=MESH,
        )

    barrier = pltpu.get_barrier_semaphore()
    for device in (partner, cross, lower, upper):
        pl.semaphore_signal(barrier, inc=1, device_id=device, device_id_type=MESH)
    pl.semaphore_wait(barrier, 4)

    class_copies = [
        remote(class_ref, class_pair, class_send.at[0], class_recv.at[0], partner),
    ]
    class_copies[0].start()
    class_other = []

    def class_sends(plane, land, slot, devices):
        made = []
        for place, device in enumerate(devices):
            made.append(remote(
                class_ref.at[plane], land, class_send.at[1 + place], class_recv.at[slot], device
            ))
        return made

    @pl.when(half == 0)
    def _():
        for copy in class_sends(0, class_high, 2, (lower, cross)):
            copy.start()

    @pl.when(half == 1)
    def _():
        for copy in class_sends(own - 1, class_low, 1, (upper, cross)):
            copy.start()

    order = [0] + list(range(own - 1, 0, -1))
    swaps = []
    for turn, q in enumerate(order):
        plane = q + half * (own - 1 - 2 * q)
        copy = remote(
            snap_ref.at[plane, pl.ds((rows - 1) * (1 - half), rows + 1)],
            swap.at[turn], swap_send.at[turn], swap_recv.at[turn], partner,
        )
        copy.start()
        swaps.append(copy)

    @pl.when(half == 0)
    def _():
        remote(
            snap_ref.at[0, pl.ds(0, rows)], zland.at[0, 1], z_send.at[0, 0], z_recv.at[0, 1], lower
        ).start()

    @pl.when(half == 1)
    def _():
        remote(
            snap_ref.at[own - 1, pl.ds(rows, rows)], zland.at[0, 0], z_send.at[0, 1],
            z_recv.at[0, 0], upper
        ).start()

    shift = 1 - half

    def fill_own(p, _):
        def fill(r, _):
            field[0, 1 + own * half + p, shift + r, inner, :] = snap_ref[
                p, (rows - 1) * half + r
            ].astype(jnp.float32)
            return 0
        return lax.fori_loop(0, rows + 1, fill, 0)

    lax.fori_loop(0, own, fill_own, 0)

    face = face_ref[...]

    def pick(side):
        return jnp.where(face == side, 1.0, 0.0)

    side_y = jnp.where(half == 0, pick(0), pick(1))
    ghost_y = yface_ref[...].astype(jnp.float32) * side_y
    zface = zface_ref[...].astype(jnp.float32)
    ghost_z[0] = zface * pick(2)
    ghost_z[1] = zface * pick(3)

    def set_ghosts(p, _):
        for buf in range(2):
            field[buf, p + 1, (rows + 1) * half, inner, :] = ghost_y

            def one(y, _):
                field[buf, p + 1, y + 1, pl.ds(base - 1, 1), :] = ghost_z[0, pl.ds(rows * half + y, 1), :]
                field[buf, p + 1, y + 1, pl.ds(base + depth, 1), :] = ghost_z[1, pl.ds(rows * half + y, 1), :]
                return 0

            lax.fori_loop(0, rows, one, 0)
        return 0

    lax.fori_loop(0, both, set_ghosts, 0)

    def to_kappa(classes):
        return jnp.left_shift(1, 2 * classes).astype(jnp.float32)

    def land(slot, ref):
        remote(ref, ref, class_send.at[0], class_recv.at[slot], partner).wait_recv()

    land(0, class_pair)
    land(1, class_low)
    land(2, class_high)
    kappa[0] = to_kappa(class_low[...])
    kappa[top] = to_kappa(class_high[...])
    for p in range(own):
        kappa[1 + own * half + p] = to_kappa(class_ref[p])
        kappa[1 + own * (1 - half) + p] = to_kappa(class_pair[p])

    def coefficients(p, _):
        centre = kappa[p + 1]
        has_low = jnp.logical_or(tower > 0, p > 0)
        has_high = jnp.logical_or(tower < towers - 1, p < both - 1)
        face_low = harmonic(centre, kappa[p])
        face_high = harmonic(centre, kappa[p + 2])
        x_lower = jnp.where(has_low, face_low, centre)
        x_upper = jnp.where(has_high, face_high, centre)
        y_inner = harmonic(centre[1:], centre[:-1])
        y_lower = jnp.concatenate([centre[:1], y_inner], axis=0)
        y_upper = jnp.concatenate([y_inner, centre[-1:]], axis=0)
        z_inner = harmonic(centre[:, 1:], centre[:, :-1])
        z_lower = jnp.concatenate([centre[:, :1], z_inner], axis=1)
        z_upper = jnp.concatenate([z_inner, centre[:, -1:]], axis=1)
        denom = x_lower + x_upper + y_lower + y_upper + z_lower + z_upper
        inverse = 1.0 / denom
        compact[0] = jnp.where(has_low, face_low, 0.0) * inverse
        compact[1] = jnp.where(has_high, face_high, 0.0) * inverse
        compact[2] = y_lower * inverse
        compact[3] = y_upper * inverse
        compact[4] = z_lower * inverse
        compact[5] = z_upper * inverse
        compact[6] = denom
        compact[7] = centre * (1.0 / 16.0)
        first = pl.multiple_of(rows * half, rows)
        for kind in range(8):
            turned = compact[kind, pl.ds(first, rows), :].T
            for y in range(rows):
                coef[kind, p, y] = jnp.broadcast_to(turned[:, y:y + 1], (depth, width))
        return 0

    lax.fori_loop(0, both, coefficients, 0)

    def row(sweep, p, y):
        src, dst = (sweep + 1) % 2, sweep % 2
        c = [coef.at[kind, p - 1, y - 1] for kind in range(6)]
        value = c[0][...] * field[src, p - 1, y, inner, :]
        value += c[1][...] * field[src, p + 1, y, inner, :]
        value += c[2][...] * field[src, p, y - 1, inner, :]
        value += c[3][...] * field[src, p, y + 1, inner, :]
        value += c[4][...] * field[src, p, y, pl.ds(base - 1, depth), :]
        value += c[5][...] * field[src, p, y, pl.ds(base + 1, depth), :]
        low = value.astype(jnp.bfloat16)
        field[dst, p, y, inner, :] = low.astype(jnp.float32)
        if sweep < SWEEPS:
            early[sweep - 1, p - 1, y - 1] = low
        else:
            state_ref[p - 1, y - 1] = low
            field[dst, p, y, pl.ds(base + depth, 1), :] = jnp.zeros((1, width), jnp.float32)

    def line(sweep, p, first, count):
        def body(i, _):
            row(sweep, p, first + i)
            return 0
        lax.fori_loop(0, count, body, 0)

    def fill_z(buf, round_no, side):
        remote(
            zland.at[round_no, side], zland.at[round_no, side], z_send.at[round_no, side],
            z_recv.at[round_no, side], lower,
        ).wait_recv()

        def fill(y, _):
            field[buf, top * side, y + 1, inner, :] = zland[round_no, side, y].astype(jnp.float32)
            return 0
        lax.fori_loop(0, rows, fill, 0)

    def plane_of(e):
        return e + (1 - half) * (top - 2 * e)

    for e in range(own + 2, both):
        line(1, plane_of(e), 1, rows)
    for turn, q in enumerate(order):
        swaps[turn].wait_recv()
        plane = q + (1 - half) * (own - 1 - 2 * q)
        if turn == 0:
            @pl.when(half == 0)
            def _():
                remote(
                    swap.at[0, pl.ds(0, rows)], zland.at[0, 0], z_send.at[0, 1], z_recv.at[0, 0], upper
                ).start()

            @pl.when(half == 1)
            def _():
                remote(
                    swap.at[0, pl.ds(1, rows)], zland.at[0, 1], z_send.at[0, 0], z_recv.at[0, 1], lower
                ).start()

        def fill(r, _):
            field[0, 1 + own * (1 - half) + plane, shift + r, inner, :] = swap[turn, r].astype(
                jnp.float32
            )
            return 0

        lax.fori_loop(0, rows + 1, fill, 0)
        if turn >= 1:
            line(1, plane_of(q + 2), 1, rows)
    line(1, plane_of(2), 1, rows)
    fill_z(0, 0, 0)
    line(1, 1, 1, rows)
    fill_z(0, 0, 1)
    line(1, both, 1, rows)

    edge = rows - (rows - 1) * half
    started = []

    def send_edges(sweep):
        held = early.at[sweep - 1] if sweep < SWEEPS else state_ref
        copies = [
            remote(held.at[0], zland.at[sweep, 1], z_send.at[sweep, 0], z_recv.at[sweep, 1], lower),
        ]
        if sweep < SWEEPS:
            copies.append(remote(
                held.at[both - 1], zland.at[sweep, 0], z_send.at[sweep, 1], z_recv.at[sweep, 0], upper
            ))
        ycopy = remote(
            held.at[pl.ds(0, both), edge - 1], yland.at[sweep - 1], y_send.at[sweep - 1],
            y_recv.at[sweep - 1], partner,
        )
        if sweep < SWEEPS:
            copies.append(ycopy)
        for copy in copies:
            copy.start()
        started.extend(copies)
        return ycopy

    def fill_y(buf, sweep, ycopy):
        ycopy.wait_recv()

        def fill(p, _):
            field[buf, p + 1, (rows + 1) * (1 - half), inner, :] = yland[sweep - 1, p].astype(jnp.float32)
            return 0
        lax.fori_loop(0, both, fill, 0)

    for sweep in range(2, SWEEPS + 1):
        ycopy = send_edges(sweep - 1)
        src = (sweep + 1) % 2

        def middle(i, _):
            line(sweep, i + 2, 1 + half, rows - 1)
            return 0
        lax.fori_loop(0, both - 2, middle, 0)
        fill_y(src, sweep - 1, ycopy)

        def border(i, _):
            row(sweep, i + 2, edge)
            return 0
        lax.fori_loop(0, both - 2, border, 0)
        fill_z(src, sweep - 1, 0)
        line(sweep, 1, 1, rows)
        fill_z(src, sweep - 1, 1)
        line(sweep, both, 1, rows)

    ycopy = send_edges(SWEEPS)

    @pl.when(half == 1)
    def _():
        ycopy.start()

    last = SWEEPS % 2

    def stiff_row(p, y, place):
        here = field[last, p, y, inner, :]
        ahead = coef[1, p - 1, y - 1] * field[last, p + 1, y, inner, :]
        ahead += coef[3, p - 1, y - 1] * field[last, p, y + 1, inner, :]
        ahead += coef[5, p - 1, y - 1] * field[last, p, y, pl.ds(base + 1, depth), :]
        value = coef[6, p - 1, y - 1] * (here - 2.0 * ahead)
        high = value.astype(jnp.bfloat16)
        rest = (value - high.astype(jnp.float32)).astype(jnp.bfloat16)
        rhs[place, :, pl.ds(0, width)] = (here * coef[7, p - 1, y - 1]).astype(jnp.bfloat16)
        rhs[place, :, pl.ds(width, width)] = high
        rhs[place, :, pl.ds(2 * width, width)] = rest

    def gram(left, count):
        right = rhs[pl.ds(0, count)].reshape(count * depth, 3 * width)
        part = lax.dot_general(
            left.reshape(count * depth, width), right, (((0,), (0,)), ((), ())),
            preferred_element_type=jnp.float32,
        )
        gram_ref[pl.ds(0, width), :] += part[:, :width]
        gram_ref[pl.ds(width, width), :] += part[:, width:2 * width] + part[:, 2 * width:]

    gram_ref[...] = jnp.zeros_like(gram_ref)

    def inside(i, _):
        def body(y, _):
            stiff_row(i + 1, y + 1, y)
            return 0
        lax.fori_loop(0, rows - 1, body, 0)
        gram(state_ref[i, pl.ds(0, rows - 1)], rows - 1)
        return 0
    lax.fori_loop(0, both - 1, inside, 0)

    @pl.when(half == 0)
    def _():
        fill_y(last, SWEEPS, ycopy)

    @pl.when(half == 1)
    def _():
        def clear(p, _):
            field[last, p + 1, rows + 1, inner, :] = jnp.zeros((depth, width), jnp.float32)
            return 0
        lax.fori_loop(0, both, clear, 0)

    def side(i, _):
        stiff_row(i + 1, rows, i)
        return 0
    lax.fori_loop(0, both - 1, side, 0)
    gram(state_ref[pl.ds(0, both - 1), rows - 1], both - 1)
    fill_z(last, SWEEPS, 1)

    def roof(y, _):
        stiff_row(both, y + 1, y)
        return 0
    lax.fori_loop(0, rows, roof, 0)
    gram(state_ref[both - 1], rows)

    class_copies[0].wait_send()
    for place in range(2):
        remote(
            class_ref.at[0], class_low, class_send.at[1 + place], class_recv.at[1], partner
        ).wait_send()
    for copy in swaps:
        copy.wait_send()
    for direction in range(2):
        remote(
            snap_ref.at[0, pl.ds(0, rows)], zland.at[0, 0], z_send.at[0, direction], z_recv.at[0, 0], lower
        ).wait_send()
    for copy in started:
        copy.wait_send()

    @pl.when(half == 1)
    def _():
        ycopy.wait_send()


def relax_and_gram(snap, classes, yface, zface, face, members):
    own, rows_all, depth, width = snap.shape
    both, rows = 2 * own, rows_all // 2
    vmem = pl.BlockSpec(memory_space=pltpu.VMEM)
    f32, bf16 = jnp.float32, jnp.bfloat16
    dma = pltpu.SemaphoreType.DMA
    return pl.pallas_call(
        functools.partial(relax_kernel, members=members),
        out_shape=(
            jax.ShapeDtypeStruct((both, rows, depth, width), bf16),
            jax.ShapeDtypeStruct((2 * width, width), f32),
        ),
        in_specs=[vmem] * 5,
        out_specs=(vmem, vmem),
        scratch_shapes=[
            pltpu.VMEM((2, both + 2, rows + 2, depth + 16, width), f32),
            pltpu.VMEM((8, both, rows, depth, width), f32),
            pltpu.VMEM((8, rows_all, depth), f32),
            pltpu.VMEM((both + 2, rows_all, depth), f32),
            pltpu.VMEM((2, rows_all, width), f32),
            pltpu.VMEM((SWEEPS - 1, both, rows, depth, width), bf16),
            pltpu.VMEM((own, rows + 1, depth, width), bf16),
            pltpu.VMEM((SWEEPS + 1, 2, rows, depth, width), bf16),
            pltpu.VMEM((SWEEPS, both, depth, width), bf16),
            pltpu.VMEM((max(both, rows), depth, 3 * width), bf16),
            pltpu.VMEM((own, rows_all, depth), jnp.int32),
            pltpu.VMEM((rows_all, depth), jnp.int32),
            pltpu.VMEM((rows_all, depth), jnp.int32),
            dma((own,)),
            dma((own,)),
            dma((SWEEPS + 1, 2)),
            dma((SWEEPS + 1, 2)),
            dma((SWEEPS,)),
            dma((SWEEPS,)),
            dma((3,)),
            dma((3,)),
        ],
        compiler_params=pltpu.CompilerParams(
            collective_id=0, has_side_effects=True, vmem_limit_bytes=60 << 20
        ),
    )(snap, classes, yface, zface, face)


TILE = 8


def spread(tile, col, width):
    return jnp.broadcast_to(tile[:, col:col + 1], (tile.shape[0], width))


def eliminate_spd(full, size, block):
    lanes = lax.broadcasted_iota(jnp.int32, (TILE, size), 1)
    rows = lax.broadcasted_iota(jnp.int32, (TILE, size), 0)
    wide = lax.broadcasted_iota(jnp.int32, (size, size), 1)
    block_lanes = lax.broadcasted_iota(jnp.int32, (block, size), 1)
    count = block // TILE
    for first in range(0, size, block):
        panel = full[first:first + block]
        signed = jnp.where(block_lanes < first, -panel, panel) if first else panel
        tiles = [panel[TILE * u:TILE * (u + 1)] for u in range(count)]
        for t in range(count):
            base = first + TILE * t
            columns = [[spread(tile, base + j, size) for tile in tiles] for j in range(TILE)]
            for i in range(TILE):
                here = rows == i
                at_col = lanes == base + i
                lead = columns[i]
                pivot = 1.0 / lead[t][i:i + 1]
                row = jnp.where(at_col[:1], 1.0, tiles[t][i:i + 1]) * pivot
                for j in range(i + 1, TILE):
                    scaled = columns[j][t][i:i + 1] * pivot
                    columns[j] = [columns[j][u] - lead[u] * scaled for u in range(count)]
                    columns[j][t] = jnp.where(here, scaled, columns[j][t])
                tiles = [jnp.where(at_col, 0.0, tiles[u]) - lead[u] * row for u in range(count)]
                tiles[t] = jnp.where(here, row, tiles[t])
        panel = jnp.concatenate(tiles, axis=0)
        inside = (wide >= first) & (wide < first + block)
        update = lax.dot_general(
            signed, panel, (((0,), (0,)), ((), ())),
            precision=lax.Precision.HIGHEST, preferred_element_type=jnp.float32,
        )
        rest = jnp.where(inside, 0.0, full) - update
        parts = []
        if first:
            parts.append(rest[:first])
        parts.append(panel)
        if first + block < size:
            parts.append(rest[first + block:])
        full = jnp.concatenate(parts, axis=0)
    return full


def normalize(inner, vectors):
    width = vectors.shape[1]
    count = inner.shape[0] // TILE
    rows = lax.broadcasted_iota(jnp.int32, (TILE, width), 0)
    left = [inner[TILE * u:TILE * (u + 1)] for u in range(count)]
    right = [vectors[TILE * u:TILE * (u + 1)] for u in range(count)]
    scales = []
    for t in range(count):
        columns = [
            [spread(left[u], TILE * t + j, width) for u in range(t, count)] for j in range(TILE)
        ]
        scale = jnp.zeros((TILE, width), jnp.float32)
        for i in range(TILE):
            lead = columns[i]
            value = lead[0][i:i + 1]
            pivot = 1.0 / value
            scale = jnp.where(rows == i, value, scale)
            for j in range(i + 1, TILE):
                scaled = columns[j][0][i:i + 1] * pivot
                columns[j] = [column - part * scaled for column, part in zip(columns[j], lead)]
            below = [jnp.where(rows > i, lead[0], 0.0)] + lead[1:]
            mate = right[t][i:i + 1] * pivot
            for u in range(t, count):
                right[u] = right[u] - below[u - t] * mate
            if t + 1 < count:
                ahead = left[t][i:i + 1] * pivot[:, :left[t].shape[1]]
                for u in range(t, count):
                    left[u] = left[u] - below[u - t][:, :left[t].shape[1]] * ahead
        scales.append(scale)
    return jnp.concatenate([tile / jnp.sqrt(scale) for tile, scale in zip(right, scales)], axis=0)


def modes_kernel(
    snaps_ref, gram_ref, start_ref, corr_ref, out_ref,
    slots, summed, total, stage, send_sem, recv_sem, send_two, recv_two, send_out, recv_out,
    *, members, owners, own, cell_count,
):
    me_sub = lax.axis_index("sub")
    me_nbhd = lax.axis_index("nbhd")
    size = gram_ref.shape[1]
    chunk = 2 * size // members

    def sub_at(step):
        return lax.rem(me_sub + step, members)

    half = lax.rem(me_sub, 2)
    tower = me_sub - half
    planes = own
    across = owners // planes
    mine = across // 2
    from_half = lax.rem(me_nbhd, across) // mine
    whole = jnp.where(from_half == half, 1, 0)

    barrier = pltpu.get_barrier_semaphore()
    for step in range(1, members):
        pl.semaphore_signal(barrier, inc=1, device_id=(me_nbhd, sub_at(step)), device_id_type=MESH)

    def is_me(nbhd):
        return jnp.logical_and(nbhd == me_nbhd, from_half == half)

    for nbhd in range(owners):
        @pl.when(jnp.logical_not(is_me(nbhd)))
        def _():
            pl.semaphore_signal(
                barrier, inc=1, device_id=(nbhd, tower + from_half), device_id_type=MESH
            )
    pl.semaphore_wait(barrier, members - 1 + owners - whole)

    def part(owner):
        return pl.ds(pl.multiple_of(owner * chunk, chunk), chunk)

    copies = []
    for step in range(1, members):
        peer = sub_at(step)
        copy = pltpu.make_async_remote_copy(
            src_ref=gram_ref.at[part(peer)],
            dst_ref=slots.at[step],
            send_sem=send_sem.at[step],
            recv_sem=recv_sem.at[step],
            device_id=(me_nbhd, peer),
            device_id_type=MESH,
        )
        copy.start()
        copies.append(copy)
    acc = gram_ref[part(me_sub)]
    for step in range(1, members):
        copies[step - 1].wait_recv()
        acc = acc + slots[step]
    summed[...] = acc
    total[part(me_sub)] = acc
    spread = []
    for step in range(1, members):
        copy = pltpu.make_async_remote_copy(
            src_ref=summed,
            dst_ref=total.at[part(me_sub)],
            send_sem=send_two.at[step],
            recv_sem=recv_two.at[step],
            device_id=(me_nbhd, sub_at(step)),
            device_id_type=MESH,
        )
        copy.start()
        spread.append(copy)
    for copy in spread:
        copy.wait_recv()

    dot = functools.partial(
        lax.dot_general, precision=lax.Precision.HIGHEST, preferred_element_type=jnp.float32
    )
    mass = total[:size] / cell_count
    stiff = total[size:]
    stiff = (stiff + stiff.T) * (0.5 / cell_count)
    inverse = eliminate_spd(stiff, size, 32)
    step_map = dot(mass, inverse, (((1,), (0,)), ((), ())))
    both = jnp.concatenate([step_map, dot(step_map, mass, (((1,), (0,)), ((), ())))], axis=1)
    rows = None
    for turn in range(ITERS):
        if turn == 0:
            pair = dot(start_ref[...], both, (((0,), (0,)), ((), ())))
        else:
            pair = dot(rows, both, (((1,), (0,)), ((), ())))
        solved, image = pair[:, :size], pair[:, size:]
        inner = dot(solved, image, (((1,), (1,)), ((), ())))
        inner = 0.5 * (inner + inner.T)
        rows = normalize(inner, solved)
    modes = rows.astype(jnp.bfloat16)

    def piece(index, owner):
        values = lax.dot_general(
            modes, snaps_ref[index], (((1,), (1,)), ((), ())), preferred_element_type=jnp.float32
        )
        return (values * corr_ref[me_nbhd, owner].astype(jnp.float32)).astype(jnp.bfloat16)

    def leave(step, owner, sub):
        return pltpu.make_async_remote_copy(
            src_ref=stage.at[step],
            dst_ref=out_ref.at[me_nbhd],
            send_sem=send_out.at[step],
            recv_sem=recv_out.at[me_nbhd],
            device_id=(owner, sub),
            device_id_type=MESH,
        )

    leaving = []
    for step in range(owners):
        index = lax.rem(step + me_nbhd, owners)
        level = index // mine
        owner = across * lax.rem(level, planes) + mine * half + lax.rem(index, mine)
        sub = tower + level // planes
        here = jnp.logical_and(owner == me_nbhd, sub == me_sub)
        stage[step] = piece(index, owner)

        @pl.when(jnp.logical_not(here))
        def _():
            leave(step, owner, sub).start()

        @pl.when(here)
        def _():
            out_ref[me_nbhd] = stage[step]

        leaving.append((step, owner, sub, here))
    for nbhd in range(owners):
        @pl.when(jnp.logical_not(is_me(nbhd)))
        def _():
            pltpu.make_async_remote_copy(
                src_ref=stage.at[0], dst_ref=out_ref.at[nbhd], send_sem=send_out.at[0],
                recv_sem=recv_out.at[nbhd], device_id=(nbhd, me_sub), device_id_type=MESH,
            ).wait_recv()
    for step, owner, sub, here in leaving:
        @pl.when(jnp.logical_not(here))
        def _():
            leave(step, owner, sub).wait_send()
    for copy in copies + spread:
        copy.wait_send()


def modes_and_pieces(snaps, gram, start, corr, members, owners, own, cell_count):
    pieces, cells, size = snaps.shape
    modes = start.shape[1]
    vmem = pl.BlockSpec(memory_space=pltpu.VMEM)
    return pl.pallas_call(
        functools.partial(
            modes_kernel, members=members, owners=owners, own=own, cell_count=cell_count
        ),
        out_shape=jax.ShapeDtypeStruct((owners, modes, cells), jnp.bfloat16),
        in_specs=[vmem, vmem, vmem, pl.BlockSpec(memory_space=pltpu.SMEM)],
        out_specs=vmem,
        scratch_shapes=[
            pltpu.VMEM((members, 2 * size // members, size), jnp.float32),
            pltpu.VMEM((2 * size // members, size), jnp.float32),
            pltpu.VMEM((2 * size, size), jnp.float32),
            pltpu.VMEM((owners, modes, cells), jnp.bfloat16),
            pltpu.SemaphoreType.DMA((members,)),
            pltpu.SemaphoreType.DMA((members,)),
            pltpu.SemaphoreType.DMA((members,)),
            pltpu.SemaphoreType.DMA((members,)),
            pltpu.SemaphoreType.DMA((owners,)),
            pltpu.SemaphoreType.DMA((owners,)),
        ],
        compiler_params=pltpu.CompilerParams(
            collective_id=1, has_side_effects=True, vmem_limit_bytes=32 << 20
        ),
    )(snaps, gram, start, corr)


def on_device(snap_init, channel_map, yface_vals, zface_vals, face_of, start_block, correlation):
    own, rows, depth, width = snap_init.shape[1:]
    members, owners = lax.axis_size("sub"), lax.axis_size("nbhd")
    state, gram = relax_and_gram(
        snap_init[0], channel_map[0], yface_vals[0], zface_vals[0], face_of, members
    )
    cells = own * rows * depth
    result = modes_and_pieces(
        state.reshape(owners, cells // owners, width), gram, start_block[0], correlation,
        members, owners, own, float(cells * members),
    )
    return result[None, None]


def solution(mesh):
    return jax.shard_map(
        on_device,
        mesh=mesh,
        in_specs=(
            P("nbhd", "sub", None, None, None),
            P("nbhd", "sub", None, None),
            P("nbhd", None, None),
            P("nbhd", None, None),
            P("nbhd", None),
            P("nbhd", None, None),
            P(),
        ),
        out_specs=P("nbhd", "sub", None, None, None),
        check_vma=False,
    )
```

```python
import functools

import jax
import jax.numpy as jnp
from jax import lax
from jax.experimental import pallas as pl
from jax.experimental.pallas import tpu as pltpu
from jax.sharding import PartitionSpec as P

MESH = pl.DeviceIdType.MESH

SWEEPS = 3
ITERS = 4


def harmonic(left_k, right_k):
    return 2.0 * left_k * right_k / (left_k + right_k)


def relax_kernel(
    snap_ref, class_ref, yface_ref, zface_ref, face_ref, state_ref, gram_ref,
    field, coef, compact, kappa, ghost_z, early, swap, zland, yland, rhs,
    class_pair, class_low, class_high,
    swap_send, swap_recv, z_send, z_recv, y_send, y_recv, class_send, class_recv,
    *, members,
):
    me_nbhd = lax.axis_index("nbhd")
    me = lax.axis_index("sub")
    half = lax.rem(me, 2)
    tower = me // 2
    towers = members // 2
    own, rows_all, depth, width = snap_ref.shape
    both = 2 * own
    rows = rows_all // 2
    top = both + 1
    base = 8
    inner = pl.ds(base, depth)

    def at(sub):
        return (me_nbhd, lax.rem(sub + members, members))

    partner = at(me + 1 - 2 * half)
    cross = at(me - 1 + 2 * half)
    lower = at(me - 2)
    upper = at(me + 2)

    def remote(src, dst, send, recv, device):
        return pltpu.make_async_remote_copy(
            src_ref=src, dst_ref=dst, send_sem=send, recv_sem=recv,
            device_id=device, device_id_type=MESH,
        )

    barrier = pltpu.get_barrier_semaphore()
    for device in (partner, cross, lower, upper):
        pl.semaphore_signal(barrier, inc=1, device_id=device, device_id_type=MESH)
    pl.semaphore_wait(barrier, 4)

    class_copies = [
        remote(class_ref, class_pair, class_send.at[0], class_recv.at[0], partner),
    ]
    class_copies[0].start()
    class_other = []

    def class_sends(plane, land, slot, devices):
        made = []
        for place, device in enumerate(devices):
            made.append(remote(
                class_ref.at[plane], land, class_send.at[1 + place], class_recv.at[slot], device
            ))
        return made

    @pl.when(half == 0)
    def _():
        for copy in class_sends(0, class_high, 2, (lower, cross)):
            copy.start()

    @pl.when(half == 1)
    def _():
        for copy in class_sends(own - 1, class_low, 1, (upper, cross)):
            copy.start()

    order = [0, 1] + list(range(own - 1, 1, -1))
    swaps = []
    for turn, q in enumerate(order):
        plane = q + half * (own - 1 - 2 * q)
        copy = remote(
            snap_ref.at[plane, pl.ds((rows - 1) * (1 - half), rows + 1)],
            swap.at[turn], swap_send.at[turn], swap_recv.at[turn], partner,
        )
        copy.start()
        swaps.append(copy)

    @pl.when(half == 0)
    def _():
        remote(
            snap_ref.at[0, pl.ds(0, rows)], zland.at[0, 1], z_send.at[0, 0, 0],
            z_recv.at[0, 1, 0], lower
        ).start()

    @pl.when(half == 1)
    def _():
        remote(
            snap_ref.at[own - 1, pl.ds(rows, rows)], zland.at[0, 0], z_send.at[0, 1, 0],
            z_recv.at[0, 0, 0], upper
        ).start()

    shift = 1 - half

    def fill_own(p, _):
        def fill(r, _):
            field[0, 1 + own * half + p, shift + r, inner, :] = snap_ref[
                p, (rows - 1) * half + r
            ].astype(jnp.float32)
            return 0
        return lax.fori_loop(0, rows + 1, fill, 0)

    lax.fori_loop(0, own, fill_own, 0)

    face = face_ref[...]

    def pick(side):
        return jnp.where(face == side, 1.0, 0.0)

    side_y = jnp.where(half == 0, pick(0), pick(1))
    ghost_y = yface_ref[...].astype(jnp.float32) * side_y
    zface = zface_ref[...].astype(jnp.float32)
    ghost_z[0] = zface * pick(2)
    ghost_z[1] = zface * pick(3)

    def set_ghosts(p, _):
        for buf in range(2):
            field[buf, p + 1, (rows + 1) * half, inner, :] = ghost_y

            def one(y, _):
                field[buf, p + 1, y + 1, pl.ds(base - 1, 1), :] = ghost_z[0, pl.ds(rows * half + y, 1), :]
                field[buf, p + 1, y + 1, pl.ds(base + depth, 1), :] = ghost_z[1, pl.ds(rows * half + y, 1), :]
                return 0

            lax.fori_loop(0, rows, one, 0)
        return 0

    lax.fori_loop(0, both, set_ghosts, 0)

    def to_kappa(classes):
        return jnp.left_shift(1, 2 * classes).astype(jnp.float32)

    def land(slot, ref):
        remote(ref, ref, class_send.at[0], class_recv.at[slot], partner).wait_recv()

    land(0, class_pair)
    land(1, class_low)
    land(2, class_high)
    kappa[0] = to_kappa(class_low[...])
    kappa[top] = to_kappa(class_high[...])
    for p in range(own):
        kappa[1 + own * half + p] = to_kappa(class_ref[p])
        kappa[1 + own * (1 - half) + p] = to_kappa(class_pair[p])

    def coefficients(p, _):
        centre = kappa[p + 1]
        has_low = jnp.logical_or(tower > 0, p > 0)
        has_high = jnp.logical_or(tower < towers - 1, p < both - 1)
        face_low = harmonic(centre, kappa[p])
        face_high = harmonic(centre, kappa[p + 2])
        x_lower = jnp.where(has_low, face_low, centre)
        x_upper = jnp.where(has_high, face_high, centre)
        y_inner = harmonic(centre[1:], centre[:-1])
        y_lower = jnp.concatenate([centre[:1], y_inner], axis=0)
        y_upper = jnp.concatenate([y_inner, centre[-1:]], axis=0)
        z_inner = harmonic(centre[:, 1:], centre[:, :-1])
        z_lower = jnp.concatenate([centre[:, :1], z_inner], axis=1)
        z_upper = jnp.concatenate([z_inner, centre[:, -1:]], axis=1)
        denom = x_lower + x_upper + y_lower + y_upper + z_lower + z_upper
        inverse = 1.0 / denom
        compact[0] = jnp.where(has_low, face_low, 0.0) * inverse
        compact[1] = jnp.where(has_high, face_high, 0.0) * inverse
        compact[2] = y_lower * inverse
        compact[3] = y_upper * inverse
        compact[4] = z_lower * inverse
        compact[5] = z_upper * inverse
        compact[6] = denom
        compact[7] = centre * (1.0 / 16.0)
        first = pl.multiple_of(rows * half, rows)
        for kind in range(8):
            turned = compact[kind, pl.ds(first, rows), :].T
            for y in range(rows):
                coef[kind, p, y] = jnp.broadcast_to(turned[:, y:y + 1], (depth, width))
        return 0

    lax.fori_loop(0, both, coefficients, 0)

    def row(sweep, p, y):
        src, dst = (sweep + 1) % 2, sweep % 2
        c = [coef.at[kind, p - 1, y - 1] for kind in range(6)]
        value = c[0][...] * field[src, p - 1, y, inner, :]
        value += c[1][...] * field[src, p + 1, y, inner, :]
        value += c[2][...] * field[src, p, y - 1, inner, :]
        value += c[3][...] * field[src, p, y + 1, inner, :]
        value += c[4][...] * field[src, p, y, pl.ds(base - 1, depth), :]
        value += c[5][...] * field[src, p, y, pl.ds(base + 1, depth), :]
        low = value.astype(jnp.bfloat16)
        field[dst, p, y, inner, :] = low.astype(jnp.float32)
        if sweep < SWEEPS:
            early[sweep - 1, p - 1, y - 1] = low
        else:
            state_ref[p - 1, y - 1] = low
            field[dst, p, y, pl.ds(base + depth, 1), :] = jnp.zeros((1, width), jnp.float32)

    def line(sweep, p, first, count):
        def body(i, _):
            row(sweep, p, first + i)
            return 0
        lax.fori_loop(0, count, body, 0)

    chunk = rows // 2
    edge = rows - (rows - 1) * half

    def chunk_at(part):
        return chunk * half if part == 0 else chunk - chunk * half

    def held(sweep):
        return early.at[sweep - 1] if sweep < SWEEPS else state_ref

    def send_z(sweep, side, part):
        cells = pl.ds(chunk_at(part), chunk)
        remote(
            held(sweep).at[side * (both - 1), cells], zland.at[sweep, 1 - side, cells],
            z_send.at[sweep, side, part], z_recv.at[sweep, 1 - side, part], at(me - 2 + 4 * side),
        ).start()

    def send_y(sweep, part, first, count):
        planes = pl.ds(first, count)
        remote(
            held(sweep).at[planes, edge - 1], yland.at[sweep - 1, planes], y_send.at[sweep - 1, part],
            y_recv.at[sweep - 1, part], partner,
        ).start()

    def take_z(buf, sweep, side, part):
        cells = pl.ds(0, rows if sweep == 0 else chunk)
        remote(
            zland.at[sweep, side, cells], zland.at[sweep, side, cells], z_send.at[sweep, side, part],
            z_recv.at[sweep, side, part], lower,
        ).wait_recv()
        first = 0 if sweep == 0 else chunk_at(part)

        def fill(i, _):
            field[buf, top * side, first + i + 1, inner, :] = zland[sweep, side, first + i].astype(
                jnp.float32
            )
            return 0
        lax.fori_loop(0, rows if sweep == 0 else chunk, fill, 0)

    y_parts = ((1, own - 1), (own, own - 1), (0, 1), (both - 1, 1))

    def take_y(buf, sweep, part):
        first, count = y_parts[part]
        planes = pl.ds(first, count)
        remote(
            yland.at[sweep - 1, planes], yland.at[sweep - 1, planes], y_send.at[sweep - 1, part],
            y_recv.at[sweep - 1, part], partner,
        ).wait_recv()

        def fill(i, _):
            p = first + i
            field[buf, p + 1, (rows + 1) * (1 - half), inner, :] = yland[sweep - 1, p].astype(jnp.float32)
            return 0
        lax.fori_loop(0, count, fill, 0)

    def plane_of(e):
        return e + (1 - half) * (top - 2 * e)

    for e in range(own + 2, both):
        line(1, plane_of(e), 1, rows)
    for turn, q in enumerate(order):
        swaps[turn].wait_recv()
        plane = q + (1 - half) * (own - 1 - 2 * q)
        if turn == 0:
            @pl.when(half == 0)
            def _():
                remote(
                    swap.at[0, pl.ds(0, rows)], zland.at[0, 0], z_send.at[0, 1, 0], z_recv.at[0, 0, 0],
                    upper,
                ).start()

            @pl.when(half == 1)
            def _():
                remote(
                    swap.at[0, pl.ds(1, rows)], zland.at[0, 1], z_send.at[0, 0, 0], z_recv.at[0, 1, 0],
                    lower,
                ).start()

        def fill(r, _):
            field[0, 1 + own * (1 - half) + plane, shift + r, inner, :] = swap[turn, r].astype(
                jnp.float32
            )
            return 0

        lax.fori_loop(0, rows + 1, fill, 0)
        if turn == 1:
            take_z(0, 0, 0, 0)
            take_z(0, 0, 1, 0)
            for e, side in ((both, half), (1, 1 - half)):
                line(1, plane_of(e), 1, rows)
                send_z(1, side, 0)
                send_z(1, side, 1)
                send_y(1, 2 + side, side * (both - 1), 1)
        if turn >= 2:
            line(1, plane_of(q + 2), 1, rows)
        if q == own - 1:
            send_y(1, half, 1 + (own - 1) * half, own - 1)
    line(1, plane_of(3), 1, rows)
    line(1, plane_of(2), 1, rows)
    send_y(1, 1 - half, 1 + (own - 1) * (1 - half), own - 1)

    def only_if_last(sweep, action):
        if sweep < SWEEPS:
            action()
        else:
            pl.when(half == 1)(action)

    for sweep in range(2, SWEEPS + 1):
        src = (sweep + 1) % 2
        sides = (0, 1) if sweep < SWEEPS else (0,)

        def middle(i, _):
            line(sweep, i + 2, 1 + half, rows - 1)
            return 0
        lax.fori_loop(0, both - 2, middle, 0)
        for side in (0, 1):
            take_z(src, sweep - 1, side, 0)
            line(sweep, 1 + side * (both - 1), 1 + chunk_at(0), chunk)
            if side in sides:
                send_z(sweep, side, 0)
        take_y(src, sweep - 1, 0)
        take_y(src, sweep - 1, 1)

        def border(i, _):
            row(sweep, i + 2, edge)
            return 0
        lax.fori_loop(0, both - 2, border, 0)

        def first_parts():
            send_y(sweep, 0, *y_parts[0])
            send_y(sweep, 1, *y_parts[1])
        only_if_last(sweep, first_parts)
        for side in (0, 1):
            take_y(src, sweep - 1, 2 + side)
            take_z(src, sweep - 1, side, 1)
            line(sweep, 1 + side * (both - 1), 1 + chunk_at(1), chunk)
            if side in sides:
                send_z(sweep, side, 1)

            def last_part():
                send_y(sweep, 2 + side, *y_parts[2 + side])
            only_if_last(sweep, last_part)

    last = SWEEPS % 2

    def stiff_row(p, y, place):
        here = field[last, p, y, inner, :]
        ahead = coef[1, p - 1, y - 1] * field[last, p + 1, y, inner, :]
        ahead += coef[3, p - 1, y - 1] * field[last, p, y + 1, inner, :]
        ahead += coef[5, p - 1, y - 1] * field[last, p, y, pl.ds(base + 1, depth), :]
        value = coef[6, p - 1, y - 1] * (here - 2.0 * ahead)
        high = value.astype(jnp.bfloat16)
        rest = (value - high.astype(jnp.float32)).astype(jnp.bfloat16)
        rhs[place, :, pl.ds(0, width)] = (here * coef[7, p - 1, y - 1]).astype(jnp.bfloat16)
        rhs[place, :, pl.ds(width, width)] = high
        rhs[place, :, pl.ds(2 * width, width)] = rest

    def gram(left, count):
        right = rhs[pl.ds(0, count)].reshape(count * depth, 3 * width)
        part = lax.dot_general(
            left.reshape(count * depth, width), right, (((0,), (0,)), ((), ())),
            preferred_element_type=jnp.float32,
        )
        gram_ref[pl.ds(0, width), :] += part[:, :width]
        gram_ref[pl.ds(width, width), :] += part[:, width:2 * width] + part[:, 2 * width:]

    gram_ref[...] = jnp.zeros_like(gram_ref)

    def inside(i, _):
        def body(y, _):
            stiff_row(i + 1, y + 1, y)
            return 0
        lax.fori_loop(0, rows - 1, body, 0)
        gram(state_ref[i, pl.ds(0, rows - 1)], rows - 1)
        return 0
    lax.fori_loop(0, both - 1, inside, 0)

    @pl.when(half == 0)
    def _():
        for part in range(4):
            take_y(last, SWEEPS, part)

    @pl.when(half == 1)
    def _():
        def clear(p, _):
            field[last, p + 1, rows + 1, inner, :] = jnp.zeros((depth, width), jnp.float32)
            return 0
        lax.fori_loop(0, both, clear, 0)

    def side(i, _):
        stiff_row(i + 1, rows, i)
        return 0
    lax.fori_loop(0, both - 1, side, 0)
    gram(state_ref[pl.ds(0, both - 1), rows - 1], both - 1)
    take_z(last, SWEEPS, 1, 0)
    take_z(last, SWEEPS, 1, 1)

    def roof(y, _):
        stiff_row(both, y + 1, y)
        return 0
    lax.fori_loop(0, rows, roof, 0)
    gram(state_ref[both - 1], rows)

    class_copies[0].wait_send()
    for place in range(2):
        remote(
            class_ref.at[0], class_low, class_send.at[1 + place], class_recv.at[1], partner
        ).wait_send()
    for copy in swaps:
        copy.wait_send()
    for side in range(2):
        remote(
            snap_ref.at[0, pl.ds(0, rows)], zland.at[0, 0], z_send.at[0, side, 0], z_recv.at[0, 0, 0], lower
        ).wait_send()

    def left_z(sweep, side, part):
        cells = pl.ds(0, chunk)
        remote(
            held(sweep).at[0, cells], zland.at[sweep, 0, cells], z_send.at[sweep, side, part],
            z_recv.at[sweep, 0, part], lower,
        ).wait_send()

    def left_y(sweep, part):
        planes = pl.ds(*y_parts[part])
        remote(
            held(sweep).at[planes, 0], yland.at[sweep - 1, planes], y_send.at[sweep - 1, part],
            y_recv.at[sweep - 1, part], partner,
        ).wait_send()

    for sweep in range(1, SWEEPS + 1):
        for side in range(2 if sweep < SWEEPS else 1):
            for part in range(2):
                left_z(sweep, side, part)

        def all_y():
            for part in range(4):
                left_y(sweep, part)
        only_if_last(sweep, all_y)


def relax_and_gram(snap, classes, yface, zface, face, members):
    own, rows_all, depth, width = snap.shape
    both, rows = 2 * own, rows_all // 2
    vmem = pl.BlockSpec(memory_space=pltpu.VMEM)
    f32, bf16 = jnp.float32, jnp.bfloat16
    dma = pltpu.SemaphoreType.DMA
    return pl.pallas_call(
        functools.partial(relax_kernel, members=members),
        out_shape=(
            jax.ShapeDtypeStruct((both, rows, depth, width), bf16),
            jax.ShapeDtypeStruct((2 * width, width), f32),
        ),
        in_specs=[vmem] * 5,
        out_specs=(vmem, vmem),
        scratch_shapes=[
            pltpu.VMEM((2, both + 2, rows + 2, depth + 16, width), f32),
            pltpu.VMEM((8, both, rows, depth, width), f32),
            pltpu.VMEM((8, rows_all, depth), f32),
            pltpu.VMEM((both + 2, rows_all, depth), f32),
            pltpu.VMEM((2, rows_all, width), f32),
            pltpu.VMEM((SWEEPS - 1, both, rows, depth, width), bf16),
            pltpu.VMEM((own, rows + 1, depth, width), bf16),
            pltpu.VMEM((SWEEPS + 1, 2, rows, depth, width), bf16),
            pltpu.VMEM((SWEEPS, both, depth, width), bf16),
            pltpu.VMEM((max(both, rows), depth, 3 * width), bf16),
            pltpu.VMEM((own, rows_all, depth), jnp.int32),
            pltpu.VMEM((rows_all, depth), jnp.int32),
            pltpu.VMEM((rows_all, depth), jnp.int32),
            dma((own,)),
            dma((own,)),
            dma((SWEEPS + 1, 2, 2)),
            dma((SWEEPS + 1, 2, 2)),
            dma((SWEEPS, 4)),
            dma((SWEEPS, 4)),
            dma((3,)),
            dma((3,)),
        ],
        compiler_params=pltpu.CompilerParams(
            collective_id=0, has_side_effects=True, vmem_limit_bytes=60 << 20
        ),
    )(snap, classes, yface, zface, face)


TILE = 8


def spread(tile, col, width):
    return jnp.broadcast_to(tile[:, col:col + 1], (tile.shape[0], width))


def eliminate_spd(full, size, block):
    lanes = lax.broadcasted_iota(jnp.int32, (TILE, size), 1)
    rows = lax.broadcasted_iota(jnp.int32, (TILE, size), 0)
    wide = lax.broadcasted_iota(jnp.int32, (size, size), 1)
    block_lanes = lax.broadcasted_iota(jnp.int32, (block, size), 1)
    count = block // TILE
    for first in range(0, size, block):
        panel = full[first:first + block]
        signed = jnp.where(block_lanes < first, -panel, panel) if first else panel
        tiles = [panel[TILE * u:TILE * (u + 1)] for u in range(count)]
        for t in range(count):
            base = first + TILE * t
            columns = [[spread(tile, base + j, size) for tile in tiles] for j in range(TILE)]
            for i in range(TILE):
                here = rows == i
                at_col = lanes == base + i
                lead = columns[i]
                pivot = 1.0 / lead[t][i:i + 1]
                row = jnp.where(at_col[:1], 1.0, tiles[t][i:i + 1]) * pivot
                for j in range(i + 1, TILE):
                    scaled = columns[j][t][i:i + 1] * pivot
                    columns[j] = [columns[j][u] - lead[u] * scaled for u in range(count)]
                    columns[j][t] = jnp.where(here, scaled, columns[j][t])
                tiles = [jnp.where(at_col, 0.0, tiles[u]) - lead[u] * row for u in range(count)]
                tiles[t] = jnp.where(here, row, tiles[t])
        panel = jnp.concatenate(tiles, axis=0)
        inside = (wide >= first) & (wide < first + block)
        update = lax.dot_general(
            signed, panel, (((0,), (0,)), ((), ())),
            precision=lax.Precision.HIGHEST, preferred_element_type=jnp.float32,
        )
        rest = jnp.where(inside, 0.0, full) - update
        parts = []
        if first:
            parts.append(rest[:first])
        parts.append(panel)
        if first + block < size:
            parts.append(rest[first + block:])
        full = jnp.concatenate(parts, axis=0)
    return full


def normalize(inner, vectors):
    width = vectors.shape[1]
    count = inner.shape[0] // TILE
    rows = lax.broadcasted_iota(jnp.int32, (TILE, width), 0)
    left = [inner[TILE * u:TILE * (u + 1)] for u in range(count)]
    right = [vectors[TILE * u:TILE * (u + 1)] for u in range(count)]
    scales = []
    for t in range(count):
        columns = [
            [spread(left[u], TILE * t + j, width) for u in range(t, count)] for j in range(TILE)
        ]
        scale = jnp.zeros((TILE, width), jnp.float32)
        for i in range(TILE):
            lead = columns[i]
            value = lead[0][i:i + 1]
            pivot = 1.0 / value
            scale = jnp.where(rows == i, value, scale)
            for j in range(i + 1, TILE):
                scaled = columns[j][0][i:i + 1] * pivot
                columns[j] = [column - part * scaled for column, part in zip(columns[j], lead)]
            below = [jnp.where(rows > i, lead[0], 0.0)] + lead[1:]
            mate = right[t][i:i + 1] * pivot
            for u in range(t, count):
                right[u] = right[u] - below[u - t] * mate
            if t + 1 < count:
                ahead = left[t][i:i + 1] * pivot[:, :left[t].shape[1]]
                for u in range(t, count):
                    left[u] = left[u] - below[u - t][:, :left[t].shape[1]] * ahead
        scales.append(scale)
    return jnp.concatenate([tile / jnp.sqrt(scale) for tile, scale in zip(right, scales)], axis=0)


def modes_kernel(
    snaps_ref, gram_ref, start_ref, corr_ref, out_ref,
    slots, summed, total, stage, send_sem, recv_sem, send_two, recv_two, send_out, recv_out,
    *, members, owners, own, cell_count,
):
    me_sub = lax.axis_index("sub")
    me_nbhd = lax.axis_index("nbhd")
    size = gram_ref.shape[1]
    chunk = 2 * size // members

    def sub_at(step):
        return lax.rem(me_sub + step, members)

    half = lax.rem(me_sub, 2)
    tower = me_sub - half
    planes = own
    across = owners // planes
    mine = across // 2
    from_half = lax.rem(me_nbhd, across) // mine
    whole = jnp.where(from_half == half, 1, 0)

    barrier = pltpu.get_barrier_semaphore()
    for step in range(1, members):
        pl.semaphore_signal(barrier, inc=1, device_id=(me_nbhd, sub_at(step)), device_id_type=MESH)

    def is_me(nbhd):
        return jnp.logical_and(nbhd == me_nbhd, from_half == half)

    for nbhd in range(owners):
        @pl.when(jnp.logical_not(is_me(nbhd)))
        def _():
            pl.semaphore_signal(
                barrier, inc=1, device_id=(nbhd, tower + from_half), device_id_type=MESH
            )
    pl.semaphore_wait(barrier, members - 1 + owners - whole)

    def part(owner):
        return pl.ds(pl.multiple_of(owner * chunk, chunk), chunk)

    copies = []
    for step in range(1, members):
        peer = sub_at(step)
        copy = pltpu.make_async_remote_copy(
            src_ref=gram_ref.at[part(peer)],
            dst_ref=slots.at[step],
            send_sem=send_sem.at[step],
            recv_sem=recv_sem.at[step],
            device_id=(me_nbhd, peer),
            device_id_type=MESH,
        )
        copy.start()
        copies.append(copy)
    acc = gram_ref[part(me_sub)]
    for step in range(1, members):
        copies[step - 1].wait_recv()
        acc = acc + slots[step]
    summed[...] = acc
    total[part(me_sub)] = acc
    spread = []
    for step in range(1, members):
        copy = pltpu.make_async_remote_copy(
            src_ref=summed,
            dst_ref=total.at[part(me_sub)],
            send_sem=send_two.at[step],
            recv_sem=recv_two.at[step],
            device_id=(me_nbhd, sub_at(step)),
            device_id_type=MESH,
        )
        copy.start()
        spread.append(copy)
    for copy in spread:
        copy.wait_recv()

    dot = functools.partial(
        lax.dot_general, precision=lax.Precision.HIGHEST, preferred_element_type=jnp.float32
    )
    mass = total[:size] / cell_count
    stiff = total[size:]
    stiff = (stiff + stiff.T) * (0.5 / cell_count)
    inverse = eliminate_spd(stiff, size, 32)
    step_map = dot(mass, inverse, (((1,), (0,)), ((), ())))
    both = jnp.concatenate([step_map, dot(step_map, mass, (((1,), (0,)), ((), ())))], axis=1)
    rows = None
    for turn in range(ITERS):
        if turn == 0:
            pair = dot(start_ref[...], both, (((0,), (0,)), ((), ())))
        else:
            pair = dot(rows, both, (((1,), (0,)), ((), ())))
        solved, image = pair[:, :size], pair[:, size:]
        inner = dot(solved, image, (((1,), (1,)), ((), ())))
        inner = 0.5 * (inner + inner.T)
        rows = normalize(inner, solved)
    modes = rows.astype(jnp.bfloat16)

    def piece(index, owner):
        values = lax.dot_general(
            modes, snaps_ref[index], (((1,), (1,)), ((), ())), preferred_element_type=jnp.float32
        )
        return (values * corr_ref[me_nbhd, owner].astype(jnp.float32)).astype(jnp.bfloat16)

    def leave(step, owner, sub):
        return pltpu.make_async_remote_copy(
            src_ref=stage.at[step],
            dst_ref=out_ref.at[me_nbhd],
            send_sem=send_out.at[step],
            recv_sem=recv_out.at[me_nbhd],
            device_id=(owner, sub),
            device_id_type=MESH,
        )

    leaving = []
    for step in range(owners):
        index = lax.rem(step + me_nbhd, owners)
        level = index // mine
        owner = across * lax.rem(level, planes) + mine * half + lax.rem(index, mine)
        sub = tower + level // planes
        here = jnp.logical_and(owner == me_nbhd, sub == me_sub)
        stage[step] = piece(index, owner)

        @pl.when(jnp.logical_not(here))
        def _():
            leave(step, owner, sub).start()

        @pl.when(here)
        def _():
            out_ref[me_nbhd] = stage[step]

        leaving.append((step, owner, sub, here))
    for nbhd in range(owners):
        @pl.when(jnp.logical_not(is_me(nbhd)))
        def _():
            pltpu.make_async_remote_copy(
                src_ref=stage.at[0], dst_ref=out_ref.at[nbhd], send_sem=send_out.at[0],
                recv_sem=recv_out.at[nbhd], device_id=(nbhd, me_sub), device_id_type=MESH,
            ).wait_recv()
    for step, owner, sub, here in leaving:
        @pl.when(jnp.logical_not(here))
        def _():
            leave(step, owner, sub).wait_send()
    for copy in copies + spread:
        copy.wait_send()


def modes_and_pieces(snaps, gram, start, corr, members, owners, own, cell_count):
    pieces, cells, size = snaps.shape
    modes = start.shape[1]
    vmem = pl.BlockSpec(memory_space=pltpu.VMEM)
    return pl.pallas_call(
        functools.partial(
            modes_kernel, members=members, owners=owners, own=own, cell_count=cell_count
        ),
        out_shape=jax.ShapeDtypeStruct((owners, modes, cells), jnp.bfloat16),
        in_specs=[vmem, vmem, vmem, pl.BlockSpec(memory_space=pltpu.SMEM)],
        out_specs=vmem,
        scratch_shapes=[
            pltpu.VMEM((members, 2 * size // members, size), jnp.float32),
            pltpu.VMEM((2 * size // members, size), jnp.float32),
            pltpu.VMEM((2 * size, size), jnp.float32),
            pltpu.VMEM((owners, modes, cells), jnp.bfloat16),
            pltpu.SemaphoreType.DMA((members,)),
            pltpu.SemaphoreType.DMA((members,)),
            pltpu.SemaphoreType.DMA((members,)),
            pltpu.SemaphoreType.DMA((members,)),
            pltpu.SemaphoreType.DMA((owners,)),
            pltpu.SemaphoreType.DMA((owners,)),
        ],
        compiler_params=pltpu.CompilerParams(
            collective_id=1, has_side_effects=True, vmem_limit_bytes=32 << 20
        ),
    )(snaps, gram, start, corr)


def on_device(snap_init, channel_map, yface_vals, zface_vals, face_of, start_block, correlation):
    own, rows, depth, width = snap_init.shape[1:]
    members, owners = lax.axis_size("sub"), lax.axis_size("nbhd")
    state, gram = relax_and_gram(
        snap_init[0], channel_map[0], yface_vals[0], zface_vals[0], face_of, members
    )
    cells = own * rows * depth
    result = modes_and_pieces(
        state.reshape(owners, cells // owners, width), gram, start_block[0], correlation,
        members, owners, own, float(cells * members),
    )
    return result[None, None]


def solution(mesh):
    return jax.shard_map(
        on_device,
        mesh=mesh,
        in_specs=(
            P("nbhd", "sub", None, None, None),
            P("nbhd", "sub", None, None),
            P("nbhd", None, None),
            P("nbhd", None, None),
            P("nbhd", None),
            P("nbhd", None, None),
            P(),
        ),
        out_specs=P("nbhd", "sub", None, None, None),
        check_vma=False,
    )
```

```python
import functools

import jax
import jax.numpy as jnp
from jax import lax
from jax.experimental import pallas as pl
from jax.experimental.pallas import tpu as pltpu
from jax.sharding import PartitionSpec as P

MESH = pl.DeviceIdType.MESH

SWEEPS = 3
ITERS = 4


def harmonic(left_k, right_k):
    return 2.0 * left_k * right_k / (left_k + right_k)


def relax_kernel(
    snap_ref, class_ref, yface_ref, zface_ref, face_ref, state_ref, gram_ref,
    field, coef, compact, select, kappa, ghost_z, early, swap, zland, yland, rhs,
    class_pair, class_low, class_high,
    swap_send, swap_recv, z_send, z_recv, y_send, y_recv, class_send, class_recv,
    *, members,
):
    me_nbhd = lax.axis_index("nbhd")
    me = lax.axis_index("sub")
    half = lax.rem(me, 2)
    tower = me // 2
    towers = members // 2
    own, rows_all, depth, width = snap_ref.shape
    both = 2 * own
    rows = rows_all // 2
    top = both + 1
    base = 8
    inner = pl.ds(base, depth)

    def at(sub):
        return (me_nbhd, lax.rem(sub + members, members))

    partner = at(me + 1 - 2 * half)
    cross = at(me - 1 + 2 * half)
    lower = at(me - 2)
    upper = at(me + 2)

    def remote(src, dst, send, recv, device):
        return pltpu.make_async_remote_copy(
            src_ref=src, dst_ref=dst, send_sem=send, recv_sem=recv,
            device_id=device, device_id_type=MESH,
        )

    barrier = pltpu.get_barrier_semaphore()
    for device in (partner, cross, lower, upper):
        pl.semaphore_signal(barrier, inc=1, device_id=device, device_id_type=MESH)
    pl.semaphore_wait(barrier, 4)

    class_copies = [
        remote(class_ref, class_pair, class_send.at[0], class_recv.at[0], partner),
    ]
    class_copies[0].start()
    class_other = []

    def class_sends(plane, land, slot, devices):
        made = []
        for place, device in enumerate(devices):
            made.append(remote(
                class_ref.at[plane], land, class_send.at[1 + place], class_recv.at[slot], device
            ))
        return made

    @pl.when(half == 0)
    def _():
        for copy in class_sends(0, class_high, 2, (lower, cross)):
            copy.start()

    @pl.when(half == 1)
    def _():
        for copy in class_sends(own - 1, class_low, 1, (upper, cross)):
            copy.start()

    order = [0, 1] + list(range(own - 1, 1, -1))
    swaps = []
    for turn, q in enumerate(order):
        plane = q + half * (own - 1 - 2 * q)
        copy = remote(
            snap_ref.at[plane, pl.ds((rows - 1) * (1 - half), rows + 1)],
            swap.at[turn], swap_send.at[turn], swap_recv.at[turn], partner,
        )
        copy.start()
        swaps.append(copy)

    @pl.when(half == 0)
    def _():
        remote(
            snap_ref.at[0, pl.ds(0, rows)], zland.at[0, 1], z_send.at[0, 0, 0],
            z_recv.at[0, 1, 0], lower
        ).start()

    @pl.when(half == 1)
    def _():
        remote(
            snap_ref.at[own - 1, pl.ds(rows, rows)], zland.at[0, 0], z_send.at[0, 1, 0],
            z_recv.at[0, 0, 0], upper
        ).start()

    shift = 1 - half

    def fill_own(p, _):
        def fill(r, _):
            field[0, 1 + own * half + p, shift + r, inner, :] = snap_ref[
                p, (rows - 1) * half + r
            ].astype(jnp.float32)
            return 0
        return lax.fori_loop(0, rows + 1, fill, 0)

    lax.fori_loop(0, own, fill_own, 0)

    face = face_ref[...]

    def pick(side):
        return jnp.where(face == side, 1.0, 0.0)

    side_y = jnp.where(half == 0, pick(0), pick(1))
    ghost_y = yface_ref[...].astype(jnp.float32) * side_y
    zface = zface_ref[...].astype(jnp.float32)
    ghost_z[0] = zface * pick(2)
    ghost_z[1] = zface * pick(3)

    def set_ghosts(p, _):
        for buf in range(2):
            field[buf, p + 1, (rows + 1) * half, inner, :] = ghost_y

            def one(y, _):
                field[buf, p + 1, y + 1, pl.ds(base - 1, 1), :] = ghost_z[0, pl.ds(rows * half + y, 1), :]
                field[buf, p + 1, y + 1, pl.ds(base + depth, 1), :] = ghost_z[1, pl.ds(rows * half + y, 1), :]
                return 0

            lax.fori_loop(0, rows, one, 0)
        return 0

    lax.fori_loop(0, both, set_ghosts, 0)

    def to_kappa(classes):
        return jnp.left_shift(1, 2 * classes).astype(jnp.float32)

    def land(slot, ref):
        remote(ref, ref, class_send.at[0], class_recv.at[slot], partner).wait_recv()

    land(0, class_pair)
    land(1, class_low)
    land(2, class_high)
    kappa[0] = to_kappa(class_low[...])
    kappa[top] = to_kappa(class_high[...])
    for p in range(own):
        kappa[1 + own * half + p] = to_kappa(class_ref[p])
        kappa[1 + own * (1 - half) + p] = to_kappa(class_pair[p])

    def coefficients(p, _):
        centre = kappa[p + 1]
        has_low = jnp.logical_or(tower > 0, p > 0)
        has_high = jnp.logical_or(tower < towers - 1, p < both - 1)
        face_low = harmonic(centre, kappa[p])
        face_high = harmonic(centre, kappa[p + 2])
        x_lower = jnp.where(has_low, face_low, centre)
        x_upper = jnp.where(has_high, face_high, centre)
        y_inner = harmonic(centre[1:], centre[:-1])
        y_lower = jnp.concatenate([centre[:1], y_inner], axis=0)
        y_upper = jnp.concatenate([y_inner, centre[-1:]], axis=0)
        z_inner = harmonic(centre[:, 1:], centre[:, :-1])
        z_lower = jnp.concatenate([centre[:, :1], z_inner], axis=1)
        z_upper = jnp.concatenate([z_inner, centre[:, -1:]], axis=1)
        denom = x_lower + x_upper + y_lower + y_upper + z_lower + z_upper
        inverse = 1.0 / denom
        compact[0, p] = jnp.where(has_low, face_low, 0.0) * inverse
        compact[1, p] = jnp.where(has_high, face_high, 0.0) * inverse
        compact[2, p] = y_lower * inverse
        compact[3, p] = y_upper * inverse
        compact[4, p] = z_lower * inverse
        compact[5, p] = z_upper * inverse
        compact[6, p] = denom
        compact[7, p] = centre * (1.0 / 16.0)
        return 0

    lax.fori_loop(0, both, coefficients, 0)
    taken = lax.broadcasted_iota(jnp.int32, select.shape, 0)
    given = lax.broadcasted_iota(jnp.int32, select.shape, 1)
    select[...] = jnp.where(lax.rem(taken, rows) == given // width, 1.0, 0.0).astype(jnp.bfloat16)

    def widen(kinds):
        def one(p, _):
            for kind in kinds:
                exact = compact[kind, p, pl.ds(pl.multiple_of(rows * half, rows), rows), :]
                terms = []
                for _ in range(3):
                    term = exact.astype(jnp.bfloat16).astype(jnp.float32)
                    terms.append(term)
                    exact = exact - term
                terms.append(jnp.zeros_like(exact))
                wide = lax.dot_general(
                    jnp.concatenate(terms, axis=0).astype(jnp.bfloat16), select[...],
                    (((0,), (0,)), ((), ())), preferred_element_type=jnp.float32,
                )
                for y in range(rows):
                    coef[kind, p, y] = wide[:, width * y:width * (y + 1)]
            return 0
        lax.fori_loop(0, both, one, 0)

    widen(range(6))

    def row(sweep, p, y):
        src, dst = (sweep + 1) % 2, sweep % 2
        c = [coef.at[kind, p - 1, y - 1] for kind in range(6)]
        value = c[0][...] * field[src, p - 1, y, inner, :]
        value += c[1][...] * field[src, p + 1, y, inner, :]
        value += c[2][...] * field[src, p, y - 1, inner, :]
        value += c[3][...] * field[src, p, y + 1, inner, :]
        value += c[4][...] * field[src, p, y, pl.ds(base - 1, depth), :]
        value += c[5][...] * field[src, p, y, pl.ds(base + 1, depth), :]
        low = value.astype(jnp.bfloat16)
        field[dst, p, y, inner, :] = low.astype(jnp.float32)
        if sweep < SWEEPS:
            early[sweep - 1, p - 1, y - 1] = low
        else:
            state_ref[p - 1, y - 1] = low
            field[dst, p, y, pl.ds(base + depth, 1), :] = jnp.zeros((1, width), jnp.float32)

    def line(sweep, p, first, count):
        def body(i, _):
            row(sweep, p, first + i)
            return 0
        lax.fori_loop(0, count, body, 0)

    chunk = rows // 2
    edge = rows - (rows - 1) * half

    def chunk_at(part):
        return chunk * half if part == 0 else chunk - chunk * half

    def held(sweep):
        return early.at[sweep - 1] if sweep < SWEEPS else state_ref

    def send_z(sweep, side, part):
        cells = pl.ds(chunk_at(part), chunk)
        remote(
            held(sweep).at[side * (both - 1), cells], zland.at[sweep, 1 - side, cells],
            z_send.at[sweep, side, part], z_recv.at[sweep, 1 - side, part], at(me - 2 + 4 * side),
        ).start()

    def send_y(sweep, part, first, count):
        planes = pl.ds(first, count)
        remote(
            held(sweep).at[planes, edge - 1], yland.at[sweep - 1, planes], y_send.at[sweep - 1, part],
            y_recv.at[sweep - 1, part], partner,
        ).start()

    def take_z(buf, sweep, side, part):
        cells = pl.ds(0, rows if sweep == 0 else chunk)
        remote(
            zland.at[sweep, side, cells], zland.at[sweep, side, cells], z_send.at[sweep, side, part],
            z_recv.at[sweep, side, part], lower,
        ).wait_recv()
        first = 0 if sweep == 0 else chunk_at(part)

        def fill(i, _):
            field[buf, top * side, first + i + 1, inner, :] = zland[sweep, side, first + i].astype(
                jnp.float32
            )
            return 0
        lax.fori_loop(0, rows if sweep == 0 else chunk, fill, 0)

    y_parts = ((1, own - 1), (own, own - 1), (0, 1), (both - 1, 1))

    def take_y(buf, sweep, part):
        first, count = y_parts[part]
        planes = pl.ds(first, count)
        remote(
            yland.at[sweep - 1, planes], yland.at[sweep - 1, planes], y_send.at[sweep - 1, part],
            y_recv.at[sweep - 1, part], partner,
        ).wait_recv()

        def fill(i, _):
            p = first + i
            field[buf, p + 1, (rows + 1) * (1 - half), inner, :] = yland[sweep - 1, p].astype(jnp.float32)
            return 0
        lax.fori_loop(0, count, fill, 0)

    def plane_of(e):
        return e + (1 - half) * (top - 2 * e)

    for e in range(own + 2, both):
        line(1, plane_of(e), 1, rows)
    for turn, q in enumerate(order):
        swaps[turn].wait_recv()
        plane = q + (1 - half) * (own - 1 - 2 * q)
        if turn == 0:
            @pl.when(half == 0)
            def _():
                remote(
                    swap.at[0, pl.ds(0, rows)], zland.at[0, 0], z_send.at[0, 1, 0], z_recv.at[0, 0, 0],
                    upper,
                ).start()

            @pl.when(half == 1)
            def _():
                remote(
                    swap.at[0, pl.ds(1, rows)], zland.at[0, 1], z_send.at[0, 0, 0], z_recv.at[0, 1, 0],
                    lower,
                ).start()

        def fill(r, _):
            field[0, 1 + own * (1 - half) + plane, shift + r, inner, :] = swap[turn, r].astype(
                jnp.float32
            )
            return 0

        lax.fori_loop(0, rows + 1, fill, 0)
        if turn == 1:
            take_z(0, 0, 0, 0)
            take_z(0, 0, 1, 0)
            for e, side in ((both, half), (1, 1 - half)):
                line(1, plane_of(e), 1, rows)
                send_z(1, side, 0)
                send_z(1, side, 1)
                send_y(1, 2 + side, side * (both - 1), 1)
        if turn >= 2:
            line(1, plane_of(q + 2), 1, rows)
        if q == own - 1:
            send_y(1, half, 1 + (own - 1) * half, own - 1)
    line(1, plane_of(3), 1, rows)
    line(1, plane_of(2), 1, rows)
    send_y(1, 1 - half, 1 + (own - 1) * (1 - half), own - 1)

    def only_if_last(sweep, action):
        if sweep < SWEEPS:
            action()
        else:
            pl.when(half == 1)(action)

    for sweep in range(2, SWEEPS + 1):
        src = (sweep + 1) % 2
        sides = (0, 1) if sweep < SWEEPS else (0,)

        def middle(i, _):
            line(sweep, i + 2, 1 + half, rows - 1)
            return 0
        lax.fori_loop(0, both - 2, middle, 0)
        if sweep >= SWEEPS - 1:
            widen((8 - 1 - SWEEPS + sweep,))
        for side in (0, 1):
            take_z(src, sweep - 1, side, 0)
            line(sweep, 1 + side * (both - 1), 1 + chunk_at(0), chunk)
            if side in sides:
                send_z(sweep, side, 0)
        take_y(src, sweep - 1, 0)
        take_y(src, sweep - 1, 1)

        def border(i, _):
            row(sweep, i + 2, edge)
            return 0
        lax.fori_loop(0, both - 2, border, 0)

        def first_parts():
            send_y(sweep, 0, *y_parts[0])
            send_y(sweep, 1, *y_parts[1])
        only_if_last(sweep, first_parts)
        for side in (0, 1):
            take_y(src, sweep - 1, 2 + side)
            take_z(src, sweep - 1, side, 1)
            line(sweep, 1 + side * (both - 1), 1 + chunk_at(1), chunk)
            if side in sides:
                send_z(sweep, side, 1)

            def last_part():
                send_y(sweep, 2 + side, *y_parts[2 + side])
            only_if_last(sweep, last_part)

    last = SWEEPS % 2

    def stiff_row(p, y, place):
        here = field[last, p, y, inner, :]
        ahead = coef[1, p - 1, y - 1] * field[last, p + 1, y, inner, :]
        ahead += coef[3, p - 1, y - 1] * field[last, p, y + 1, inner, :]
        ahead += coef[5, p - 1, y - 1] * field[last, p, y, pl.ds(base + 1, depth), :]
        value = coef[6, p - 1, y - 1] * (here - 2.0 * ahead)
        high = value.astype(jnp.bfloat16)
        rest = (value - high.astype(jnp.float32)).astype(jnp.bfloat16)
        rhs[place, :, pl.ds(0, width)] = (here * coef[7, p - 1, y - 1]).astype(jnp.bfloat16)
        rhs[place, :, pl.ds(width, width)] = high
        rhs[place, :, pl.ds(2 * width, width)] = rest

    def gram(left, count):
        right = rhs[pl.ds(0, count)].reshape(count * depth, 3 * width)
        part = lax.dot_general(
            left.reshape(count * depth, width), right, (((0,), (0,)), ((), ())),
            preferred_element_type=jnp.float32,
        )
        gram_ref[pl.ds(0, width), :] += part[:, :width]
        gram_ref[pl.ds(width, width), :] += part[:, width:2 * width] + part[:, 2 * width:]

    gram_ref[...] = jnp.zeros_like(gram_ref)

    def inside(i, _):
        def body(y, _):
            stiff_row(i + 1, y + 1, y)
            return 0
        lax.fori_loop(0, rows - 1, body, 0)
        gram(state_ref[i, pl.ds(0, rows - 1)], rows - 1)
        return 0
    lax.fori_loop(0, both - 1, inside, 0)

    @pl.when(half == 0)
    def _():
        for part in range(4):
            take_y(last, SWEEPS, part)

    @pl.when(half == 1)
    def _():
        def clear(p, _):
            field[last, p + 1, rows + 1, inner, :] = jnp.zeros((depth, width), jnp.float32)
            return 0
        lax.fori_loop(0, both, clear, 0)

    def side(i, _):
        stiff_row(i + 1, rows, i)
        return 0
    lax.fori_loop(0, both - 1, side, 0)
    gram(state_ref[pl.ds(0, both - 1), rows - 1], both - 1)
    take_z(last, SWEEPS, 1, 0)
    take_z(last, SWEEPS, 1, 1)

    def roof(y, _):
        stiff_row(both, y + 1, y)
        return 0
    lax.fori_loop(0, rows, roof, 0)
    gram(state_ref[both - 1], rows)

    class_copies[0].wait_send()
    for place in range(2):
        remote(
            class_ref.at[0], class_low, class_send.at[1 + place], class_recv.at[1], partner
        ).wait_send()
    for copy in swaps:
        copy.wait_send()
    for side in range(2):
        remote(
            snap_ref.at[0, pl.ds(0, rows)], zland.at[0, 0], z_send.at[0, side, 0], z_recv.at[0, 0, 0], lower
        ).wait_send()

    def left_z(sweep, side, part):
        cells = pl.ds(0, chunk)
        remote(
            held(sweep).at[0, cells], zland.at[sweep, 0, cells], z_send.at[sweep, side, part],
            z_recv.at[sweep, 0, part], lower,
        ).wait_send()

    def left_y(sweep, part):
        planes = pl.ds(*y_parts[part])
        remote(
            held(sweep).at[planes, 0], yland.at[sweep - 1, planes], y_send.at[sweep - 1, part],
            y_recv.at[sweep - 1, part], partner,
        ).wait_send()

    for sweep in range(1, SWEEPS + 1):
        for side in range(2 if sweep < SWEEPS else 1):
            for part in range(2):
                left_z(sweep, side, part)

        def all_y():
            for part in range(4):
                left_y(sweep, part)
        only_if_last(sweep, all_y)


def relax_and_gram(snap, classes, yface, zface, face, members):
    own, rows_all, depth, width = snap.shape
    both, rows = 2 * own, rows_all // 2
    vmem = pl.BlockSpec(memory_space=pltpu.VMEM)
    f32, bf16 = jnp.float32, jnp.bfloat16
    dma = pltpu.SemaphoreType.DMA
    return pl.pallas_call(
        functools.partial(relax_kernel, members=members),
        out_shape=(
            jax.ShapeDtypeStruct((both, rows, depth, width), bf16),
            jax.ShapeDtypeStruct((2 * width, width), f32),
        ),
        in_specs=[vmem] * 5,
        out_specs=(vmem, vmem),
        scratch_shapes=[
            pltpu.VMEM((2, both + 2, rows + 2, depth + 16, width), f32),
            pltpu.VMEM((8, both, rows, depth, width), f32),
            pltpu.VMEM((8, both, rows_all, depth), f32),
            pltpu.VMEM((4 * rows, rows * width), bf16),
            pltpu.VMEM((both + 2, rows_all, depth), f32),
            pltpu.VMEM((2, rows_all, width), f32),
            pltpu.VMEM((SWEEPS - 1, both, rows, depth, width), bf16),
            pltpu.VMEM((own, rows + 1, depth, width), bf16),
            pltpu.VMEM((SWEEPS + 1, 2, rows, depth, width), bf16),
            pltpu.VMEM((SWEEPS, both, depth, width), bf16),
            pltpu.VMEM((max(both, rows), depth, 3 * width), bf16),
            pltpu.VMEM((own, rows_all, depth), jnp.int32),
            pltpu.VMEM((rows_all, depth), jnp.int32),
            pltpu.VMEM((rows_all, depth), jnp.int32),
            dma((own,)),
            dma((own,)),
            dma((SWEEPS + 1, 2, 2)),
            dma((SWEEPS + 1, 2, 2)),
            dma((SWEEPS, 4)),
            dma((SWEEPS, 4)),
            dma((3,)),
            dma((3,)),
        ],
        compiler_params=pltpu.CompilerParams(
            collective_id=0, has_side_effects=True, vmem_limit_bytes=60 << 20
        ),
    )(snap, classes, yface, zface, face)


TILE = 8


def spread(tile, col, width):
    return jnp.broadcast_to(tile[:, col:col + 1], (tile.shape[0], width))


def eliminate_spd(full, size, block):
    lanes = lax.broadcasted_iota(jnp.int32, (TILE, size), 1)
    rows = lax.broadcasted_iota(jnp.int32, (TILE, size), 0)
    wide = lax.broadcasted_iota(jnp.int32, (size, size), 1)
    block_lanes = lax.broadcasted_iota(jnp.int32, (block, size), 1)
    count = block // TILE
    for first in range(0, size, block):
        panel = full[first:first + block]
        signed = jnp.where(block_lanes < first, -panel, panel) if first else panel
        tiles = [panel[TILE * u:TILE * (u + 1)] for u in range(count)]
        for t in range(count):
            base = first + TILE * t
            columns = [[spread(tile, base + j, size) for tile in tiles] for j in range(TILE)]
            for i in range(TILE):
                here = rows == i
                at_col = lanes == base + i
                lead = columns[i]
                pivot = 1.0 / lead[t][i:i + 1]
                row = jnp.where(at_col[:1], 1.0, tiles[t][i:i + 1]) * pivot
                for j in range(i + 1, TILE):
                    scaled = columns[j][t][i:i + 1] * pivot
                    columns[j] = [columns[j][u] - lead[u] * scaled for u in range(count)]
                    columns[j][t] = jnp.where(here, scaled, columns[j][t])
                tiles = [jnp.where(at_col, 0.0, tiles[u]) - lead[u] * row for u in range(count)]
                tiles[t] = jnp.where(here, row, tiles[t])
        panel = jnp.concatenate(tiles, axis=0)
        inside = (wide >= first) & (wide < first + block)
        update = lax.dot_general(
            signed, panel, (((0,), (0,)), ((), ())),
            precision=lax.Precision.HIGHEST, preferred_element_type=jnp.float32,
        )
        rest = jnp.where(inside, 0.0, full) - update
        parts = []
        if first:
            parts.append(rest[:first])
        parts.append(panel)
        if first + block < size:
            parts.append(rest[first + block:])
        full = jnp.concatenate(parts, axis=0)
    return full


def normalize(inner, vectors):
    width = vectors.shape[1]
    count = inner.shape[0] // TILE
    rows = lax.broadcasted_iota(jnp.int32, (TILE, width), 0)
    left = [inner[TILE * u:TILE * (u + 1)] for u in range(count)]
    right = [vectors[TILE * u:TILE * (u + 1)] for u in range(count)]
    scales = []
    for t in range(count):
        columns = [
            [spread(left[u], TILE * t + j, width) for u in range(t, count)] for j in range(TILE)
        ]
        scale = jnp.zeros((TILE, width), jnp.float32)
        for i in range(TILE):
            lead = columns[i]
            value = lead[0][i:i + 1]
            pivot = 1.0 / value
            scale = jnp.where(rows == i, value, scale)
            for j in range(i + 1, TILE):
                scaled = columns[j][0][i:i + 1] * pivot
                columns[j] = [column - part * scaled for column, part in zip(columns[j], lead)]
            below = [jnp.where(rows > i, lead[0], 0.0)] + lead[1:]
            mate = right[t][i:i + 1] * pivot
            for u in range(t, count):
                right[u] = right[u] - below[u - t] * mate
            if t + 1 < count:
                ahead = left[t][i:i + 1] * pivot[:, :left[t].shape[1]]
                for u in range(t, count):
                    left[u] = left[u] - below[u - t][:, :left[t].shape[1]] * ahead
        scales.append(scale)
    return jnp.concatenate([tile / jnp.sqrt(scale) for tile, scale in zip(right, scales)], axis=0)


def modes_kernel(
    snaps_ref, gram_ref, start_ref, corr_ref, out_ref,
    slots, summed, total, stage, send_sem, recv_sem, send_two, recv_two, send_out, recv_out,
    *, members, owners, own, cell_count,
):
    me_sub = lax.axis_index("sub")
    me_nbhd = lax.axis_index("nbhd")
    size = gram_ref.shape[1]
    chunk = 2 * size // members

    def sub_at(step):
        return lax.rem(me_sub + step, members)

    half = lax.rem(me_sub, 2)
    tower = me_sub - half
    planes = own
    across = owners // planes
    mine = across // 2
    from_half = lax.rem(me_nbhd, across) // mine
    whole = jnp.where(from_half == half, 1, 0)

    barrier = pltpu.get_barrier_semaphore()
    for step in range(1, members):
        pl.semaphore_signal(barrier, inc=1, device_id=(me_nbhd, sub_at(step)), device_id_type=MESH)

    def is_me(nbhd):
        return jnp.logical_and(nbhd == me_nbhd, from_half == half)

    for nbhd in range(owners):
        @pl.when(jnp.logical_not(is_me(nbhd)))
        def _():
            pl.semaphore_signal(
                barrier, inc=1, device_id=(nbhd, tower + from_half), device_id_type=MESH
            )
    pl.semaphore_wait(barrier, members - 1 + owners - whole)

    def part(owner):
        return pl.ds(pl.multiple_of(owner * chunk, chunk), chunk)

    copies = []
    for step in range(1, members):
        peer = sub_at(step)
        copy = pltpu.make_async_remote_copy(
            src_ref=gram_ref.at[part(peer)],
            dst_ref=slots.at[step],
            send_sem=send_sem.at[step],
            recv_sem=recv_sem.at[step],
            device_id=(me_nbhd, peer),
            device_id_type=MESH,
        )
        copy.start()
        copies.append(copy)
    acc = gram_ref[part(me_sub)]
    for step in range(1, members):
        copies[step - 1].wait_recv()
        acc = acc + slots[step]
    summed[...] = acc
    total[part(me_sub)] = acc
    spread = []
    for step in range(1, members):
        copy = pltpu.make_async_remote_copy(
            src_ref=summed,
            dst_ref=total.at[part(me_sub)],
            send_sem=send_two.at[step],
            recv_sem=recv_two.at[step],
            device_id=(me_nbhd, sub_at(step)),
            device_id_type=MESH,
        )
        copy.start()
        spread.append(copy)
    for copy in spread:
        copy.wait_recv()

    dot = functools.partial(
        lax.dot_general, precision=lax.Precision.HIGHEST, preferred_element_type=jnp.float32
    )
    mass = total[:size] / cell_count
    stiff = total[size:]
    stiff = (stiff + stiff.T) * (0.5 / cell_count)
    inverse = eliminate_spd(stiff, size, 32)
    step_map = dot(mass, inverse, (((1,), (0,)), ((), ())))
    both = jnp.concatenate([step_map, dot(step_map, mass, (((1,), (0,)), ((), ())))], axis=1)
    rows = start_ref[...]
    for turn in range(ITERS):
        pair = dot(rows, both, (((1,), (0,)), ((), ())))
        solved, image = pair[:, :size], pair[:, size:]
        inner = dot(solved, image, (((1,), (1,)), ((), ())))
        inner = 0.5 * (inner + inner.T)
        rows = normalize(inner, solved)
    modes = rows.astype(jnp.bfloat16)

    def piece(index, owner):
        values = lax.dot_general(
            modes, snaps_ref[index], (((1,), (1,)), ((), ())), preferred_element_type=jnp.float32
        )
        return (values * corr_ref[me_nbhd, owner].astype(jnp.float32)).astype(jnp.bfloat16)

    def leave(step, owner, sub):
        return pltpu.make_async_remote_copy(
            src_ref=stage.at[step],
            dst_ref=out_ref.at[me_nbhd],
            send_sem=send_out.at[step],
            recv_sem=recv_out.at[me_nbhd],
            device_id=(owner, sub),
            device_id_type=MESH,
        )

    leaving = []
    for step in range(owners):
        index = lax.rem(step + me_nbhd, owners)
        level = index // mine
        owner = across * lax.rem(level, planes) + mine * half + lax.rem(index, mine)
        sub = tower + level // planes
        here = jnp.logical_and(owner == me_nbhd, sub == me_sub)
        stage[step] = piece(index, owner)

        @pl.when(jnp.logical_not(here))
        def _():
            leave(step, owner, sub).start()

        @pl.when(here)
        def _():
            out_ref[me_nbhd] = stage[step]

        leaving.append((step, owner, sub, here))
    for nbhd in range(owners):
        @pl.when(jnp.logical_not(is_me(nbhd)))
        def _():
            pltpu.make_async_remote_copy(
                src_ref=stage.at[0], dst_ref=out_ref.at[nbhd], send_sem=send_out.at[0],
                recv_sem=recv_out.at[nbhd], device_id=(nbhd, me_sub), device_id_type=MESH,
            ).wait_recv()
    for step, owner, sub, here in leaving:
        @pl.when(jnp.logical_not(here))
        def _():
            leave(step, owner, sub).wait_send()
    for copy in copies + spread:
        copy.wait_send()


def modes_and_pieces(snaps, gram, start, corr, members, owners, own, cell_count):
    pieces, cells, size = snaps.shape
    modes = start.shape[0]
    vmem = pl.BlockSpec(memory_space=pltpu.VMEM)
    return pl.pallas_call(
        functools.partial(
            modes_kernel, members=members, owners=owners, own=own, cell_count=cell_count
        ),
        out_shape=jax.ShapeDtypeStruct((owners, modes, cells), jnp.bfloat16),
        in_specs=[vmem, vmem, vmem, pl.BlockSpec(memory_space=pltpu.SMEM)],
        out_specs=vmem,
        scratch_shapes=[
            pltpu.VMEM((members, 2 * size // members, size), jnp.float32),
            pltpu.VMEM((2 * size // members, size), jnp.float32),
            pltpu.VMEM((2 * size, size), jnp.float32),
            pltpu.VMEM((owners, modes, cells), jnp.bfloat16),
            pltpu.SemaphoreType.DMA((members,)),
            pltpu.SemaphoreType.DMA((members,)),
            pltpu.SemaphoreType.DMA((members,)),
            pltpu.SemaphoreType.DMA((members,)),
            pltpu.SemaphoreType.DMA((owners,)),
            pltpu.SemaphoreType.DMA((owners,)),
        ],
        compiler_params=pltpu.CompilerParams(
            collective_id=1, has_side_effects=True, vmem_limit_bytes=32 << 20
        ),
    )(snaps, gram, start, corr)


def on_device(snap_init, channel_map, yface_vals, zface_vals, face_of, start_block, correlation):
    own, rows, depth, width = snap_init.shape[1:]
    members, owners = lax.axis_size("sub"), lax.axis_size("nbhd")
    state, gram = relax_and_gram(
        snap_init[0], channel_map[0], yface_vals[0], zface_vals[0], face_of, members
    )
    cells = own * rows * depth
    result = modes_and_pieces(
        state.reshape(owners, cells // owners, width), gram, start_block[0].T, correlation,
        members, owners, own, float(cells * members),
    )
    return result[None, None]


def solution(mesh):
    return jax.shard_map(
        on_device,
        mesh=mesh,
        in_specs=(
            P("nbhd", "sub", None, None, None),
            P("nbhd", "sub", None, None),
            P("nbhd", None, None),
            P("nbhd", None, None),
            P("nbhd", None),
            P("nbhd", None, None),
            P(),
        ),
        out_specs=P("nbhd", "sub", None, None, None),
        check_vma=False,
    )
```

```python
import functools

import jax
import jax.numpy as jnp
from jax import lax
from jax.experimental import pallas as pl
from jax.experimental.pallas import tpu as pltpu
from jax.sharding import PartitionSpec as P

MESH = pl.DeviceIdType.MESH

SWEEPS = 3
ITERS = 4


def harmonic(left_k, right_k):
    return 2.0 * left_k * right_k / (left_k + right_k)


def relax_part(
    snap_ref, class_ref, yface_ref, zface_ref, face_ref, state_ref, mass_ref, stiff_ref,
    field, coef, compact, select, kappa, ghost_z, early, swap, zland, yland, rhs,
    class_pair, class_low, class_high, slab, slab_sem,
    swap_send, swap_recv, z_send, z_recv, y_send, y_recv, class_send, class_recv,
    members, mass_ready,
):
    me_nbhd = lax.axis_index("nbhd")
    me = lax.axis_index("sub")
    half = lax.rem(me, 2)
    tower = me // 2
    towers = members // 2
    own, rows_all, depth, width = snap_ref.shape
    both = 2 * own
    rows = rows_all // 2
    top = both + 1
    base = 8
    inner = pl.ds(base, depth)

    def at(sub):
        return (me_nbhd, lax.rem(sub + members, members))

    partner = at(me + 1 - 2 * half)
    cross = at(me - 1 + 2 * half)
    lower = at(me - 2)
    upper = at(me + 2)

    def remote(src, dst, send, recv, device):
        return pltpu.make_async_remote_copy(
            src_ref=src, dst_ref=dst, send_sem=send, recv_sem=recv,
            device_id=device, device_id_type=MESH,
        )

    class_copies = [
        remote(class_ref, class_pair, class_send.at[0], class_recv.at[0], partner),
    ]
    class_copies[0].start()
    class_other = []

    def class_sends(plane, land, slot, devices):
        made = []
        for place, device in enumerate(devices):
            made.append(remote(
                class_ref.at[plane], land, class_send.at[1 + place], class_recv.at[slot], device
            ))
        return made

    @pl.when(half == 0)
    def _():
        for copy in class_sends(0, class_high, 2, (lower, cross)):
            copy.start()

    @pl.when(half == 1)
    def _():
        for copy in class_sends(own - 1, class_low, 1, (upper, cross)):
            copy.start()

    order = [0, 1] + list(range(own - 1, 1, -1))
    swaps = []
    for turn, q in enumerate(order):
        plane = q + half * (own - 1 - 2 * q)
        copy = remote(
            snap_ref.at[plane, pl.ds((rows - 1) * (1 - half), rows + 1)],
            swap.at[turn], swap_send.at[turn], swap_recv.at[turn], partner,
        )
        copy.start()
        swaps.append(copy)

    @pl.when(half == 0)
    def _():
        remote(
            snap_ref.at[0, pl.ds(0, rows)], zland.at[0, 1], z_send.at[0, 0, 0],
            z_recv.at[0, 1, 0], lower
        ).start()

    @pl.when(half == 1)
    def _():
        remote(
            snap_ref.at[own - 1, pl.ds(rows, rows)], zland.at[0, 0], z_send.at[0, 1, 0],
            z_recv.at[0, 0, 0], upper
        ).start()

    shift = 1 - half

    def fill_own(p, _):
        def fill(r, _):
            field[0, 1 + own * half + p, shift + r, inner, :] = slab[
                p, (rows - 1) * half + r
            ].astype(jnp.float32)
            return 0
        return lax.fori_loop(0, rows + 1, fill, 0)

    pltpu.make_async_copy(snap_ref, slab, slab_sem).wait()
    lax.fori_loop(0, own, fill_own, 0)

    face = face_ref[...]

    def pick(side):
        return jnp.where(face == side, 1.0, 0.0)

    side_y = jnp.where(half == 0, pick(0), pick(1))
    ghost_y = yface_ref[...].astype(jnp.float32) * side_y
    zface = zface_ref[...].astype(jnp.float32)
    ghost_z[0] = zface * pick(2)
    ghost_z[1] = zface * pick(3)

    def set_ghosts(p, _):
        for buf in range(2):
            field[buf, p + 1, (rows + 1) * half, inner, :] = ghost_y

            def one(y, _):
                field[buf, p + 1, y + 1, pl.ds(base - 1, 1), :] = ghost_z[0, pl.ds(rows * half + y, 1), :]
                field[buf, p + 1, y + 1, pl.ds(base + depth, 1), :] = ghost_z[1, pl.ds(rows * half + y, 1), :]
                return 0

            lax.fori_loop(0, rows, one, 0)
        return 0

    lax.fori_loop(0, both, set_ghosts, 0)

    def to_kappa(classes):
        return jnp.left_shift(1, 2 * classes).astype(jnp.float32)

    def land(slot, ref):
        remote(ref, ref, class_send.at[0], class_recv.at[slot], partner).wait_recv()

    land(0, class_pair)
    land(1, class_low)
    land(2, class_high)
    kappa[0] = to_kappa(class_low[...])
    kappa[top] = to_kappa(class_high[...])
    for p in range(own):
        kappa[1 + own * half + p] = to_kappa(class_ref[p])
        kappa[1 + own * (1 - half) + p] = to_kappa(class_pair[p])

    def coefficients(p, _):
        centre = kappa[p + 1]
        has_low = jnp.logical_or(tower > 0, p > 0)
        has_high = jnp.logical_or(tower < towers - 1, p < both - 1)
        face_low = harmonic(centre, kappa[p])
        face_high = harmonic(centre, kappa[p + 2])
        x_lower = jnp.where(has_low, face_low, centre)
        x_upper = jnp.where(has_high, face_high, centre)
        y_inner = harmonic(centre[1:], centre[:-1])
        y_lower = jnp.concatenate([centre[:1], y_inner], axis=0)
        y_upper = jnp.concatenate([y_inner, centre[-1:]], axis=0)
        z_inner = harmonic(centre[:, 1:], centre[:, :-1])
        z_lower = jnp.concatenate([centre[:, :1], z_inner], axis=1)
        z_upper = jnp.concatenate([z_inner, centre[:, -1:]], axis=1)
        denom = x_lower + x_upper + y_lower + y_upper + z_lower + z_upper
        inverse = 1.0 / denom
        compact[0, p] = jnp.where(has_low, face_low, 0.0) * inverse
        compact[1, p] = jnp.where(has_high, face_high, 0.0) * inverse
        compact[2, p] = y_lower * inverse
        compact[3, p] = y_upper * inverse
        compact[4, p] = z_lower * inverse
        compact[5, p] = z_upper * inverse
        compact[6, p] = denom
        compact[7, p] = centre * (1.0 / 16.0)
        return 0

    lax.fori_loop(0, both, coefficients, 0)
    taken = lax.broadcasted_iota(jnp.int32, select.shape, 0)
    given = lax.broadcasted_iota(jnp.int32, select.shape, 1)
    select[...] = jnp.where(lax.rem(taken, rows) == given // width, 1.0, 0.0).astype(jnp.bfloat16)

    def widen(kinds):
        def one(p, _):
            for kind in kinds:
                exact = compact[kind, p, pl.ds(pl.multiple_of(rows * half, rows), rows), :]
                terms = []
                for _ in range(3):
                    term = exact.astype(jnp.bfloat16).astype(jnp.float32)
                    terms.append(term)
                    exact = exact - term
                terms.append(jnp.zeros_like(exact))
                wide = lax.dot_general(
                    jnp.concatenate(terms, axis=0).astype(jnp.bfloat16), select[...],
                    (((0,), (0,)), ((), ())), preferred_element_type=jnp.float32,
                )
                for y in range(rows):
                    coef[kind, p, y] = wide[:, width * y:width * (y + 1)]
            return 0
        lax.fori_loop(0, both, one, 0)

    widen(range(6))

    def row(sweep, p, y):
        src, dst = (sweep + 1) % 2, sweep % 2
        c = [coef.at[kind, p - 1, y - 1] for kind in range(6)]
        value = c[0][...] * field[src, p - 1, y, inner, :]
        value += c[1][...] * field[src, p + 1, y, inner, :]
        value += c[2][...] * field[src, p, y - 1, inner, :]
        value += c[3][...] * field[src, p, y + 1, inner, :]
        value += c[4][...] * field[src, p, y, pl.ds(base - 1, depth), :]
        value += c[5][...] * field[src, p, y, pl.ds(base + 1, depth), :]
        low = value.astype(jnp.bfloat16)
        field[dst, p, y, inner, :] = low.astype(jnp.float32)
        if sweep < SWEEPS:
            early[sweep - 1, p - 1, y - 1] = low
        else:
            state_ref[p - 1, y - 1] = low
            field[dst, p, y, pl.ds(base + depth, 1), :] = jnp.zeros((1, width), jnp.float32)

    def line(sweep, p, first, count):
        def body(i, _):
            row(sweep, p, first + i)
            return 0
        lax.fori_loop(0, count, body, 0)

    chunk = rows // 2
    edge = rows - (rows - 1) * half

    def chunk_at(part):
        return chunk * half if part == 0 else chunk - chunk * half

    def held(sweep):
        return early.at[sweep - 1] if sweep < SWEEPS else state_ref

    def send_z(sweep, side, part):
        cells = pl.ds(chunk_at(part), chunk)
        remote(
            held(sweep).at[side * (both - 1), cells], zland.at[sweep, 1 - side, cells],
            z_send.at[sweep, side, part], z_recv.at[sweep, 1 - side, part], at(me - 2 + 4 * side),
        ).start()

    def send_y(sweep, part, first, count):
        planes = pl.ds(first, count)
        remote(
            held(sweep).at[planes, edge - 1], yland.at[sweep - 1, planes], y_send.at[sweep - 1, part],
            y_recv.at[sweep - 1, part], partner,
        ).start()

    def take_z(buf, sweep, side, part):
        cells = pl.ds(0, rows if sweep == 0 else chunk)
        remote(
            zland.at[sweep, side, cells], zland.at[sweep, side, cells], z_send.at[sweep, side, part],
            z_recv.at[sweep, side, part], lower,
        ).wait_recv()
        first = 0 if sweep == 0 else chunk_at(part)

        def fill(i, _):
            field[buf, top * side, first + i + 1, inner, :] = zland[sweep, side, first + i].astype(
                jnp.float32
            )
            return 0
        lax.fori_loop(0, rows if sweep == 0 else chunk, fill, 0)

    y_parts = ((1, own - 1), (own, own - 1), (0, 1), (both - 1, 1))

    def take_y(buf, sweep, part):
        first, count = y_parts[part]
        planes = pl.ds(first, count)
        remote(
            yland.at[sweep - 1, planes], yland.at[sweep - 1, planes], y_send.at[sweep - 1, part],
            y_recv.at[sweep - 1, part], partner,
        ).wait_recv()

        def fill(i, _):
            p = first + i
            field[buf, p + 1, (rows + 1) * (1 - half), inner, :] = yland[sweep - 1, p].astype(jnp.float32)
            return 0
        lax.fori_loop(0, count, fill, 0)

    def plane_of(e):
        return e + (1 - half) * (top - 2 * e)

    for e in range(own + 2, both):
        line(1, plane_of(e), 1, rows)
    for turn, q in enumerate(order):
        swaps[turn].wait_recv()
        plane = q + (1 - half) * (own - 1 - 2 * q)
        if turn == 0:
            @pl.when(half == 0)
            def _():
                remote(
                    swap.at[0, pl.ds(0, rows)], zland.at[0, 0], z_send.at[0, 1, 0], z_recv.at[0, 0, 0],
                    upper,
                ).start()

            @pl.when(half == 1)
            def _():
                remote(
                    swap.at[0, pl.ds(1, rows)], zland.at[0, 1], z_send.at[0, 0, 0], z_recv.at[0, 1, 0],
                    lower,
                ).start()

        def fill(r, _):
            field[0, 1 + own * (1 - half) + plane, shift + r, inner, :] = swap[turn, r].astype(
                jnp.float32
            )
            return 0

        lax.fori_loop(0, rows + 1, fill, 0)
        if turn == 1:
            take_z(0, 0, 0, 0)
            take_z(0, 0, 1, 0)
            for e, side in ((both, half), (1, 1 - half)):
                line(1, plane_of(e), 1, rows)
                send_z(1, side, 0)
                send_z(1, side, 1)
                send_y(1, 2 + side, side * (both - 1), 1)
        if turn >= 2:
            line(1, plane_of(q + 2), 1, rows)
        if q == own - 1:
            send_y(1, half, 1 + (own - 1) * half, own - 1)
    line(1, plane_of(3), 1, rows)
    line(1, plane_of(2), 1, rows)
    send_y(1, 1 - half, 1 + (own - 1) * (1 - half), own - 1)

    def only_if_last(sweep, action):
        if sweep < SWEEPS:
            action()
        else:
            pl.when(half == 1)(action)

    for sweep in range(2, SWEEPS + 1):
        src = (sweep + 1) % 2
        sides = (0, 1) if sweep < SWEEPS else (0,)

        def middle(i, _):
            line(sweep, i + 2, 1 + half, rows - 1)
            return 0
        lax.fori_loop(0, both - 2, middle, 0)
        if sweep >= SWEEPS - 1:
            widen((8 - 1 - SWEEPS + sweep,))
        for side in (0, 1):
            take_z(src, sweep - 1, side, 0)
            line(sweep, 1 + side * (both - 1), 1 + chunk_at(0), chunk)
            if side in sides:
                send_z(sweep, side, 0)
        take_y(src, sweep - 1, 0)
        take_y(src, sweep - 1, 1)

        def border(i, _):
            row(sweep, i + 2, edge)
            return 0
        lax.fori_loop(0, both - 2, border, 0)

        def first_parts():
            send_y(sweep, 0, *y_parts[0])
            send_y(sweep, 1, *y_parts[1])
        only_if_last(sweep, first_parts)
        for side in (0, 1):
            take_y(src, sweep - 1, 2 + side)
            take_z(src, sweep - 1, side, 1)
            line(sweep, 1 + side * (both - 1), 1 + chunk_at(1), chunk)
            if side in sides:
                send_z(sweep, side, 1)

            def last_part():
                send_y(sweep, 2 + side, *y_parts[2 + side])
            only_if_last(sweep, last_part)

    last = SWEEPS % 2

    def stiff_row(p, y, place):
        here = field[last, p, y, inner, :]
        ahead = coef[1, p - 1, y - 1] * field[last, p + 1, y, inner, :]
        ahead += coef[3, p - 1, y - 1] * field[last, p, y + 1, inner, :]
        ahead += coef[5, p - 1, y - 1] * field[last, p, y, pl.ds(base + 1, depth), :]
        value = coef[6, p - 1, y - 1] * (here - 2.0 * ahead)
        high = value.astype(jnp.bfloat16)
        rest = (value - high.astype(jnp.float32)).astype(jnp.bfloat16)
        rhs[place, :, pl.ds(0, width)] = high
        rhs[place, :, pl.ds(width, width)] = rest

    def gram(left, count, used):
        right = rhs[pl.ds(0, count), :, pl.ds(0, used)].reshape(count * depth, used)
        return lax.dot_general(
            left.reshape(count * depth, width), right, (((0,), (0,)), ((), ())),
            preferred_element_type=jnp.float32,
        )

    def add_stiff(left, count):
        terms = gram(left, count, 2 * width)
        stiff_ref[...] += terms[:, :width] + terms[:, width:]

    mass_ref[...] = jnp.zeros_like(mass_ref)
    stiff_ref[...] = jnp.zeros_like(stiff_ref)

    def weigh(p, _):
        def body(y, _):
            here = state_ref[p, y].astype(jnp.float32)
            rhs[y, :, pl.ds(0, width)] = (here * coef[7, p, y]).astype(jnp.bfloat16)
            return 0
        lax.fori_loop(0, rows, body, 0)
        mass_ref[...] += gram(state_ref[p], rows, width)
        return 0
    lax.fori_loop(0, both, weigh, 0)
    mass_ready()

    def inside(i, _):
        def body(y, _):
            stiff_row(i + 1, y + 1, y)
            return 0
        lax.fori_loop(0, rows - 1, body, 0)
        add_stiff(state_ref[i, pl.ds(0, rows - 1)], rows - 1)
        return 0
    lax.fori_loop(0, both - 1, inside, 0)

    @pl.when(half == 0)
    def _():
        for part in range(4):
            take_y(last, SWEEPS, part)

    @pl.when(half == 1)
    def _():
        def clear(p, _):
            field[last, p + 1, rows + 1, inner, :] = jnp.zeros((depth, width), jnp.float32)
            return 0
        lax.fori_loop(0, both, clear, 0)

    def side(i, _):
        stiff_row(i + 1, rows, i)
        return 0
    lax.fori_loop(0, both - 1, side, 0)
    add_stiff(state_ref[pl.ds(0, both - 1), rows - 1], both - 1)
    take_z(last, SWEEPS, 1, 0)
    take_z(last, SWEEPS, 1, 1)

    def roof(y, _):
        stiff_row(both, y + 1, y)
        return 0
    lax.fori_loop(0, rows, roof, 0)
    add_stiff(state_ref[both - 1], rows)

    def drain():
        class_copies[0].wait_send()
        for place in range(2):
            remote(
                class_ref.at[0], class_low, class_send.at[1 + place], class_recv.at[1], partner
            ).wait_send()
        for copy in swaps:
            copy.wait_send()
        for side in range(2):
            remote(
                snap_ref.at[0, pl.ds(0, rows)], zland.at[0, 0], z_send.at[0, side, 0], z_recv.at[0, 0, 0], lower
            ).wait_send()

        def left_z(sweep, side, part):
            cells = pl.ds(0, chunk)
            remote(
                held(sweep).at[0, cells], zland.at[sweep, 0, cells], z_send.at[sweep, side, part],
                z_recv.at[sweep, 0, part], lower,
            ).wait_send()

        def left_y(sweep, part):
            planes = pl.ds(*y_parts[part])
            remote(
                held(sweep).at[planes, 0], yland.at[sweep - 1, planes], y_send.at[sweep - 1, part],
                y_recv.at[sweep - 1, part], partner,
            ).wait_send()

        for sweep in range(1, SWEEPS + 1):
            for side in range(2 if sweep < SWEEPS else 1):
                for part in range(2):
                    left_z(sweep, side, part)

            def all_y():
                for part in range(4):
                    left_y(sweep, part)
            only_if_last(sweep, all_y)

    return drain


TILE = 8


def spread(tile, col, width):
    return jnp.broadcast_to(tile[:, col:col + 1], (tile.shape[0], width))


def eliminate_spd(full, size, block):
    lanes = lax.broadcasted_iota(jnp.int32, (TILE, size), 1)
    rows = lax.broadcasted_iota(jnp.int32, (TILE, size), 0)
    wide = lax.broadcasted_iota(jnp.int32, (size, size), 1)
    block_lanes = lax.broadcasted_iota(jnp.int32, (block, size), 1)
    count = block // TILE
    for first in range(0, size, block):
        panel = full[first:first + block]
        signed = jnp.where(block_lanes < first, -panel, panel) if first else panel
        tiles = [panel[TILE * u:TILE * (u + 1)] for u in range(count)]
        for t in range(count):
            base = first + TILE * t
            columns = [[spread(tile, base + j, size) for tile in tiles] for j in range(TILE)]
            for i in range(TILE):
                here = rows == i
                at_col = lanes == base + i
                lead = columns[i]
                pivot = 1.0 / lead[t][i:i + 1]
                row = jnp.where(at_col[:1], 1.0, tiles[t][i:i + 1]) * pivot
                for j in range(i + 1, TILE):
                    scaled = columns[j][t][i:i + 1] * pivot
                    columns[j] = [columns[j][u] - lead[u] * scaled for u in range(count)]
                    columns[j][t] = jnp.where(here, scaled, columns[j][t])
                tiles = [jnp.where(at_col, 0.0, tiles[u]) - lead[u] * row for u in range(count)]
                tiles[t] = jnp.where(here, row, tiles[t])
        panel = jnp.concatenate(tiles, axis=0)
        inside = (wide >= first) & (wide < first + block)
        update = lax.dot_general(
            signed, panel, (((0,), (0,)), ((), ())),
            precision=lax.Precision.HIGHEST, preferred_element_type=jnp.float32,
        )
        rest = jnp.where(inside, 0.0, full) - update
        parts = []
        if first:
            parts.append(rest[:first])
        parts.append(panel)
        if first + block < size:
            parts.append(rest[first + block:])
        full = jnp.concatenate(parts, axis=0)
    return full


def normalize(inner, vectors):
    width = vectors.shape[1]
    count = inner.shape[0] // TILE
    rows = lax.broadcasted_iota(jnp.int32, (TILE, width), 0)
    left = [inner[TILE * u:TILE * (u + 1)] for u in range(count)]
    right = [vectors[TILE * u:TILE * (u + 1)] for u in range(count)]
    scales = []
    for t in range(count):
        columns = [
            [spread(left[u], TILE * t + j, width) for u in range(t, count)] for j in range(TILE)
        ]
        scale = jnp.zeros((TILE, width), jnp.float32)
        for i in range(TILE):
            lead = columns[i]
            value = lead[0][i:i + 1]
            pivot = 1.0 / value
            scale = jnp.where(rows == i, value, scale)
            for j in range(i + 1, TILE):
                scaled = columns[j][0][i:i + 1] * pivot
                columns[j] = [column - part * scaled for column, part in zip(columns[j], lead)]
            below = [jnp.where(rows > i, lead[0], 0.0)] + lead[1:]
            mate = right[t][i:i + 1] * pivot
            for u in range(t, count):
                right[u] = right[u] - below[u - t] * mate
            if t + 1 < count:
                ahead = left[t][i:i + 1] * pivot[:, :left[t].shape[1]]
                for u in range(t, count):
                    left[u] = left[u] - below[u - t][:, :left[t].shape[1]] * ahead
        scales.append(scale)
    return jnp.concatenate([tile / jnp.sqrt(scale) for tile, scale in zip(right, scales)], axis=0)


def whole_kernel(
    snap_ref, class_ref, yface_ref, zface_ref, face_ref, start_ref, corr_ref, out_ref,
    field, coef, compact, select, kappa, ghost_z, early, swap, zland, yland, rhs,
    class_pair, class_low, class_high, slab, slab_sem,
    swap_send, swap_recv, z_send, z_recv, y_send, y_recv, class_send, class_recv,
    state, mass_part, stiff_part, slots, summed, mass_total, stiff_total, stage,
    sum_sem, send_out, recv_out,
    *, members, owners, own, cell_count,
):
    me_sub = lax.axis_index("sub")
    me_nbhd = lax.axis_index("nbhd")
    size = mass_part.shape[1]
    chunk = size // members
    half = lax.rem(me_sub, 2)
    tower = me_sub - half
    across = owners // own
    mine = across // 2
    from_half = lax.rem(me_nbhd, across) // mine
    whole = jnp.where(from_half == half, 1, 0)

    pltpu.make_async_copy(snap_ref, slab, slab_sem).start()

    def sub_at(step):
        return lax.rem(me_sub + step, members)

    def is_me(nbhd):
        return jnp.logical_and(nbhd == me_nbhd, from_half == half)

    barrier = pltpu.get_barrier_semaphore()
    for step in range(1, members):
        pl.semaphore_signal(barrier, inc=1, device_id=(me_nbhd, sub_at(step)), device_id_type=MESH)
    for nbhd in range(owners):
        @pl.when(jnp.logical_not(is_me(nbhd)))
        def _():
            pl.semaphore_signal(
                barrier, inc=1, device_id=(nbhd, tower + from_half), device_id_type=MESH
            )
    pl.semaphore_wait(barrier, members - 1 + owners - whole)

    def rows_of(sub):
        return pl.ds(pl.multiple_of(sub * chunk, chunk), chunk)

    def scatter(which, partial_ref):
        copies = []
        for step in range(1, members):
            peer = sub_at(step)
            copy = pltpu.make_async_remote_copy(
                src_ref=partial_ref.at[rows_of(peer)],
                dst_ref=slots.at[which, step],
                send_sem=sum_sem.at[which, 0, step],
                recv_sem=sum_sem.at[which, 1, step],
                device_id=(me_nbhd, peer),
                device_id_type=MESH,
            )
            copy.start()
            copies.append(copy)
        return copies

    def share(which, partial_ref, total_ref, copies):
        acc = partial_ref[rows_of(me_sub)]
        for step in range(1, members):
            copies[step - 1].wait_recv()
            acc = acc + slots[which, step]
        summed[which] = acc
        total_ref[rows_of(me_sub)] = acc
        spreads = []
        for step in range(1, members):
            copy = pltpu.make_async_remote_copy(
                src_ref=summed.at[which],
                dst_ref=total_ref.at[rows_of(me_sub)],
                send_sem=sum_sem.at[which, 2, step],
                recv_sem=sum_sem.at[which, 3, step],
                device_id=(me_nbhd, sub_at(step)),
                device_id_type=MESH,
            )
            copy.start()
            spreads.append(copy)
        return spreads

    sent = []
    drain = relax_part(
        snap_ref, class_ref, yface_ref, zface_ref, face_ref, state, mass_part, stiff_part,
        field, coef, compact, select, kappa, ghost_z, early, swap, zland, yland, rhs,
        class_pair, class_low, class_high, slab, slab_sem,
        swap_send, swap_recv, z_send, z_recv, y_send, y_recv, class_send, class_recv,
        members, lambda: sent.append(scatter(0, mass_part)),
    )
    sent.append(scatter(1, stiff_part))
    sent.append(share(0, mass_part, mass_total, sent[0]))
    sent.append(share(1, stiff_part, stiff_total, sent[1]))

    dot = functools.partial(
        lax.dot_general, precision=lax.Precision.HIGHEST, preferred_element_type=jnp.float32
    )
    for copy in sent[3]:
        copy.wait_recv()
    stiff = stiff_total[...]
    stiff = (stiff + stiff.T) * (0.5 / cell_count)
    inverse = eliminate_spd(stiff, size, 32)
    for copy in sent[2]:
        copy.wait_recv()
    mass = mass_total[...] / cell_count
    step_map = dot(mass, inverse, (((1,), (0,)), ((), ())))
    both = jnp.concatenate([step_map, dot(step_map, mass, (((1,), (0,)), ((), ())))], axis=1)
    rows = start_ref[...]
    for turn in range(ITERS):
        pair = dot(rows, both, (((1,), (0,)), ((), ())))
        solved, image = pair[:, :size], pair[:, size:]
        inner = dot(solved, image, (((1,), (1,)), ((), ())))
        inner = 0.5 * (inner + inner.T)
        rows = normalize(inner, solved)
    modes = rows.astype(jnp.bfloat16)

    lines = state.shape[1] // mine

    def piece(index, owner):
        values = lax.dot_general(
            modes, state[index // mine, pl.ds(lax.rem(index, mine) * lines, lines)].reshape(
                lines * state.shape[2], size
            ), (((1,), (1,)), ((), ())), preferred_element_type=jnp.float32,
        )
        return (values * corr_ref[me_nbhd, owner].astype(jnp.float32)).astype(jnp.bfloat16)

    def leave(step, owner, sub):
        return pltpu.make_async_remote_copy(
            src_ref=stage.at[step],
            dst_ref=out_ref.at[me_nbhd],
            send_sem=send_out.at[step],
            recv_sem=recv_out.at[me_nbhd],
            device_id=(owner, sub),
            device_id_type=MESH,
        )

    leaving = []
    for step in range(owners):
        index = lax.rem(step + me_nbhd, owners)
        level = index // mine
        owner = across * lax.rem(level, own) + mine * half + lax.rem(index, mine)
        sub = tower + level // own
        here = jnp.logical_and(owner == me_nbhd, sub == me_sub)
        stage[step] = piece(index, owner)

        @pl.when(jnp.logical_not(here))
        def _():
            leave(step, owner, sub).start()

        @pl.when(here)
        def _():
            out_ref[me_nbhd] = stage[step]

        leaving.append((step, owner, sub, here))
    for nbhd in range(owners):
        @pl.when(jnp.logical_not(is_me(nbhd)))
        def _():
            pltpu.make_async_remote_copy(
                src_ref=stage.at[0], dst_ref=out_ref.at[nbhd], send_sem=send_out.at[0],
                recv_sem=recv_out.at[nbhd], device_id=(nbhd, me_sub), device_id_type=MESH,
            ).wait_recv()
    for step, owner, sub, here in leaving:
        @pl.when(jnp.logical_not(here))
        def _():
            leave(step, owner, sub).wait_send()
    for copies in sent:
        for copy in copies:
            copy.wait_send()
    drain()


def on_device(snap_init, channel_map, yface_vals, zface_vals, face_of, start_block, correlation):
    own, rows_all, depth, width = snap_init.shape[1:]
    modes = start_block.shape[2]
    members, owners = lax.axis_size("sub"), lax.axis_size("nbhd")
    both, rows = 2 * own, rows_all // 2
    cells = own * rows_all * depth
    chunk = width // members
    vmem = pl.BlockSpec(memory_space=pltpu.VMEM)
    f32, bf16 = jnp.float32, jnp.bfloat16
    dma = pltpu.SemaphoreType.DMA
    result = pl.pallas_call(
        functools.partial(
            whole_kernel, members=members, owners=owners, own=own, cell_count=float(cells * members)
        ),
        out_shape=jax.ShapeDtypeStruct((owners, modes, cells // owners), bf16),
        in_specs=[pl.BlockSpec(memory_space=pl.ANY)] + [vmem] * 5
        + [pl.BlockSpec(memory_space=pltpu.SMEM)],
        out_specs=vmem,
        scratch_shapes=[
            pltpu.VMEM((2, both + 2, rows + 2, depth + 16, width), f32),
            pltpu.VMEM((8, both, rows, depth, width), f32),
            pltpu.VMEM((8, both, rows_all, depth), f32),
            pltpu.VMEM((4 * rows, rows * width), bf16),
            pltpu.VMEM((both + 2, rows_all, depth), f32),
            pltpu.VMEM((2, rows_all, width), f32),
            pltpu.VMEM((SWEEPS - 1, both, rows, depth, width), bf16),
            pltpu.VMEM((own, rows + 1, depth, width), bf16),
            pltpu.VMEM((SWEEPS + 1, 2, rows, depth, width), bf16),
            pltpu.VMEM((SWEEPS, both, depth, width), bf16),
            pltpu.VMEM((max(both, rows), depth, 2 * width), bf16),
            pltpu.VMEM((own, rows_all, depth), jnp.int32),
            pltpu.VMEM((rows_all, depth), jnp.int32),
            pltpu.VMEM((rows_all, depth), jnp.int32),
            pltpu.VMEM((own, rows_all, depth, width), bf16),
            dma,
            dma((own,)),
            dma((own,)),
            dma((SWEEPS + 1, 2, 2)),
            dma((SWEEPS + 1, 2, 2)),
            dma((SWEEPS, 4)),
            dma((SWEEPS, 4)),
            dma((3,)),
            dma((3,)),
            pltpu.VMEM((both, rows, depth, width), bf16),
            pltpu.VMEM((width, width), f32),
            pltpu.VMEM((width, width), f32),
            pltpu.VMEM((2, members, chunk, width), f32),
            pltpu.VMEM((2, chunk, width), f32),
            pltpu.VMEM((width, width), f32),
            pltpu.VMEM((width, width), f32),
            pltpu.VMEM((owners, modes, cells // owners), bf16),
            dma((2, 4, members)),
            dma((owners,)),
            dma((owners,)),
        ],
        compiler_params=pltpu.CompilerParams(
            collective_id=0, has_side_effects=True, vmem_limit_bytes=60 << 20
        ),
    )(
        snap_init[0], channel_map[0], yface_vals[0], zface_vals[0], face_of, start_block[0].T,
        correlation,
    )
    return result[None, None]


def solution(mesh):
    return jax.shard_map(
        on_device,
        mesh=mesh,
        in_specs=(
            P("nbhd", "sub", None, None, None),
            P("nbhd", "sub", None, None),
            P("nbhd", None, None),
            P("nbhd", None, None),
            P("nbhd", None),
            P("nbhd", None, None),
            P(),
        ),
        out_specs=P("nbhd", "sub", None, None, None),
        check_vma=False,
    )
```

```python
import functools

import jax
import jax.numpy as jnp
from jax import lax
from jax.experimental import pallas as pl
from jax.experimental.pallas import tpu as pltpu
from jax.sharding import PartitionSpec as P

MESH = pl.DeviceIdType.MESH

SWEEPS = 3
ITERS = 4


def harmonic(left_k, right_k):
    return 2.0 * left_k * right_k / (left_k + right_k)


def relax_part(
    snap_ref, class_ref, yface_ref, zface_ref, face_ref, state_ref, mass_ref, stiff_ref,
    field, coef, compact, select, kappa, ghost_z, early, swap, zland, yland, rhs,
    class_pair, class_low, class_high, slab, slab_sem,
    swap_send, swap_recv, z_send, z_recv, y_send, y_recv, class_send, class_recv,
    members, mass_ready,
):
    me_nbhd = lax.axis_index("nbhd")
    me = lax.axis_index("sub")
    half = lax.rem(me, 2)
    tower = me // 2
    towers = members // 2
    own, rows_all, depth, width = snap_ref.shape
    both = 2 * own
    rows = rows_all // 2
    top = both + 1
    base = 8
    inner = pl.ds(base, depth)

    def at(sub):
        return (me_nbhd, lax.rem(sub + members, members))

    partner = at(me + 1 - 2 * half)
    cross = at(me - 1 + 2 * half)
    lower = at(me - 2)
    upper = at(me + 2)

    def remote(src, dst, send, recv, device):
        return pltpu.make_async_remote_copy(
            src_ref=src, dst_ref=dst, send_sem=send, recv_sem=recv,
            device_id=device, device_id_type=MESH,
        )

    class_copies = [
        remote(class_ref, class_pair, class_send.at[0], class_recv.at[0], partner),
    ]
    class_copies[0].start()
    class_other = []

    def class_sends(plane, land, slot, devices):
        made = []
        for place, device in enumerate(devices):
            made.append(remote(
                class_ref.at[plane], land, class_send.at[1 + place], class_recv.at[slot], device
            ))
        return made

    @pl.when(half == 0)
    def _():
        for copy in class_sends(0, class_high, 2, (lower, cross)):
            copy.start()

    @pl.when(half == 1)
    def _():
        for copy in class_sends(own - 1, class_low, 1, (upper, cross)):
            copy.start()

    order = [0, 1] + list(range(own - 1, 1, -1))
    swaps = []
    for turn, q in enumerate(order):
        plane = q + half * (own - 1 - 2 * q)
        copy = remote(
            snap_ref.at[plane, pl.ds((rows - 1) * (1 - half), rows + 1)],
            swap.at[turn], swap_send.at[turn], swap_recv.at[turn], partner,
        )
        copy.start()
        swaps.append(copy)

    @pl.when(half == 0)
    def _():
        remote(
            snap_ref.at[0, pl.ds(0, rows)], zland.at[0, 1], z_send.at[0, 0, 0],
            z_recv.at[0, 1, 0], lower
        ).start()

    @pl.when(half == 1)
    def _():
        remote(
            snap_ref.at[own - 1, pl.ds(rows, rows)], zland.at[0, 0], z_send.at[0, 1, 0],
            z_recv.at[0, 0, 0], upper
        ).start()

    shift = 1 - half

    def fill_own(p, _):
        def fill(r, _):
            field[0, 1 + own * half + p, shift + r, inner, :] = slab[
                p, (rows - 1) * half + r
            ].astype(jnp.float32)
            return 0
        return lax.fori_loop(0, rows + 1, fill, 0)

    pltpu.make_async_copy(snap_ref, slab, slab_sem).wait()
    lax.fori_loop(0, own, fill_own, 0)

    face = face_ref[...]

    def pick(side):
        return jnp.where(face == side, 1.0, 0.0)

    side_y = jnp.where(half == 0, pick(0), pick(1))
    ghost_y = yface_ref[...].astype(jnp.float32) * side_y
    zface = zface_ref[...].astype(jnp.float32)
    ghost_z[0] = zface * pick(2)
    ghost_z[1] = zface * pick(3)

    def set_ghosts(p, _):
        for buf in range(2):
            field[buf, p + 1, (rows + 1) * half, inner, :] = ghost_y

            def one(y, _):
                field[buf, p + 1, y + 1, pl.ds(base - 1, 1), :] = ghost_z[0, pl.ds(rows * half + y, 1), :]
                field[buf, p + 1, y + 1, pl.ds(base + depth, 1), :] = ghost_z[1, pl.ds(rows * half + y, 1), :]
                return 0

            lax.fori_loop(0, rows, one, 0)
        return 0

    lax.fori_loop(0, both, set_ghosts, 0)

    def to_kappa(classes):
        return jnp.left_shift(1, 2 * classes).astype(jnp.float32)

    def land(slot, ref):
        remote(ref, ref, class_send.at[0], class_recv.at[slot], partner).wait_recv()

    land(0, class_pair)
    land(1, class_low)
    land(2, class_high)
    kappa[0] = to_kappa(class_low[...])
    kappa[top] = to_kappa(class_high[...])
    for p in range(own):
        kappa[1 + own * half + p] = to_kappa(class_ref[p])
        kappa[1 + own * (1 - half) + p] = to_kappa(class_pair[p])

    def coefficients(p, _):
        centre = kappa[p + 1]
        has_low = jnp.logical_or(tower > 0, p > 0)
        has_high = jnp.logical_or(tower < towers - 1, p < both - 1)
        face_low = harmonic(centre, kappa[p])
        face_high = harmonic(centre, kappa[p + 2])
        x_lower = jnp.where(has_low, face_low, centre)
        x_upper = jnp.where(has_high, face_high, centre)
        y_inner = harmonic(centre[1:], centre[:-1])
        y_lower = jnp.concatenate([centre[:1], y_inner], axis=0)
        y_upper = jnp.concatenate([y_inner, centre[-1:]], axis=0)
        z_inner = harmonic(centre[:, 1:], centre[:, :-1])
        z_lower = jnp.concatenate([centre[:, :1], z_inner], axis=1)
        z_upper = jnp.concatenate([z_inner, centre[:, -1:]], axis=1)
        denom = x_lower + x_upper + y_lower + y_upper + z_lower + z_upper
        inverse = 1.0 / denom
        compact[0, p] = jnp.where(has_low, face_low, 0.0) * inverse
        compact[1, p] = jnp.where(has_high, face_high, 0.0) * inverse
        compact[2, p] = y_lower * inverse
        compact[3, p] = y_upper * inverse
        compact[4, p] = z_lower * inverse
        compact[5, p] = z_upper * inverse
        compact[6, p] = denom
        compact[7, p] = centre * (1.0 / 16.0)
        return 0

    lax.fori_loop(0, both, coefficients, 0)
    taken = lax.broadcasted_iota(jnp.int32, select.shape, 0)
    given = lax.broadcasted_iota(jnp.int32, select.shape, 1)
    select[...] = jnp.where(lax.rem(taken, rows) == given // width, 1.0, 0.0).astype(jnp.bfloat16)

    def widen(kinds):
        def one(p, _):
            for kind in kinds:
                exact = compact[kind, p, pl.ds(pl.multiple_of(rows * half, rows), rows), :]
                terms = []
                for _ in range(3):
                    term = exact.astype(jnp.bfloat16).astype(jnp.float32)
                    terms.append(term)
                    exact = exact - term
                terms.append(jnp.zeros_like(exact))
                wide = lax.dot_general(
                    jnp.concatenate(terms, axis=0).astype(jnp.bfloat16), select[...],
                    (((0,), (0,)), ((), ())), preferred_element_type=jnp.float32,
                )
                for y in range(rows):
                    coef[kind, p, y] = wide[:, width * y:width * (y + 1)]
            return 0
        lax.fori_loop(0, both, one, 0)

    widen(range(6))

    def row(sweep, p, y):
        src, dst = (sweep + 1) % 2, sweep % 2
        c = [coef.at[kind, p - 1, y - 1] for kind in range(6)]
        value = c[0][...] * field[src, p - 1, y, inner, :]
        value += c[1][...] * field[src, p + 1, y, inner, :]
        value += c[2][...] * field[src, p, y - 1, inner, :]
        value += c[3][...] * field[src, p, y + 1, inner, :]
        value += c[4][...] * field[src, p, y, pl.ds(base - 1, depth), :]
        value += c[5][...] * field[src, p, y, pl.ds(base + 1, depth), :]
        low = value.astype(jnp.bfloat16)
        field[dst, p, y, inner, :] = low.astype(jnp.float32)
        if sweep < SWEEPS:
            early[sweep - 1, p - 1, y - 1] = low
        else:
            state_ref[p - 1, y - 1] = low
            field[dst, p, y, pl.ds(base + depth, 1), :] = jnp.zeros((1, width), jnp.float32)

    def line(sweep, p, first, count):
        def body(i, _):
            row(sweep, p, first + i)
            return 0
        lax.fori_loop(0, count, body, 0)

    chunk = rows // 2
    edge = rows - (rows - 1) * half

    def chunk_at(part):
        return chunk * half if part == 0 else chunk - chunk * half

    def held(sweep):
        return early.at[sweep - 1] if sweep < SWEEPS else state_ref

    def send_z(sweep, side, part):
        cells = pl.ds(chunk_at(part), chunk)
        remote(
            held(sweep).at[side * (both - 1), cells], zland.at[sweep, 1 - side, cells],
            z_send.at[sweep, side, part], z_recv.at[sweep, 1 - side, part], at(me - 2 + 4 * side),
        ).start()

    def send_y(sweep, part, first, count):
        planes = pl.ds(first, count)
        remote(
            held(sweep).at[planes, edge - 1], yland.at[sweep - 1, planes], y_send.at[sweep - 1, part],
            y_recv.at[sweep - 1, part], partner,
        ).start()

    def take_z(buf, sweep, side, part):
        cells = pl.ds(0, rows if sweep == 0 else chunk)
        remote(
            zland.at[sweep, side, cells], zland.at[sweep, side, cells], z_send.at[sweep, side, part],
            z_recv.at[sweep, side, part], lower,
        ).wait_recv()
        first = 0 if sweep == 0 else chunk_at(part)

        def fill(i, _):
            field[buf, top * side, first + i + 1, inner, :] = zland[sweep, side, first + i].astype(
                jnp.float32
            )
            return 0
        lax.fori_loop(0, rows if sweep == 0 else chunk, fill, 0)

    y_parts = ((1, own - 1), (own, own - 1), (0, 1), (both - 1, 1))

    def take_y(buf, sweep, part):
        first, count = y_parts[part]
        planes = pl.ds(first, count)
        remote(
            yland.at[sweep - 1, planes], yland.at[sweep - 1, planes], y_send.at[sweep - 1, part],
            y_recv.at[sweep - 1, part], partner,
        ).wait_recv()

        def fill(i, _):
            p = first + i
            field[buf, p + 1, (rows + 1) * (1 - half), inner, :] = yland[sweep - 1, p].astype(jnp.float32)
            return 0
        lax.fori_loop(0, count, fill, 0)

    def plane_of(e):
        return e + (1 - half) * (top - 2 * e)

    for e in range(own + 2, both):
        line(1, plane_of(e), 1, rows)
    for turn, q in enumerate(order):
        swaps[turn].wait_recv()
        plane = q + (1 - half) * (own - 1 - 2 * q)
        if turn == 0:
            @pl.when(half == 0)
            def _():
                remote(
                    swap.at[0, pl.ds(0, rows)], zland.at[0, 0], z_send.at[0, 1, 0], z_recv.at[0, 0, 0],
                    upper,
                ).start()

            @pl.when(half == 1)
            def _():
                remote(
                    swap.at[0, pl.ds(1, rows)], zland.at[0, 1], z_send.at[0, 0, 0], z_recv.at[0, 1, 0],
                    lower,
                ).start()

        def fill(r, _):
            field[0, 1 + own * (1 - half) + plane, shift + r, inner, :] = swap[turn, r].astype(
                jnp.float32
            )
            return 0

        lax.fori_loop(0, rows + 1, fill, 0)
        if turn == 1:
            take_z(0, 0, 0, 0)
            take_z(0, 0, 1, 0)
            for e, side in ((both, half), (1, 1 - half)):
                line(1, plane_of(e), 1, rows)
                send_z(1, side, 0)
                send_z(1, side, 1)
                send_y(1, 2 + side, side * (both - 1), 1)
            widen((6, 7))
        if turn >= 2:
            line(1, plane_of(q + 2), 1, rows)
        if q == own - 1:
            send_y(1, half, 1 + (own - 1) * half, own - 1)
    line(1, plane_of(3), 1, rows)
    line(1, plane_of(2), 1, rows)
    send_y(1, 1 - half, 1 + (own - 1) * (1 - half), own - 1)

    def only_if_last(sweep, action):
        if sweep < SWEEPS:
            action()
        else:
            pl.when(half == 1)(action)

    for sweep in range(2, SWEEPS + 1):
        src = (sweep + 1) % 2
        sides = (0, 1) if sweep < SWEEPS else (0,)

        def middle(i, _):
            line(sweep, i + 2, 1 + half, rows - 1)
            return 0
        lax.fori_loop(0, both - 2, middle, 0)

        def border(part):
            take_y(src, sweep - 1, part)
            first, count = y_parts[part]

            def body(i, _):
                row(sweep, first + i + 1, edge)
                return 0
            lax.fori_loop(0, count, body, 0)
            only_if_last(sweep, lambda: send_y(sweep, part, first, count))

        border(0)
        for side in (0, 1):
            take_z(src, sweep - 1, side, 0)
            line(sweep, 1 + side * (both - 1), 1 + chunk_at(0), chunk)
            if side in sides:
                send_z(sweep, side, 0)
        border(1)
        for side in (0, 1):
            take_y(src, sweep - 1, 2 + side)
            take_z(src, sweep - 1, side, 1)
            line(sweep, 1 + side * (both - 1), 1 + chunk_at(1), chunk)
            if side in sides:
                send_z(sweep, side, 1)

            def last_part():
                send_y(sweep, 2 + side, *y_parts[2 + side])
            only_if_last(sweep, last_part)

    last = SWEEPS % 2

    def stiff_row(p, y, place):
        here = field[last, p, y, inner, :]
        ahead = coef[1, p - 1, y - 1] * field[last, p + 1, y, inner, :]
        ahead += coef[3, p - 1, y - 1] * field[last, p, y + 1, inner, :]
        ahead += coef[5, p - 1, y - 1] * field[last, p, y, pl.ds(base + 1, depth), :]
        value = coef[6, p - 1, y - 1] * (here - 2.0 * ahead)
        high = value.astype(jnp.bfloat16)
        rest = (value - high.astype(jnp.float32)).astype(jnp.bfloat16)
        rhs[place, :, pl.ds(0, width)] = high
        rhs[place, :, pl.ds(width, width)] = rest

    def gram(left, count, used):
        right = rhs[pl.ds(0, count), :, pl.ds(0, used)].reshape(count * depth, used)
        return lax.dot_general(
            left.reshape(count * depth, width), right, (((0,), (0,)), ((), ())),
            preferred_element_type=jnp.float32,
        )

    def add_stiff(left, count):
        terms = gram(left, count, 2 * width)
        stiff_ref[...] += terms[:, :width] + terms[:, width:]

    mass_ref[...] = jnp.zeros_like(mass_ref)
    stiff_ref[...] = jnp.zeros_like(stiff_ref)

    def weigh(p, _):
        def body(y, _):
            here = state_ref[p, y].astype(jnp.float32)
            rhs[y, :, pl.ds(0, width)] = (here * coef[7, p, y]).astype(jnp.bfloat16)
            return 0
        lax.fori_loop(0, rows, body, 0)
        mass_ref[...] += gram(state_ref[p], rows, width)
        return 0
    lax.fori_loop(0, both, weigh, 0)
    mass_ready()

    def inside(i, _):
        def body(y, _):
            stiff_row(i + 1, y + 1, y)
            return 0
        lax.fori_loop(0, rows - 1, body, 0)
        add_stiff(state_ref[i, pl.ds(0, rows - 1)], rows - 1)
        return 0
    lax.fori_loop(0, both - 1, inside, 0)

    @pl.when(half == 0)
    def _():
        for part in range(4):
            take_y(last, SWEEPS, part)

    @pl.when(half == 1)
    def _():
        def clear(p, _):
            field[last, p + 1, rows + 1, inner, :] = jnp.zeros((depth, width), jnp.float32)
            return 0
        lax.fori_loop(0, both, clear, 0)

    def side(i, _):
        stiff_row(i + 1, rows, i)
        return 0
    lax.fori_loop(0, both - 1, side, 0)
    add_stiff(state_ref[pl.ds(0, both - 1), rows - 1], both - 1)
    take_z(last, SWEEPS, 1, 0)
    take_z(last, SWEEPS, 1, 1)

    def roof(y, _):
        stiff_row(both, y + 1, y)
        return 0
    lax.fori_loop(0, rows, roof, 0)
    add_stiff(state_ref[both - 1], rows)

    def drain():
        class_copies[0].wait_send()
        for place in range(2):
            remote(
                class_ref.at[0], class_low, class_send.at[1 + place], class_recv.at[1], partner
            ).wait_send()
        for copy in swaps:
            copy.wait_send()
        for side in range(2):
            remote(
                snap_ref.at[0, pl.ds(0, rows)], zland.at[0, 0], z_send.at[0, side, 0], z_recv.at[0, 0, 0], lower
            ).wait_send()

        def left_z(sweep, side, part):
            cells = pl.ds(0, chunk)
            remote(
                held(sweep).at[0, cells], zland.at[sweep, 0, cells], z_send.at[sweep, side, part],
                z_recv.at[sweep, 0, part], lower,
            ).wait_send()

        def left_y(sweep, part):
            planes = pl.ds(*y_parts[part])
            remote(
                held(sweep).at[planes, 0], yland.at[sweep - 1, planes], y_send.at[sweep - 1, part],
                y_recv.at[sweep - 1, part], partner,
            ).wait_send()

        for sweep in range(1, SWEEPS + 1):
            for side in range(2 if sweep < SWEEPS else 1):
                for part in range(2):
                    left_z(sweep, side, part)

            def all_y():
                for part in range(4):
                    left_y(sweep, part)
            only_if_last(sweep, all_y)

    return drain


TILE = 8


def spread(tile, col, width):
    return jnp.broadcast_to(tile[:, col:col + 1], (tile.shape[0], width))


def eliminate_spd(full, size, block):
    lanes = lax.broadcasted_iota(jnp.int32, (TILE, size), 1)
    rows = lax.broadcasted_iota(jnp.int32, (TILE, size), 0)
    wide = lax.broadcasted_iota(jnp.int32, (size, size), 1)
    block_lanes = lax.broadcasted_iota(jnp.int32, (block, size), 1)
    count = block // TILE
    for first in range(0, size, block):
        panel = full[first:first + block]
        signed = jnp.where(block_lanes < first, -panel, panel) if first else panel
        tiles = [panel[TILE * u:TILE * (u + 1)] for u in range(count)]
        for t in range(count):
            base = first + TILE * t
            columns = [[spread(tile, base + j, size) for tile in tiles] for j in range(TILE)]
            for i in range(TILE):
                here = rows == i
                at_col = lanes == base + i
                lead = columns[i]
                pivot = 1.0 / lead[t][i:i + 1]
                row = jnp.where(at_col[:1], 1.0, tiles[t][i:i + 1]) * pivot
                for j in range(i + 1, TILE):
                    scaled = columns[j][t][i:i + 1] * pivot
                    columns[j] = [columns[j][u] - lead[u] * scaled for u in range(count)]
                    columns[j][t] = jnp.where(here, scaled, columns[j][t])
                tiles = [jnp.where(at_col, 0.0, tiles[u]) - lead[u] * row for u in range(count)]
                tiles[t] = jnp.where(here, row, tiles[t])
        panel = jnp.concatenate(tiles, axis=0)
        inside = (wide >= first) & (wide < first + block)
        update = lax.dot_general(
            signed, panel, (((0,), (0,)), ((), ())),
            precision=lax.Precision.HIGHEST, preferred_element_type=jnp.float32,
        )
        rest = jnp.where(inside, 0.0, full) - update
        parts = []
        if first:
            parts.append(rest[:first])
        parts.append(panel)
        if first + block < size:
            parts.append(rest[first + block:])
        full = jnp.concatenate(parts, axis=0)
    return full


def normalize(inner, vectors):
    width = vectors.shape[1]
    count = inner.shape[0] // TILE
    rows = lax.broadcasted_iota(jnp.int32, (TILE, width), 0)
    left = [inner[TILE * u:TILE * (u + 1)] for u in range(count)]
    right = [vectors[TILE * u:TILE * (u + 1)] for u in range(count)]
    scales = []
    for t in range(count):
        columns = [
            [spread(left[u], TILE * t + j, width) for u in range(t, count)] for j in range(TILE)
        ]
        scale = jnp.zeros((TILE, width), jnp.float32)
        for i in range(TILE):
            lead = columns[i]
            value = lead[0][i:i + 1]
            pivot = 1.0 / value
            scale = jnp.where(rows == i, value, scale)
            for j in range(i + 1, TILE):
                scaled = columns[j][0][i:i + 1] * pivot
                columns[j] = [column - part * scaled for column, part in zip(columns[j], lead)]
            below = [jnp.where(rows > i, lead[0], 0.0)] + lead[1:]
            mate = right[t][i:i + 1] * pivot
            for u in range(t, count):
                right[u] = right[u] - below[u - t] * mate
            if t + 1 < count:
                ahead = left[t][i:i + 1] * pivot[:, :left[t].shape[1]]
                for u in range(t, count):
                    left[u] = left[u] - below[u - t][:, :left[t].shape[1]] * ahead
        scales.append(scale)
    return jnp.concatenate([tile / jnp.sqrt(scale) for tile, scale in zip(right, scales)], axis=0)


def whole_kernel(
    snap_ref, class_ref, yface_ref, zface_ref, face_ref, start_ref, corr_ref, out_ref,
    field, coef, compact, select, kappa, ghost_z, early, swap, zland, yland, rhs,
    class_pair, class_low, class_high, slab, slab_sem,
    swap_send, swap_recv, z_send, z_recv, y_send, y_recv, class_send, class_recv,
    state, mass_part, stiff_part, slots, summed, mass_total, stiff_total, stage,
    sum_sem, send_out, recv_out,
    *, members, owners, own, cell_count,
):
    me_sub = lax.axis_index("sub")
    me_nbhd = lax.axis_index("nbhd")
    size = mass_part.shape[1]
    chunk = size // members
    half = lax.rem(me_sub, 2)
    tower = me_sub - half
    across = owners // own
    mine = across // 2
    from_half = lax.rem(me_nbhd, across) // mine
    whole = jnp.where(from_half == half, 1, 0)

    pltpu.make_async_copy(snap_ref, slab, slab_sem).start()

    def sub_at(step):
        return lax.rem(me_sub + step, members)

    def is_me(nbhd):
        return jnp.logical_and(nbhd == me_nbhd, from_half == half)

    barrier = pltpu.get_barrier_semaphore()
    for step in range(1, members):
        pl.semaphore_signal(barrier, inc=1, device_id=(me_nbhd, sub_at(step)), device_id_type=MESH)
    for nbhd in range(owners):
        @pl.when(jnp.logical_not(is_me(nbhd)))
        def _():
            pl.semaphore_signal(
                barrier, inc=1, device_id=(nbhd, tower + from_half), device_id_type=MESH
            )
    pl.semaphore_wait(barrier, members - 1 + owners - whole)

    def rows_of(sub):
        return pl.ds(pl.multiple_of(sub * chunk, chunk), chunk)

    def scatter(which, partial_ref):
        copies = []
        for step in range(1, members):
            peer = sub_at(step)
            copy = pltpu.make_async_remote_copy(
                src_ref=partial_ref.at[rows_of(peer)],
                dst_ref=slots.at[which, step],
                send_sem=sum_sem.at[which, 0, step],
                recv_sem=sum_sem.at[which, 1, step],
                device_id=(me_nbhd, peer),
                device_id_type=MESH,
            )
            copy.start()
            copies.append(copy)
        return copies

    def share(which, partial_ref, total_ref, copies):
        acc = partial_ref[rows_of(me_sub)]
        for step in range(1, members):
            copies[step - 1].wait_recv()
            acc = acc + slots[which, step]
        summed[which] = acc
        total_ref[rows_of(me_sub)] = acc
        spreads = []
        for step in range(1, members):
            copy = pltpu.make_async_remote_copy(
                src_ref=summed.at[which],
                dst_ref=total_ref.at[rows_of(me_sub)],
                send_sem=sum_sem.at[which, 2, step],
                recv_sem=sum_sem.at[which, 3, step],
                device_id=(me_nbhd, sub_at(step)),
                device_id_type=MESH,
            )
            copy.start()
            spreads.append(copy)
        return spreads

    sent = []
    drain = relax_part(
        snap_ref, class_ref, yface_ref, zface_ref, face_ref, state, mass_part, stiff_part,
        field, coef, compact, select, kappa, ghost_z, early, swap, zland, yland, rhs,
        class_pair, class_low, class_high, slab, slab_sem,
        swap_send, swap_recv, z_send, z_recv, y_send, y_recv, class_send, class_recv,
        members, lambda: sent.append(scatter(0, mass_part)),
    )
    sent.append(scatter(1, stiff_part))
    sent.append(share(0, mass_part, mass_total, sent[0]))
    sent.append(share(1, stiff_part, stiff_total, sent[1]))

    dot = functools.partial(
        lax.dot_general, precision=lax.Precision.HIGHEST, preferred_element_type=jnp.float32
    )
    for copy in sent[3]:
        copy.wait_recv()
    stiff = stiff_total[...]
    stiff = (stiff + stiff.T) * (0.5 / cell_count)
    inverse = eliminate_spd(stiff, size, 32)
    for copy in sent[2]:
        copy.wait_recv()
    mass = mass_total[...] / cell_count
    step_map = dot(mass, inverse, (((1,), (0,)), ((), ())))
    both = jnp.concatenate([step_map, dot(step_map, mass, (((1,), (0,)), ((), ())))], axis=1)
    rows = start_ref[...]
    for turn in range(ITERS):
        pair = dot(rows, both, (((1,), (0,)), ((), ())))
        solved, image = pair[:, :size], pair[:, size:]
        inner = dot(solved, image, (((1,), (1,)), ((), ())))
        inner = 0.5 * (inner + inner.T)
        rows = normalize(inner, solved)
    modes = rows.astype(jnp.bfloat16)

    lines = state.shape[1] // mine

    def piece(index, owner):
        values = lax.dot_general(
            modes, state[index // mine, pl.ds(lax.rem(index, mine) * lines, lines)].reshape(
                lines * state.shape[2], size
            ), (((1,), (1,)), ((), ())), preferred_element_type=jnp.float32,
        )
        return (values * corr_ref[me_nbhd, owner].astype(jnp.float32)).astype(jnp.bfloat16)

    def leave(step, owner, sub):
        return pltpu.make_async_remote_copy(
            src_ref=stage.at[step],
            dst_ref=out_ref.at[me_nbhd],
            send_sem=send_out.at[step],
            recv_sem=recv_out.at[me_nbhd],
            device_id=(owner, sub),
            device_id_type=MESH,
        )

    leaving = []
    for step in range(owners):
        index = lax.rem(step + me_nbhd, owners)
        level = index // mine
        owner = across * lax.rem(level, own) + mine * half + lax.rem(index, mine)
        sub = tower + level // own
        here = jnp.logical_and(owner == me_nbhd, sub == me_sub)
        stage[step] = piece(index, owner)

        @pl.when(jnp.logical_not(here))
        def _():
            leave(step, owner, sub).start()

        @pl.when(here)
        def _():
            out_ref[me_nbhd] = stage[step]

        leaving.append((step, owner, sub, here))
    for nbhd in range(owners):
        @pl.when(jnp.logical_not(is_me(nbhd)))
        def _():
            pltpu.make_async_remote_copy(
                src_ref=stage.at[0], dst_ref=out_ref.at[nbhd], send_sem=send_out.at[0],
                recv_sem=recv_out.at[nbhd], device_id=(nbhd, me_sub), device_id_type=MESH,
            ).wait_recv()
    for step, owner, sub, here in leaving:
        @pl.when(jnp.logical_not(here))
        def _():
            leave(step, owner, sub).wait_send()
    for copies in sent:
        for copy in copies:
            copy.wait_send()
    drain()


def on_device(snap_init, channel_map, yface_vals, zface_vals, face_of, start_block, correlation):
    own, rows_all, depth, width = snap_init.shape[1:]
    modes = start_block.shape[2]
    members, owners = lax.axis_size("sub"), lax.axis_size("nbhd")
    both, rows = 2 * own, rows_all // 2
    cells = own * rows_all * depth
    chunk = width // members
    vmem = pl.BlockSpec(memory_space=pltpu.VMEM)
    f32, bf16 = jnp.float32, jnp.bfloat16
    dma = pltpu.SemaphoreType.DMA
    result = pl.pallas_call(
        functools.partial(
            whole_kernel, members=members, owners=owners, own=own, cell_count=float(cells * members)
        ),
        out_shape=jax.ShapeDtypeStruct((owners, modes, cells // owners), bf16),
        in_specs=[pl.BlockSpec(memory_space=pl.ANY)] + [vmem] * 5
        + [pl.BlockSpec(memory_space=pltpu.SMEM)],
        out_specs=vmem,
        scratch_shapes=[
            pltpu.VMEM((2, both + 2, rows + 2, depth + 16, width), f32),
            pltpu.VMEM((8, both, rows, depth, width), f32),
            pltpu.VMEM((8, both, rows_all, depth), f32),
            pltpu.VMEM((4 * rows, rows * width), bf16),
            pltpu.VMEM((both + 2, rows_all, depth), f32),
            pltpu.VMEM((2, rows_all, width), f32),
            pltpu.VMEM((SWEEPS - 1, both, rows, depth, width), bf16),
            pltpu.VMEM((own, rows + 1, depth, width), bf16),
            pltpu.VMEM((SWEEPS + 1, 2, rows, depth, width), bf16),
            pltpu.VMEM((SWEEPS, both, depth, width), bf16),
            pltpu.VMEM((max(both, rows), depth, 2 * width), bf16),
            pltpu.VMEM((own, rows_all, depth), jnp.int32),
            pltpu.VMEM((rows_all, depth), jnp.int32),
            pltpu.VMEM((rows_all, depth), jnp.int32),
            pltpu.VMEM((own, rows_all, depth, width), bf16),
            dma,
            dma((own,)),
            dma((own,)),
            dma((SWEEPS + 1, 2, 2)),
            dma((SWEEPS + 1, 2, 2)),
            dma((SWEEPS, 4)),
            dma((SWEEPS, 4)),
            dma((3,)),
            dma((3,)),
            pltpu.VMEM((both, rows, depth, width), bf16),
            pltpu.VMEM((width, width), f32),
            pltpu.VMEM((width, width), f32),
            pltpu.VMEM((2, members, chunk, width), f32),
            pltpu.VMEM((2, chunk, width), f32),
            pltpu.VMEM((width, width), f32),
            pltpu.VMEM((width, width), f32),
            pltpu.VMEM((owners, modes, cells // owners), bf16),
            dma((2, 4, members)),
            dma((owners,)),
            dma((owners,)),
        ],
        compiler_params=pltpu.CompilerParams(
            collective_id=0, has_side_effects=True, vmem_limit_bytes=52 << 20
        ),
    )(
        snap_init[0], channel_map[0], yface_vals[0], zface_vals[0], face_of, start_block[0].T,
        correlation,
    )
    return result[None, None]


def solution(mesh):
    return jax.shard_map(
        on_device,
        mesh=mesh,
        in_specs=(
            P("nbhd", "sub", None, None, None),
            P("nbhd", "sub", None, None),
            P("nbhd", None, None),
            P("nbhd", None, None),
            P("nbhd", None),
            P("nbhd", None, None),
            P(),
        ),
        out_specs=P("nbhd", "sub", None, None, None),
        check_vma=False,
    )
```

```python
import functools

import jax
import jax.numpy as jnp
from jax import lax
from jax.experimental import pallas as pl
from jax.experimental.pallas import tpu as pltpu
from jax.sharding import PartitionSpec as P

MESH = pl.DeviceIdType.MESH

SWEEPS = 3
ITERS = 4


def harmonic(left_k, right_k):
    return 2.0 * left_k * right_k / (left_k + right_k)


def relax_part(
    snap_ref, class_ref, yface_ref, zface_ref, face_ref, state_ref, mass_ref, stiff_ref,
    field, coef, compact, select, kappa, ghost_z, early, swap, zland, yland, rhs,
    class_pair, class_low, class_high, slab, slab_sem,
    swap_send, swap_recv, z_send, z_recv, y_send, y_recv, class_send, class_recv,
    members, stiff_ready,
):
    me_nbhd = lax.axis_index("nbhd")
    me = lax.axis_index("sub")
    half = lax.rem(me, 2)
    tower = me // 2
    towers = members // 2
    own, rows_all, depth, width = snap_ref.shape
    both = 2 * own
    rows = rows_all // 2
    top = both + 1
    base = 8
    inner = pl.ds(base, depth)

    def at(sub):
        return (me_nbhd, lax.rem(sub + members, members))

    partner = at(me + 1 - 2 * half)
    cross = at(me - 1 + 2 * half)
    lower = at(me - 2)
    upper = at(me + 2)

    def remote(src, dst, send, recv, device):
        return pltpu.make_async_remote_copy(
            src_ref=src, dst_ref=dst, send_sem=send, recv_sem=recv,
            device_id=device, device_id_type=MESH,
        )

    class_copies = [
        remote(class_ref, class_pair, class_send.at[0], class_recv.at[0], partner),
    ]
    class_copies[0].start()
    class_other = []

    def class_sends(plane, land, slot, devices):
        made = []
        for place, device in enumerate(devices):
            made.append(remote(
                class_ref.at[plane], land, class_send.at[1 + place], class_recv.at[slot], device
            ))
        return made

    @pl.when(half == 0)
    def _():
        for copy in class_sends(0, class_high, 2, (lower, cross)):
            copy.start()

    @pl.when(half == 1)
    def _():
        for copy in class_sends(own - 1, class_low, 1, (upper, cross)):
            copy.start()

    order = [0, 1] + list(range(own - 1, 1, -1))
    swaps = []
    for turn, q in enumerate(order):
        plane = q + half * (own - 1 - 2 * q)
        copy = remote(
            snap_ref.at[plane, pl.ds((rows - 1) * (1 - half), rows + 1)],
            swap.at[turn], swap_send.at[turn], swap_recv.at[turn], partner,
        )
        copy.start()
        swaps.append(copy)

    @pl.when(half == 0)
    def _():
        remote(
            snap_ref.at[0, pl.ds(0, rows)], zland.at[0, 1], z_send.at[0, 0, 0],
            z_recv.at[0, 1, 0], lower
        ).start()

    @pl.when(half == 1)
    def _():
        remote(
            snap_ref.at[own - 1, pl.ds(rows, rows)], zland.at[0, 0], z_send.at[0, 1, 0],
            z_recv.at[0, 0, 0], upper
        ).start()

    shift = 1 - half

    def fill_own(p, _):
        def fill(r, _):
            field[0, 1 + own * half + p, shift + r, inner, :] = slab[
                p, (rows - 1) * half + r
            ].astype(jnp.float32)
            return 0
        return lax.fori_loop(0, rows + 1, fill, 0)

    pltpu.make_async_copy(snap_ref, slab, slab_sem).wait()
    lax.fori_loop(0, own, fill_own, 0)

    face = face_ref[...]

    def pick(side):
        return jnp.where(face == side, 1.0, 0.0)

    side_y = jnp.where(half == 0, pick(0), pick(1))
    ghost_y = yface_ref[...].astype(jnp.float32) * side_y
    zface = zface_ref[...].astype(jnp.float32)
    ghost_z[0] = zface * pick(2)
    ghost_z[1] = zface * pick(3)

    def set_ghosts(p, _):
        for buf in range(2):
            field[buf, p + 1, (rows + 1) * half, inner, :] = ghost_y

            def one(y, _):
                field[buf, p + 1, y + 1, pl.ds(base - 1, 1), :] = ghost_z[0, pl.ds(rows * half + y, 1), :]
                field[buf, p + 1, y + 1, pl.ds(base + depth, 1), :] = ghost_z[1, pl.ds(rows * half + y, 1), :]
                return 0

            lax.fori_loop(0, rows, one, 0)
        return 0

    lax.fori_loop(0, both, set_ghosts, 0)

    def to_kappa(classes):
        return jnp.left_shift(1, 2 * classes).astype(jnp.float32)

    def land(slot, ref):
        remote(ref, ref, class_send.at[0], class_recv.at[slot], partner).wait_recv()

    land(0, class_pair)
    land(1, class_low)
    land(2, class_high)
    kappa[0] = to_kappa(class_low[...])
    kappa[top] = to_kappa(class_high[...])
    for p in range(own):
        kappa[1 + own * half + p] = to_kappa(class_ref[p])
        kappa[1 + own * (1 - half) + p] = to_kappa(class_pair[p])

    def coefficients(p, _):
        centre = kappa[p + 1]
        has_low = jnp.logical_or(tower > 0, p > 0)
        has_high = jnp.logical_or(tower < towers - 1, p < both - 1)
        face_low = harmonic(centre, kappa[p])
        face_high = harmonic(centre, kappa[p + 2])
        x_lower = jnp.where(has_low, face_low, centre)
        x_upper = jnp.where(has_high, face_high, centre)
        y_inner = harmonic(centre[1:], centre[:-1])
        y_lower = jnp.concatenate([centre[:1], y_inner], axis=0)
        y_upper = jnp.concatenate([y_inner, centre[-1:]], axis=0)
        z_inner = harmonic(centre[:, 1:], centre[:, :-1])
        z_lower = jnp.concatenate([centre[:, :1], z_inner], axis=1)
        z_upper = jnp.concatenate([z_inner, centre[:, -1:]], axis=1)
        denom = x_lower + x_upper + y_lower + y_upper + z_lower + z_upper
        inverse = 1.0 / denom
        compact[0, p] = jnp.where(has_low, face_low, 0.0) * inverse
        compact[1, p] = jnp.where(has_high, face_high, 0.0) * inverse
        compact[2, p] = y_lower * inverse
        compact[3, p] = y_upper * inverse
        compact[4, p] = z_lower * inverse
        compact[5, p] = z_upper * inverse
        compact[6, p] = denom
        compact[7, p] = centre * (1.0 / 16.0)
        return 0

    lax.fori_loop(0, both, coefficients, 0)
    taken = lax.broadcasted_iota(jnp.int32, select.shape, 0)
    given = lax.broadcasted_iota(jnp.int32, select.shape, 1)
    select[...] = jnp.where(lax.rem(taken, rows) == given // width, 1.0, 0.0).astype(jnp.bfloat16)

    def widen(kinds):
        def one(p, _):
            for kind in kinds:
                exact = compact[kind, p, pl.ds(pl.multiple_of(rows * half, rows), rows), :]
                terms = []
                for _ in range(3):
                    term = exact.astype(jnp.bfloat16).astype(jnp.float32)
                    terms.append(term)
                    exact = exact - term
                terms.append(jnp.zeros_like(exact))
                wide = lax.dot_general(
                    jnp.concatenate(terms, axis=0).astype(jnp.bfloat16), select[...],
                    (((0,), (0,)), ((), ())), preferred_element_type=jnp.float32,
                )
                for y in range(rows):
                    coef[kind, p, y] = wide[:, width * y:width * (y + 1)]
            return 0
        lax.fori_loop(0, both, one, 0)

    widen(range(3))
    swaps[0].wait_recv()

    @pl.when(half == 0)
    def _():
        remote(
            swap.at[0, pl.ds(0, rows)], zland.at[0, 0], z_send.at[0, 1, 0], z_recv.at[0, 0, 0],
            upper,
        ).start()

    @pl.when(half == 1)
    def _():
        remote(
            swap.at[0, pl.ds(1, rows)], zland.at[0, 1], z_send.at[0, 0, 0], z_recv.at[0, 1, 0],
            lower,
        ).start()

    widen(range(3, 6))

    def row(sweep, p, y):
        src, dst = (sweep + 1) % 2, sweep % 2
        c = [coef.at[kind, p - 1, y - 1] for kind in range(6)]
        value = c[0][...] * field[src, p - 1, y, inner, :]
        value += c[1][...] * field[src, p + 1, y, inner, :]
        value += c[2][...] * field[src, p, y - 1, inner, :]
        value += c[3][...] * field[src, p, y + 1, inner, :]
        value += c[4][...] * field[src, p, y, pl.ds(base - 1, depth), :]
        value += c[5][...] * field[src, p, y, pl.ds(base + 1, depth), :]
        low = value.astype(jnp.bfloat16)
        field[dst, p, y, inner, :] = low.astype(jnp.float32)
        if sweep < SWEEPS:
            early[sweep - 1, p - 1, y - 1] = low
        else:
            state_ref[p - 1, y - 1] = low
            field[dst, p, y, pl.ds(base + depth, 1), :] = jnp.zeros((1, width), jnp.float32)

    def line(sweep, p, first, count):
        def body(i, _):
            row(sweep, p, first + i)
            return 0
        lax.fori_loop(0, count, body, 0)

    chunk = rows // 2
    edge = rows - (rows - 1) * half

    def chunk_at(part):
        return chunk * half if part == 0 else chunk - chunk * half

    def held(sweep):
        return early.at[sweep - 1] if sweep < SWEEPS else state_ref

    def send_z(sweep, side, part):
        cells = pl.ds(chunk_at(part), chunk)
        remote(
            held(sweep).at[side * (both - 1), cells], zland.at[sweep, 1 - side, cells],
            z_send.at[sweep, side, part], z_recv.at[sweep, 1 - side, part], at(me - 2 + 4 * side),
        ).start()

    def send_y(sweep, part, first, count):
        planes = pl.ds(first, count)
        remote(
            held(sweep).at[planes, edge - 1], yland.at[sweep - 1, planes], y_send.at[sweep - 1, part],
            y_recv.at[sweep - 1, part], partner,
        ).start()

    def take_z(buf, sweep, side, part):
        cells = pl.ds(0, rows if sweep == 0 else chunk)
        remote(
            zland.at[sweep, side, cells], zland.at[sweep, side, cells], z_send.at[sweep, side, part],
            z_recv.at[sweep, side, part], lower,
        ).wait_recv()
        first = 0 if sweep == 0 else chunk_at(part)

        def fill(i, _):
            field[buf, top * side, first + i + 1, inner, :] = zland[sweep, side, first + i].astype(
                jnp.float32
            )
            return 0
        lax.fori_loop(0, rows if sweep == 0 else chunk, fill, 0)

    y_parts = ((1, own - 1), (own, own - 1), (0, 1), (both - 1, 1))

    def take_y(buf, sweep, part):
        first, count = y_parts[part]
        planes = pl.ds(first, count)
        remote(
            yland.at[sweep - 1, planes], yland.at[sweep - 1, planes], y_send.at[sweep - 1, part],
            y_recv.at[sweep - 1, part], partner,
        ).wait_recv()

        def fill(i, _):
            p = first + i
            field[buf, p + 1, (rows + 1) * (1 - half), inner, :] = yland[sweep - 1, p].astype(jnp.float32)
            return 0
        lax.fori_loop(0, count, fill, 0)

    def plane_of(e):
        return e + (1 - half) * (top - 2 * e)

    ahead = range(own + 2, both)
    for e in ahead:
        line(1, plane_of(e), 1, rows)
    for turn, q in enumerate(order):
        if turn:
            swaps[turn].wait_recv()
        plane = q + (1 - half) * (own - 1 - 2 * q)
        def fill(r, _):
            field[0, 1 + own * (1 - half) + plane, shift + r, inner, :] = swap[turn, r].astype(
                jnp.float32
            )
            return 0

        lax.fori_loop(0, rows + 1, fill, 0)
        if turn == 1:
            take_z(0, 0, 0, 0)
            take_z(0, 0, 1, 0)
            for e, side in ((both, half), (1, 1 - half)):
                line(1, plane_of(e), 1, rows)
                send_z(1, side, 0)
                send_z(1, side, 1)
                send_y(1, 2 + side, side * (both - 1), 1)
        if turn >= 2:
            line(1, plane_of(q + 2), 1, rows)
        if q == own - 1:
            send_y(1, half, 1 + (own - 1) * half, own - 1)
            widen((6, 7))
            for e in ahead:
                line(2, plane_of(e), 1 + half, rows - 1)
    line(1, plane_of(3), 1, rows)
    line(1, plane_of(2), 1, rows)
    send_y(1, 1 - half, 1 + (own - 1) * (1 - half), own - 1)

    def only_if_last(sweep, action):
        if sweep < SWEEPS:
            action()
        else:
            pl.when(half == 1)(action)

    for sweep in range(2, SWEEPS + 1):
        src = (sweep + 1) % 2
        sides = (0, 1) if sweep < SWEEPS else (0,)

        def middle(i, _):
            line(sweep, plane_of(i + 2), 1 + half, rows - 1)
            return 0
        lax.fori_loop(0, both - 2 - (len(ahead) if sweep == 2 else 0), middle, 0)
        for side in (0, 1):
            take_z(src, sweep - 1, side, 0)
            line(sweep, 1 + side * (both - 1), 1 + chunk_at(0), chunk)
            if side in sides:
                send_z(sweep, side, 0)
        take_y(src, sweep - 1, 0)
        take_y(src, sweep - 1, 1)

        def border(i, _):
            row(sweep, i + 2, edge)
            return 0
        lax.fori_loop(0, both - 2, border, 0)

        def first_parts():
            send_y(sweep, 0, *y_parts[0])
            send_y(sweep, 1, *y_parts[1])
        only_if_last(sweep, first_parts)
        for side in (0, 1):
            take_y(src, sweep - 1, 2 + side)
            take_z(src, sweep - 1, side, 1)
            line(sweep, 1 + side * (both - 1), 1 + chunk_at(1), chunk)
            if side in sides:
                send_z(sweep, side, 1)

            def last_part():
                send_y(sweep, 2 + side, *y_parts[2 + side])
            only_if_last(sweep, last_part)

    last = SWEEPS % 2

    def stiff_row(p, y, place):
        here = field[last, p, y, inner, :]
        ahead = coef[1, p - 1, y - 1] * field[last, p + 1, y, inner, :]
        ahead += coef[3, p - 1, y - 1] * field[last, p, y + 1, inner, :]
        ahead += coef[5, p - 1, y - 1] * field[last, p, y, pl.ds(base + 1, depth), :]
        value = coef[6, p - 1, y - 1] * (here - 2.0 * ahead)
        high = value.astype(jnp.bfloat16)
        rest = (value - high.astype(jnp.float32)).astype(jnp.bfloat16)
        rhs[place, :, pl.ds(0, width)] = high
        rhs[place, :, pl.ds(width, width)] = rest

    def gram(left, count, used):
        right = rhs[pl.ds(0, count), :, pl.ds(0, used)].reshape(count * depth, used)
        return lax.dot_general(
            left.reshape(count * depth, width), right, (((0,), (0,)), ((), ())),
            preferred_element_type=jnp.float32,
        )

    def add_stiff(left, count):
        terms = gram(left, count, 2 * width)
        stiff_ref[...] += terms[:, :width] + terms[:, width:]

    mass_ref[...] = jnp.zeros_like(mass_ref)
    stiff_ref[...] = jnp.zeros_like(stiff_ref)

    def weigh(p, _):
        def body(y, _):
            here = state_ref[p, y].astype(jnp.float32)
            rhs[y, :, pl.ds(0, width)] = (here * coef[7, p, y]).astype(jnp.bfloat16)
            return 0
        lax.fori_loop(0, rows, body, 0)
        mass_ref[...] += gram(state_ref[p], rows, width)
        return 0
    def inside(i, _):
        def body(y, _):
            stiff_row(i + 1, y + 1, y)
            return 0
        lax.fori_loop(0, rows - 1, body, 0)
        add_stiff(state_ref[i, pl.ds(0, rows - 1)], rows - 1)
        return 0
    lax.fori_loop(0, both - 1, inside, 0)
    lax.fori_loop(0, own - 1, weigh, 0)

    @pl.when(half == 0)
    def _():
        for part in range(4):
            take_y(last, SWEEPS, part)

    @pl.when(half == 1)
    def _():
        def clear(p, _):
            field[last, p + 1, rows + 1, inner, :] = jnp.zeros((depth, width), jnp.float32)
            return 0
        lax.fori_loop(0, both, clear, 0)

    def side(i, _):
        stiff_row(i + 1, rows, i)
        return 0
    lax.fori_loop(0, both - 1, side, 0)
    add_stiff(state_ref[pl.ds(0, both - 1), rows - 1], both - 1)
    take_z(last, SWEEPS, 1, 0)
    take_z(last, SWEEPS, 1, 1)

    def roof(y, _):
        stiff_row(both, y + 1, y)
        return 0
    lax.fori_loop(0, rows, roof, 0)
    add_stiff(state_ref[both - 1], rows)
    stiff_ready()
    lax.fori_loop(own - 1, both, weigh, 0)

    def drain():
        class_copies[0].wait_send()
        for place in range(2):
            remote(
                class_ref.at[0], class_low, class_send.at[1 + place], class_recv.at[1], partner
            ).wait_send()
        for copy in swaps:
            copy.wait_send()
        for side in range(2):
            remote(
                snap_ref.at[0, pl.ds(0, rows)], zland.at[0, 0], z_send.at[0, side, 0], z_recv.at[0, 0, 0], lower
            ).wait_send()

        def left_z(sweep, side, part):
            cells = pl.ds(0, chunk)
            remote(
                held(sweep).at[0, cells], zland.at[sweep, 0, cells], z_send.at[sweep, side, part],
                z_recv.at[sweep, 0, part], lower,
            ).wait_send()

        def left_y(sweep, part):
            planes = pl.ds(*y_parts[part])
            remote(
                held(sweep).at[planes, 0], yland.at[sweep - 1, planes], y_send.at[sweep - 1, part],
                y_recv.at[sweep - 1, part], partner,
            ).wait_send()

        for sweep in range(1, SWEEPS + 1):
            for side in range(2 if sweep < SWEEPS else 1):
                for part in range(2):
                    left_z(sweep, side, part)

            def all_y():
                for part in range(4):
                    left_y(sweep, part)
            only_if_last(sweep, all_y)

    return drain


TILE = 8


def spread(tile, col, width):
    return jnp.broadcast_to(tile[:, col:col + 1], (tile.shape[0], width))


def eliminate_spd(full, size, block):
    lanes = lax.broadcasted_iota(jnp.int32, (TILE, size), 1)
    rows = lax.broadcasted_iota(jnp.int32, (TILE, size), 0)
    wide = lax.broadcasted_iota(jnp.int32, (size, size), 1)
    block_lanes = lax.broadcasted_iota(jnp.int32, (block, size), 1)
    count = block // TILE
    for first in range(0, size, block):
        panel = full[first:first + block]
        signed = jnp.where(block_lanes < first, -panel, panel) if first else panel
        tiles = [panel[TILE * u:TILE * (u + 1)] for u in range(count)]
        for t in range(count):
            base = first + TILE * t
            columns = [[spread(tile, base + j, size) for tile in tiles] for j in range(TILE)]
            for i in range(TILE):
                here = rows == i
                at_col = lanes == base + i
                lead = columns[i]
                pivot = 1.0 / lead[t][i:i + 1]
                row = jnp.where(at_col[:1], 1.0, tiles[t][i:i + 1]) * pivot
                for j in range(i + 1, TILE):
                    scaled = columns[j][t][i:i + 1] * pivot
                    columns[j] = [columns[j][u] - lead[u] * scaled for u in range(count)]
                    columns[j][t] = jnp.where(here, scaled, columns[j][t])
                tiles = [jnp.where(at_col, 0.0, tiles[u]) - lead[u] * row for u in range(count)]
                tiles[t] = jnp.where(here, row, tiles[t])
        panel = jnp.concatenate(tiles, axis=0)
        inside = (wide >= first) & (wide < first + block)
        update = lax.dot_general(
            signed, panel, (((0,), (0,)), ((), ())),
            precision=lax.Precision.HIGHEST, preferred_element_type=jnp.float32,
        )
        rest = jnp.where(inside, 0.0, full) - update
        parts = []
        if first:
            parts.append(rest[:first])
        parts.append(panel)
        if first + block < size:
            parts.append(rest[first + block:])
        full = jnp.concatenate(parts, axis=0)
    return full


def normalize(inner, vectors):
    width = vectors.shape[1]
    count = inner.shape[0] // TILE
    rows = lax.broadcasted_iota(jnp.int32, (TILE, width), 0)
    left = [inner[TILE * u:TILE * (u + 1)] for u in range(count)]
    right = [vectors[TILE * u:TILE * (u + 1)] for u in range(count)]
    scales = []
    for t in range(count):
        columns = [
            [spread(left[u], TILE * t + j, width) for u in range(t, count)] for j in range(TILE)
        ]
        scale = jnp.zeros((TILE, width), jnp.float32)
        for i in range(TILE):
            lead = columns[i]
            value = lead[0][i:i + 1]
            pivot = 1.0 / value
            scale = jnp.where(rows == i, value, scale)
            for j in range(i + 1, TILE):
                scaled = columns[j][0][i:i + 1] * pivot
                columns[j] = [column - part * scaled for column, part in zip(columns[j], lead)]
            below = [jnp.where(rows > i, lead[0], 0.0)] + lead[1:]
            mate = right[t][i:i + 1] * pivot
            for u in range(t, count):
                right[u] = right[u] - below[u - t] * mate
            if t + 1 < count:
                ahead = left[t][i:i + 1] * pivot[:, :left[t].shape[1]]
                for u in range(t, count):
                    left[u] = left[u] - below[u - t][:, :left[t].shape[1]] * ahead
        scales.append(scale)
    return jnp.concatenate([tile / jnp.sqrt(scale) for tile, scale in zip(right, scales)], axis=0)


def whole_kernel(
    snap_ref, class_ref, yface_ref, zface_ref, face_ref, start_ref, corr_ref, out_ref,
    field, coef, compact, select, kappa, ghost_z, early, swap, zland, yland, rhs,
    class_pair, class_low, class_high, slab, slab_sem,
    swap_send, swap_recv, z_send, z_recv, y_send, y_recv, class_send, class_recv,
    state, mass_part, stiff_part, slots, summed, mass_total, stiff_total, stage,
    sum_sem, send_out, recv_out,
    *, members, owners, own, cell_count,
):
    me_sub = lax.axis_index("sub")
    me_nbhd = lax.axis_index("nbhd")
    size = mass_part.shape[1]
    chunk = size // members
    half = lax.rem(me_sub, 2)
    tower = me_sub - half
    across = owners // own
    mine = across // 2
    from_half = lax.rem(me_nbhd, across) // mine
    whole = jnp.where(from_half == half, 1, 0)

    pltpu.make_async_copy(snap_ref, slab, slab_sem).start()

    def sub_at(step):
        return lax.rem(me_sub + step, members)

    def is_me(nbhd):
        return jnp.logical_and(nbhd == me_nbhd, from_half == half)

    barrier = pltpu.get_barrier_semaphore()
    for step in range(1, members):
        pl.semaphore_signal(barrier, inc=1, device_id=(me_nbhd, sub_at(step)), device_id_type=MESH)
    for nbhd in range(owners):
        @pl.when(jnp.logical_not(is_me(nbhd)))
        def _():
            pl.semaphore_signal(
                barrier, inc=1, device_id=(nbhd, tower + from_half), device_id_type=MESH
            )
    pl.semaphore_wait(barrier, members - 1 + owners - whole)

    def rows_of(sub):
        return pl.ds(pl.multiple_of(sub * chunk, chunk), chunk)

    def scatter(which, partial_ref):
        copies = []
        for step in range(1, members):
            peer = sub_at(step)
            copy = pltpu.make_async_remote_copy(
                src_ref=partial_ref.at[rows_of(peer)],
                dst_ref=slots.at[which, step],
                send_sem=sum_sem.at[which, 0, step],
                recv_sem=sum_sem.at[which, 1, step],
                device_id=(me_nbhd, peer),
                device_id_type=MESH,
            )
            copy.start()
            copies.append(copy)
        return copies

    def share(which, partial_ref, total_ref, copies):
        acc = partial_ref[rows_of(me_sub)]
        for step in range(1, members):
            copies[step - 1].wait_recv()
            acc = acc + slots[which, step]
        summed[which] = acc
        total_ref[rows_of(me_sub)] = acc
        spreads = []
        for step in range(1, members):
            copy = pltpu.make_async_remote_copy(
                src_ref=summed.at[which],
                dst_ref=total_ref.at[rows_of(me_sub)],
                send_sem=sum_sem.at[which, 2, step],
                recv_sem=sum_sem.at[which, 3, step],
                device_id=(me_nbhd, sub_at(step)),
                device_id_type=MESH,
            )
            copy.start()
            spreads.append(copy)
        return spreads

    sent = []
    drain = relax_part(
        snap_ref, class_ref, yface_ref, zface_ref, face_ref, state, mass_part, stiff_part,
        field, coef, compact, select, kappa, ghost_z, early, swap, zland, yland, rhs,
        class_pair, class_low, class_high, slab, slab_sem,
        swap_send, swap_recv, z_send, z_recv, y_send, y_recv, class_send, class_recv,
        members, lambda: sent.append(scatter(1, stiff_part)),
    )
    sent.append(scatter(0, mass_part))
    sent.append(share(1, stiff_part, stiff_total, sent[0]))
    sent.append(share(0, mass_part, mass_total, sent[1]))

    dot = functools.partial(
        lax.dot_general, precision=lax.Precision.HIGHEST, preferred_element_type=jnp.float32
    )
    for copy in sent[2]:
        copy.wait_recv()
    stiff = stiff_total[...]
    stiff = (stiff + stiff.T) * (0.5 / cell_count)
    inverse = eliminate_spd(stiff, size, 32)
    for copy in sent[3]:
        copy.wait_recv()
    mass = mass_total[...] / cell_count
    step_map = dot(mass, inverse, (((1,), (0,)), ((), ())))
    both = jnp.concatenate([step_map, dot(step_map, mass, (((1,), (0,)), ((), ())))], axis=1)
    rows = start_ref[...]
    for turn in range(ITERS):
        pair = dot(rows, both, (((1,), (0,)), ((), ())))
        solved, image = pair[:, :size], pair[:, size:]
        inner = dot(solved, image, (((1,), (1,)), ((), ())))
        inner = 0.5 * (inner + inner.T)
        rows = normalize(inner, solved)
    modes = rows.astype(jnp.bfloat16)

    lines = state.shape[1] // mine

    def piece(index, owner):
        values = lax.dot_general(
            modes, state[index // mine, pl.ds(lax.rem(index, mine) * lines, lines)].reshape(
                lines * state.shape[2], size
            ), (((1,), (1,)), ((), ())), preferred_element_type=jnp.float32,
        )
        return (values * corr_ref[me_nbhd, owner].astype(jnp.float32)).astype(jnp.bfloat16)

    def leave(step, owner, sub):
        return pltpu.make_async_remote_copy(
            src_ref=stage.at[step],
            dst_ref=out_ref.at[me_nbhd],
            send_sem=send_out.at[step],
            recv_sem=recv_out.at[me_nbhd],
            device_id=(owner, sub),
            device_id_type=MESH,
        )

    leaving = []
    for step in range(owners):
        index = lax.rem(step + me_nbhd, owners)
        level = index // mine
        owner = across * lax.rem(level, own) + mine * half + lax.rem(index, mine)
        sub = tower + level // own
        here = jnp.logical_and(owner == me_nbhd, sub == me_sub)
        stage[step] = piece(index, owner)

        @pl.when(jnp.logical_not(here))
        def _():
            leave(step, owner, sub).start()

        @pl.when(here)
        def _():
            out_ref[me_nbhd] = stage[step]

        leaving.append((step, owner, sub, here))
    for nbhd in range(owners):
        @pl.when(jnp.logical_not(is_me(nbhd)))
        def _():
            pltpu.make_async_remote_copy(
                src_ref=stage.at[0], dst_ref=out_ref.at[nbhd], send_sem=send_out.at[0],
                recv_sem=recv_out.at[nbhd], device_id=(nbhd, me_sub), device_id_type=MESH,
            ).wait_recv()
    for step, owner, sub, here in leaving:
        @pl.when(jnp.logical_not(here))
        def _():
            leave(step, owner, sub).wait_send()
    for copies in sent:
        for copy in copies:
            copy.wait_send()
    drain()


def on_device(snap_init, channel_map, yface_vals, zface_vals, face_of, start_block, correlation):
    own, rows_all, depth, width = snap_init.shape[1:]
    modes = start_block.shape[2]
    members, owners = lax.axis_size("sub"), lax.axis_size("nbhd")
    both, rows = 2 * own, rows_all // 2
    cells = own * rows_all * depth
    chunk = width // members
    vmem = pl.BlockSpec(memory_space=pltpu.VMEM)
    f32, bf16 = jnp.float32, jnp.bfloat16
    dma = pltpu.SemaphoreType.DMA
    result = pl.pallas_call(
        functools.partial(
            whole_kernel, members=members, owners=owners, own=own, cell_count=float(cells * members)
        ),
        out_shape=jax.ShapeDtypeStruct((owners, modes, cells // owners), bf16),
        in_specs=[pl.BlockSpec(memory_space=pl.ANY)] + [vmem] * 5
        + [pl.BlockSpec(memory_space=pltpu.SMEM)],
        out_specs=vmem,
        scratch_shapes=[
            pltpu.VMEM((2, both + 2, rows + 2, depth + 16, width), f32),
            pltpu.VMEM((8, both, rows, depth, width), f32),
            pltpu.VMEM((8, both, rows_all, depth), f32),
            pltpu.VMEM((4 * rows, rows * width), bf16),
            pltpu.VMEM((both + 2, rows_all, depth), f32),
            pltpu.VMEM((2, rows_all, width), f32),
            pltpu.VMEM((SWEEPS - 1, both, rows, depth, width), bf16),
            pltpu.VMEM((own, rows + 1, depth, width), bf16),
            pltpu.VMEM((SWEEPS + 1, 2, rows, depth, width), bf16),
            pltpu.VMEM((SWEEPS, both, depth, width), bf16),
            pltpu.VMEM((max(both, rows), depth, 2 * width), bf16),
            pltpu.VMEM((own, rows_all, depth), jnp.int32),
            pltpu.VMEM((rows_all, depth), jnp.int32),
            pltpu.VMEM((rows_all, depth), jnp.int32),
            pltpu.VMEM((own, rows_all, depth, width), bf16),
            dma,
            dma((own,)),
            dma((own,)),
            dma((SWEEPS + 1, 2, 2)),
            dma((SWEEPS + 1, 2, 2)),
            dma((SWEEPS, 4)),
            dma((SWEEPS, 4)),
            dma((3,)),
            dma((3,)),
            pltpu.VMEM((both, rows, depth, width), bf16),
            pltpu.VMEM((width, width), f32),
            pltpu.VMEM((width, width), f32),
            pltpu.VMEM((2, members, chunk, width), f32),
            pltpu.VMEM((2, chunk, width), f32),
            pltpu.VMEM((width, width), f32),
            pltpu.VMEM((width, width), f32),
            pltpu.VMEM((owners, modes, cells // owners), bf16),
            dma((2, 4, members)),
            dma((owners,)),
            dma((owners,)),
        ],
        compiler_params=pltpu.CompilerParams(
            collective_id=0, has_side_effects=True, vmem_limit_bytes=60 << 20
        ),
    )(
        snap_init[0], channel_map[0], yface_vals[0], zface_vals[0], face_of, start_block[0].T,
        correlation,
    )
    return result[None, None]


def solution(mesh):
    return jax.shard_map(
        on_device,
        mesh=mesh,
        in_specs=(
            P("nbhd", "sub", None, None, None),
            P("nbhd", "sub", None, None),
            P("nbhd", None, None),
            P("nbhd", None, None),
            P("nbhd", None),
            P("nbhd", None, None),
            P(),
        ),
        out_specs=P("nbhd", "sub", None, None, None),
        check_vma=False,
    )
```

```python
import functools

import jax
import jax.numpy as jnp
from jax import lax
from jax.experimental import pallas as pl
from jax.experimental.pallas import tpu as pltpu
from jax.sharding import PartitionSpec as P

MESH = pl.DeviceIdType.MESH

SWEEPS = 3
ITERS = 4


def harmonic(left_k, right_k):
    return 2.0 * left_k * right_k / (left_k + right_k)


def relax_part(
    snap_ref, class_ref, yface_ref, zface_ref, face_ref, state_ref, mass_ref, stiff_ref,
    field, coef, compact, select, kappa, ghost_z, early, swap, zland, yland, rhs,
    class_pair, class_low, class_high, slab, slab_sem,
    swap_send, swap_recv, z_send, z_recv, y_send, y_recv, class_send, class_recv,
    members, stiff_ready,
):
    me_nbhd = lax.axis_index("nbhd")
    me = lax.axis_index("sub")
    half = lax.rem(me, 2)
    tower = me // 2
    towers = members // 2
    own, rows_all, depth, width = snap_ref.shape
    both = 2 * own
    rows = rows_all // 2
    top = both + 1
    base = 8
    inner = pl.ds(base, depth)

    def at(sub):
        return (me_nbhd, lax.rem(sub + members, members))

    partner = at(me + 1 - 2 * half)
    cross = at(me - 1 + 2 * half)
    lower = at(me - 2)
    upper = at(me + 2)

    def remote(src, dst, send, recv, device):
        return pltpu.make_async_remote_copy(
            src_ref=src, dst_ref=dst, send_sem=send, recv_sem=recv,
            device_id=device, device_id_type=MESH,
        )

    class_copies = [
        remote(class_ref, class_pair, class_send.at[0], class_recv.at[0], partner),
    ]
    class_copies[0].start()
    class_other = []

    def class_sends(plane, land, slot, devices):
        made = []
        for place, device in enumerate(devices):
            made.append(remote(
                class_ref.at[plane], land, class_send.at[1 + place], class_recv.at[slot], device
            ))
        return made

    @pl.when(half == 0)
    def _():
        for copy in class_sends(0, class_high, 2, (lower, cross)):
            copy.start()

    @pl.when(half == 1)
    def _():
        for copy in class_sends(own - 1, class_low, 1, (upper, cross)):
            copy.start()

    order = [0, 1] + list(range(own - 1, 1, -1))
    swaps = []
    for turn, q in enumerate(order):
        plane = q + half * (own - 1 - 2 * q)
        copy = remote(
            snap_ref.at[plane, pl.ds((rows - 1) * (1 - half), rows + 1)],
            swap.at[turn], swap_send.at[turn], swap_recv.at[turn], partner,
        )
        copy.start()
        swaps.append(copy)

    @pl.when(half == 0)
    def _():
        remote(
            snap_ref.at[0, pl.ds(0, rows)], zland.at[0, 1], z_send.at[0, 0, 0],
            z_recv.at[0, 1, 0], lower
        ).start()

    @pl.when(half == 1)
    def _():
        remote(
            snap_ref.at[own - 1, pl.ds(rows, rows)], zland.at[0, 0], z_send.at[0, 1, 0],
            z_recv.at[0, 0, 0], upper
        ).start()

    shift = 1 - half

    def fill_own(p, _):
        def fill(r, _):
            field[0, 1 + own * half + p, shift + r, inner, :] = slab[
                p, (rows - 1) * half + r
            ].astype(jnp.float32)
            return 0
        return lax.fori_loop(0, rows + 1, fill, 0)

    pltpu.make_async_copy(snap_ref, slab, slab_sem).wait()
    lax.fori_loop(0, own, fill_own, 0)

    face = face_ref[...]

    def pick(side):
        return jnp.where(face == side, 1.0, 0.0)

    side_y = jnp.where(half == 0, pick(0), pick(1))
    ghost_y = yface_ref[...].astype(jnp.float32) * side_y
    zface = zface_ref[...].astype(jnp.float32)
    ghost_z[0] = zface * pick(2)
    ghost_z[1] = zface * pick(3)

    def set_ghosts(p, _):
        for buf in range(2):
            field[buf, p + 1, (rows + 1) * half, inner, :] = ghost_y

            def one(y, _):
                field[buf, p + 1, y + 1, pl.ds(base - 1, 1), :] = ghost_z[0, pl.ds(rows * half + y, 1), :]
                field[buf, p + 1, y + 1, pl.ds(base + depth, 1), :] = ghost_z[1, pl.ds(rows * half + y, 1), :]
                return 0

            lax.fori_loop(0, rows, one, 0)
        return 0

    lax.fori_loop(0, both, set_ghosts, 0)

    def to_kappa(classes):
        return jnp.left_shift(1, 2 * classes).astype(jnp.float32)

    def land(slot, ref):
        remote(ref, ref, class_send.at[0], class_recv.at[slot], partner).wait_recv()

    land(0, class_pair)
    land(1, class_low)
    land(2, class_high)
    kappa[0] = to_kappa(class_low[...])
    kappa[top] = to_kappa(class_high[...])
    for p in range(own):
        kappa[1 + own * half + p] = to_kappa(class_ref[p])
        kappa[1 + own * (1 - half) + p] = to_kappa(class_pair[p])

    def coefficients(p, _):
        centre = kappa[p + 1]
        has_low = jnp.logical_or(tower > 0, p > 0)
        has_high = jnp.logical_or(tower < towers - 1, p < both - 1)
        face_low = harmonic(centre, kappa[p])
        face_high = harmonic(centre, kappa[p + 2])
        x_lower = jnp.where(has_low, face_low, centre)
        x_upper = jnp.where(has_high, face_high, centre)
        y_inner = harmonic(centre[1:], centre[:-1])
        y_lower = jnp.concatenate([centre[:1], y_inner], axis=0)
        y_upper = jnp.concatenate([y_inner, centre[-1:]], axis=0)
        z_inner = harmonic(centre[:, 1:], centre[:, :-1])
        z_lower = jnp.concatenate([centre[:, :1], z_inner], axis=1)
        z_upper = jnp.concatenate([z_inner, centre[:, -1:]], axis=1)
        denom = x_lower + x_upper + y_lower + y_upper + z_lower + z_upper
        inverse = 1.0 / denom
        compact[0, p] = jnp.where(has_low, face_low, 0.0) * inverse
        compact[1, p] = jnp.where(has_high, face_high, 0.0) * inverse
        compact[2, p] = y_lower * inverse
        compact[3, p] = y_upper * inverse
        compact[4, p] = z_lower * inverse
        compact[5, p] = z_upper * inverse
        compact[6, p] = denom
        compact[7, p] = centre * (1.0 / 16.0)
        return 0

    lax.fori_loop(0, both, coefficients, 0)
    taken = lax.broadcasted_iota(jnp.int32, select.shape, 0)
    given = lax.broadcasted_iota(jnp.int32, select.shape, 1)
    select[...] = jnp.where(lax.rem(taken, rows) == given // width, 1.0, 0.0).astype(jnp.bfloat16)

    def widen(kinds):
        def one(p, _):
            for kind in kinds:
                exact = compact[kind, p, pl.ds(pl.multiple_of(rows * half, rows), rows), :]
                terms = []
                for _ in range(3):
                    term = exact.astype(jnp.bfloat16).astype(jnp.float32)
                    terms.append(term)
                    exact = exact - term
                terms.append(jnp.zeros_like(exact))
                wide = lax.dot_general(
                    jnp.concatenate(terms, axis=0).astype(jnp.bfloat16), select[...],
                    (((0,), (0,)), ((), ())), preferred_element_type=jnp.float32,
                )
                for y in range(rows):
                    coef[kind, p, y] = wide[:, width * y:width * (y + 1)]
            return 0
        lax.fori_loop(0, both, one, 0)

    widen(range(3))
    swaps[0].wait_recv()

    @pl.when(half == 0)
    def _():
        remote(
            swap.at[0, pl.ds(0, rows)], zland.at[0, 0], z_send.at[0, 1, 0], z_recv.at[0, 0, 0],
            upper,
        ).start()

    @pl.when(half == 1)
    def _():
        remote(
            swap.at[0, pl.ds(1, rows)], zland.at[0, 1], z_send.at[0, 0, 0], z_recv.at[0, 1, 0],
            lower,
        ).start()

    widen(range(3, 6))

    def row(sweep, p, y):
        src, dst = (sweep + 1) % 2, sweep % 2
        c = [coef.at[kind, p - 1, y - 1] for kind in range(6)]
        value = c[0][...] * field[src, p - 1, y, inner, :]
        value += c[1][...] * field[src, p + 1, y, inner, :]
        value += c[2][...] * field[src, p, y - 1, inner, :]
        value += c[3][...] * field[src, p, y + 1, inner, :]
        value += c[4][...] * field[src, p, y, pl.ds(base - 1, depth), :]
        value += c[5][...] * field[src, p, y, pl.ds(base + 1, depth), :]
        low = value.astype(jnp.bfloat16)
        field[dst, p, y, inner, :] = low.astype(jnp.float32)
        if sweep < SWEEPS:
            early[sweep - 1, p - 1, y - 1] = low
        else:
            state_ref[p - 1, y - 1] = low
            field[dst, p, y, pl.ds(base + depth, 1), :] = jnp.zeros((1, width), jnp.float32)

    def line(sweep, p, first, count):
        def body(i, _):
            row(sweep, p, first + i)
            return 0
        lax.fori_loop(0, count, body, 0)

    chunk = rows // 2
    edge = rows - (rows - 1) * half

    def chunk_at(part):
        return chunk * half if part == 0 else chunk - chunk * half

    def held(sweep):
        return early.at[sweep - 1] if sweep < SWEEPS else state_ref

    def send_z(sweep, side, part):
        cells = pl.ds(chunk_at(part), chunk)
        remote(
            held(sweep).at[side * (both - 1), cells], zland.at[sweep, 1 - side, cells],
            z_send.at[sweep, side, part], z_recv.at[sweep, 1 - side, part], at(me - 2 + 4 * side),
        ).start()

    def send_y(sweep, part, first, count):
        planes = pl.ds(first, count)
        remote(
            held(sweep).at[planes, edge - 1], yland.at[sweep - 1, planes], y_send.at[sweep - 1, part],
            y_recv.at[sweep - 1, part], partner,
        ).start()

    def take_z(buf, sweep, side, part):
        cells = pl.ds(0, rows if sweep == 0 else chunk)
        remote(
            zland.at[sweep, side, cells], zland.at[sweep, side, cells], z_send.at[sweep, side, part],
            z_recv.at[sweep, side, part], lower,
        ).wait_recv()
        first = 0 if sweep == 0 else chunk_at(part)

        def fill(i, _):
            field[buf, top * side, first + i + 1, inner, :] = zland[sweep, side, first + i].astype(
                jnp.float32
            )
            return 0
        lax.fori_loop(0, rows if sweep == 0 else chunk, fill, 0)

    y_parts = ((1, own - 1), (own, own - 1), (0, 1), (both - 1, 1))

    def take_y(buf, sweep, part):
        first, count = y_parts[part]
        planes = pl.ds(first, count)
        remote(
            yland.at[sweep - 1, planes], yland.at[sweep - 1, planes], y_send.at[sweep - 1, part],
            y_recv.at[sweep - 1, part], partner,
        ).wait_recv()

        def fill(i, _):
            p = first + i
            field[buf, p + 1, (rows + 1) * (1 - half), inner, :] = yland[sweep - 1, p].astype(jnp.float32)
            return 0
        lax.fori_loop(0, count, fill, 0)

    def plane_of(e):
        return e + (1 - half) * (top - 2 * e)

    ahead = range(own + 2, both)
    for e in ahead:
        line(1, plane_of(e), 1, rows)
    for turn, q in enumerate(order):
        if turn:
            swaps[turn].wait_recv()
        plane = q + (1 - half) * (own - 1 - 2 * q)
        def fill(r, _):
            field[0, 1 + own * (1 - half) + plane, shift + r, inner, :] = swap[turn, r].astype(
                jnp.float32
            )
            return 0

        lax.fori_loop(0, rows + 1, fill, 0)
        if turn == 1:
            take_z(0, 0, 0, 0)
            take_z(0, 0, 1, 0)
            for e, side in ((both, half), (1, 1 - half)):
                line(1, plane_of(e), 1, rows)
                send_z(1, side, 0)
                send_z(1, side, 1)
                send_y(1, 2 + side, side * (both - 1), 1)
        if turn >= 2:
            line(1, plane_of(q + 2), 1, rows)
        if q == own - 1:
            send_y(1, half, 1 + (own - 1) * half, own - 1)
            widen((6, 7))
            for e in ahead:
                line(2, plane_of(e), 1 + half, rows - 1)
    line(1, plane_of(3), 1, rows)
    line(1, plane_of(2), 1, rows)
    send_y(1, 1 - half, 1 + (own - 1) * (1 - half), own - 1)

    def only_if_last(sweep, action):
        if sweep < SWEEPS:
            action()
        else:
            pl.when(half == 1)(action)

    for sweep in range(2, SWEEPS + 1):
        src = (sweep + 1) % 2
        sides = (0, 1) if sweep < SWEEPS else (0,)

        def middle(i, _):
            line(sweep, plane_of(i + 2), 1 + half, rows - 1)
            return 0
        lax.fori_loop(0, both - 2 - (len(ahead) if sweep == 2 else 0), middle, 0)
        def border(part):
            take_y(src, sweep - 1, part)
            first, count = y_parts[part]

            def body(i, _):
                row(sweep, first + i + 1, edge)
                return 0
            lax.fori_loop(0, count, body, 0)
            only_if_last(sweep, lambda: send_y(sweep, part, first, count))

        for side in (0, 1):
            take_z(src, sweep - 1, side, 0)
            line(sweep, 1 + side * (both - 1), 1 + chunk_at(0), chunk)
            if side in sides:
                send_z(sweep, side, 0)
        border(0)
        border(1)
        for side in (0, 1):
            take_y(src, sweep - 1, 2 + side)
            take_z(src, sweep - 1, side, 1)
            line(sweep, 1 + side * (both - 1), 1 + chunk_at(1), chunk)
            if side in sides:
                send_z(sweep, side, 1)

            def last_part():
                send_y(sweep, 2 + side, *y_parts[2 + side])
            only_if_last(sweep, last_part)

    last = SWEEPS % 2

    def stiff_row(p, y, place):
        here = field[last, p, y, inner, :]
        ahead = coef[1, p - 1, y - 1] * field[last, p + 1, y, inner, :]
        ahead += coef[3, p - 1, y - 1] * field[last, p, y + 1, inner, :]
        ahead += coef[5, p - 1, y - 1] * field[last, p, y, pl.ds(base + 1, depth), :]
        value = coef[6, p - 1, y - 1] * (here - 2.0 * ahead)
        high = value.astype(jnp.bfloat16)
        rest = (value - high.astype(jnp.float32)).astype(jnp.bfloat16)
        rhs[place, :, pl.ds(0, width)] = high
        rhs[place, :, pl.ds(width, width)] = rest

    def gram(left, count, used):
        right = rhs[pl.ds(0, count), :, pl.ds(0, used)].reshape(count * depth, used)
        return lax.dot_general(
            left.reshape(count * depth, width), right, (((0,), (0,)), ((), ())),
            preferred_element_type=jnp.float32,
        )

    def add_stiff(left, count):
        terms = gram(left, count, 2 * width)
        stiff_ref[...] += terms[:, :width] + terms[:, width:]

    mass_ref[...] = jnp.zeros_like(mass_ref)
    stiff_ref[...] = jnp.zeros_like(stiff_ref)

    def weigh(p, _):
        def body(y, _):
            here = state_ref[p, y].astype(jnp.float32)
            rhs[y, :, pl.ds(0, width)] = (here * coef[7, p, y]).astype(jnp.bfloat16)
            return 0
        lax.fori_loop(0, rows, body, 0)
        mass_ref[...] += gram(state_ref[p], rows, width)
        return 0
    def inside(i, _):
        def body(y, _):
            stiff_row(i + 1, y + 1, y)
            return 0
        lax.fori_loop(0, rows - 1, body, 0)
        add_stiff(state_ref[i, pl.ds(0, rows - 1)], rows - 1)
        return 0
    lax.fori_loop(0, both - 1, inside, 0)
    lax.fori_loop(0, own - 1, weigh, 0)

    @pl.when(half == 0)
    def _():
        for part in range(4):
            take_y(last, SWEEPS, part)

    @pl.when(half == 1)
    def _():
        def clear(p, _):
            field[last, p + 1, rows + 1, inner, :] = jnp.zeros((depth, width), jnp.float32)
            return 0
        lax.fori_loop(0, both, clear, 0)

    def side(i, _):
        stiff_row(i + 1, rows, i)
        return 0
    lax.fori_loop(0, both - 1, side, 0)
    add_stiff(state_ref[pl.ds(0, both - 1), rows - 1], both - 1)
    take_z(last, SWEEPS, 1, 0)
    take_z(last, SWEEPS, 1, 1)

    def roof(y, _):
        stiff_row(both, y + 1, y)
        return 0
    lax.fori_loop(0, rows, roof, 0)
    add_stiff(state_ref[both - 1], rows)
    stiff_ready()
    lax.fori_loop(own - 1, both, weigh, 0)

    def drain():
        class_copies[0].wait_send()
        for place in range(2):
            remote(
                class_ref.at[0], class_low, class_send.at[1 + place], class_recv.at[1], partner
            ).wait_send()
        for copy in swaps:
            copy.wait_send()
        for side in range(2):
            remote(
                snap_ref.at[0, pl.ds(0, rows)], zland.at[0, 0], z_send.at[0, side, 0], z_recv.at[0, 0, 0], lower
            ).wait_send()

        def left_z(sweep, side, part):
            cells = pl.ds(0, chunk)
            remote(
                held(sweep).at[0, cells], zland.at[sweep, 0, cells], z_send.at[sweep, side, part],
                z_recv.at[sweep, 0, part], lower,
            ).wait_send()

        def left_y(sweep, part):
            planes = pl.ds(*y_parts[part])
            remote(
                held(sweep).at[planes, 0], yland.at[sweep - 1, planes], y_send.at[sweep - 1, part],
                y_recv.at[sweep - 1, part], partner,
            ).wait_send()

        for sweep in range(1, SWEEPS + 1):
            for side in range(2 if sweep < SWEEPS else 1):
                for part in range(2):
                    left_z(sweep, side, part)

            def all_y():
                for part in range(4):
                    left_y(sweep, part)
            only_if_last(sweep, all_y)

    return drain


TILE = 8


def spread(tile, col, width):
    return jnp.broadcast_to(tile[:, col:col + 1], (tile.shape[0], width))


def eliminate_spd(full, size, block):
    lanes = lax.broadcasted_iota(jnp.int32, (TILE, size), 1)
    rows = lax.broadcasted_iota(jnp.int32, (TILE, size), 0)
    wide = lax.broadcasted_iota(jnp.int32, (size, size), 1)
    block_lanes = lax.broadcasted_iota(jnp.int32, (block, size), 1)
    count = block // TILE
    for first in range(0, size, block):
        panel = full[first:first + block]
        signed = jnp.where(block_lanes < first, -panel, panel) if first else panel
        tiles = [panel[TILE * u:TILE * (u + 1)] for u in range(count)]
        for t in range(count):
            base = first + TILE * t
            columns = [[spread(tile, base + j, size) for tile in tiles] for j in range(TILE)]
            for i in range(TILE):
                here = rows == i
                at_col = lanes == base + i
                lead = columns[i]
                pivot = 1.0 / lead[t][i:i + 1]
                row = jnp.where(at_col[:1], 1.0, tiles[t][i:i + 1]) * pivot
                for j in range(i + 1, TILE):
                    scaled = columns[j][t][i:i + 1] * pivot
                    columns[j] = [columns[j][u] - lead[u] * scaled for u in range(count)]
                    columns[j][t] = jnp.where(here, scaled, columns[j][t])
                tiles = [jnp.where(at_col, 0.0, tiles[u]) - lead[u] * row for u in range(count)]
                tiles[t] = jnp.where(here, row, tiles[t])
        panel = jnp.concatenate(tiles, axis=0)
        inside = (wide >= first) & (wide < first + block)
        update = lax.dot_general(
            signed, panel, (((0,), (0,)), ((), ())),
            precision=lax.Precision.HIGHEST, preferred_element_type=jnp.float32,
        )
        rest = jnp.where(inside, 0.0, full) - update
        parts = []
        if first:
            parts.append(rest[:first])
        parts.append(panel)
        if first + block < size:
            parts.append(rest[first + block:])
        full = jnp.concatenate(parts, axis=0)
    return full


def normalize(inner, vectors):
    width = vectors.shape[1]
    count = inner.shape[0] // TILE
    rows = lax.broadcasted_iota(jnp.int32, (TILE, width), 0)
    left = [inner[TILE * u:TILE * (u + 1)] for u in range(count)]
    right = [vectors[TILE * u:TILE * (u + 1)] for u in range(count)]
    scales = []
    for t in range(count):
        columns = [
            [spread(left[u], TILE * t + j, width) for u in range(t, count)] for j in range(TILE)
        ]
        scale = jnp.zeros((TILE, width), jnp.float32)
        for i in range(TILE):
            lead = columns[i]
            value = lead[0][i:i + 1]
            pivot = 1.0 / value
            scale = jnp.where(rows == i, value, scale)
            for j in range(i + 1, TILE):
                scaled = columns[j][0][i:i + 1] * pivot
                columns[j] = [column - part * scaled for column, part in zip(columns[j], lead)]
            below = [jnp.where(rows > i, lead[0], 0.0)] + lead[1:]
            mate = right[t][i:i + 1] * pivot
            for u in range(t, count):
                right[u] = right[u] - below[u - t] * mate
            if t + 1 < count:
                ahead = left[t][i:i + 1] * pivot[:, :left[t].shape[1]]
                for u in range(t, count):
                    left[u] = left[u] - below[u - t][:, :left[t].shape[1]] * ahead
        scales.append(scale)
    return jnp.concatenate([tile / jnp.sqrt(scale) for tile, scale in zip(right, scales)], axis=0)


def whole_kernel(
    snap_ref, class_ref, yface_ref, zface_ref, face_ref, start_ref, corr_ref, out_ref,
    field, coef, compact, select, kappa, ghost_z, early, swap, zland, yland, rhs,
    class_pair, class_low, class_high, slab, slab_sem,
    swap_send, swap_recv, z_send, z_recv, y_send, y_recv, class_send, class_recv,
    state, mass_part, stiff_part, slots, summed, mass_total, stiff_total, stage,
    sum_sem, send_out, recv_out,
    *, members, owners, own, cell_count,
):
    me_sub = lax.axis_index("sub")
    me_nbhd = lax.axis_index("nbhd")
    size = mass_part.shape[1]
    chunk = size // members
    half = lax.rem(me_sub, 2)
    tower = me_sub - half
    across = owners // own
    mine = across // 2
    from_half = lax.rem(me_nbhd, across) // mine
    whole = jnp.where(from_half == half, 1, 0)

    pltpu.make_async_copy(snap_ref, slab, slab_sem).start()

    def sub_at(step):
        return lax.rem(me_sub + step, members)

    def is_me(nbhd):
        return jnp.logical_and(nbhd == me_nbhd, from_half == half)

    barrier = pltpu.get_barrier_semaphore()
    for step in range(1, members):
        pl.semaphore_signal(barrier, inc=1, device_id=(me_nbhd, sub_at(step)), device_id_type=MESH)
    for nbhd in range(owners):
        @pl.when(jnp.logical_not(is_me(nbhd)))
        def _():
            pl.semaphore_signal(
                barrier, inc=1, device_id=(nbhd, tower + from_half), device_id_type=MESH
            )
    pl.semaphore_wait(barrier, members - 1 + owners - whole)

    def rows_of(sub):
        return pl.ds(pl.multiple_of(sub * chunk, chunk), chunk)

    def scatter(which, partial_ref):
        copies = []
        for step in range(1, members):
            peer = sub_at(step)
            copy = pltpu.make_async_remote_copy(
                src_ref=partial_ref.at[rows_of(peer)],
                dst_ref=slots.at[which, step],
                send_sem=sum_sem.at[which, 0, step],
                recv_sem=sum_sem.at[which, 1, step],
                device_id=(me_nbhd, peer),
                device_id_type=MESH,
            )
            copy.start()
            copies.append(copy)
        return copies

    def share(which, partial_ref, total_ref, copies):
        acc = partial_ref[rows_of(me_sub)]
        for step in range(1, members):
            copies[step - 1].wait_recv()
            acc = acc + slots[which, step]
        summed[which] = acc
        total_ref[rows_of(me_sub)] = acc
        spreads = []
        for step in range(1, members):
            copy = pltpu.make_async_remote_copy(
                src_ref=summed.at[which],
                dst_ref=total_ref.at[rows_of(me_sub)],
                send_sem=sum_sem.at[which, 2, step],
                recv_sem=sum_sem.at[which, 3, step],
                device_id=(me_nbhd, sub_at(step)),
                device_id_type=MESH,
            )
            copy.start()
            spreads.append(copy)
        return spreads

    sent = []
    drain = relax_part(
        snap_ref, class_ref, yface_ref, zface_ref, face_ref, state, mass_part, stiff_part,
        field, coef, compact, select, kappa, ghost_z, early, swap, zland, yland, rhs,
        class_pair, class_low, class_high, slab, slab_sem,
        swap_send, swap_recv, z_send, z_recv, y_send, y_recv, class_send, class_recv,
        members, lambda: sent.append(scatter(1, stiff_part)),
    )
    sent.append(scatter(0, mass_part))
    sent.append(share(1, stiff_part, stiff_total, sent[0]))
    sent.append(share(0, mass_part, mass_total, sent[1]))

    dot = functools.partial(
        lax.dot_general, precision=lax.Precision.HIGHEST, preferred_element_type=jnp.float32
    )
    for copy in sent[2]:
        copy.wait_recv()
    stiff = stiff_total[...]
    stiff = (stiff + stiff.T) * (0.5 / cell_count)
    inverse = eliminate_spd(stiff, size, 32)
    for copy in sent[3]:
        copy.wait_recv()
    mass = mass_total[...] / cell_count
    step_map = dot(mass, inverse, (((1,), (0,)), ((), ())))
    both = jnp.concatenate([step_map, dot(step_map, mass, (((1,), (0,)), ((), ())))], axis=1)
    rows = start_ref[...]
    for turn in range(ITERS):
        pair = dot(rows, both, (((1,), (0,)), ((), ())))
        solved, image = pair[:, :size], pair[:, size:]
        inner = dot(solved, image, (((1,), (1,)), ((), ())))
        inner = 0.5 * (inner + inner.T)
        rows = normalize(inner, solved)
    modes = rows.astype(jnp.bfloat16)

    lines = state.shape[1] // mine

    def piece(index, owner):
        values = lax.dot_general(
            modes, state[index // mine, pl.ds(lax.rem(index, mine) * lines, lines)].reshape(
                lines * state.shape[2], size
            ), (((1,), (1,)), ((), ())), preferred_element_type=jnp.float32,
        )
        return (values * corr_ref[me_nbhd, owner].astype(jnp.float32)).astype(jnp.bfloat16)

    def leave(step, owner, sub):
        return pltpu.make_async_remote_copy(
            src_ref=stage.at[step],
            dst_ref=out_ref.at[me_nbhd],
            send_sem=send_out.at[step],
            recv_sem=recv_out.at[me_nbhd],
            device_id=(owner, sub),
            device_id_type=MESH,
        )

    leaving = []
    for step in range(owners):
        index = lax.rem(step + me_nbhd, owners)
        level = index // mine
        owner = across * lax.rem(level, own) + mine * half + lax.rem(index, mine)
        sub = tower + level // own
        here = jnp.logical_and(owner == me_nbhd, sub == me_sub)
        stage[step] = piece(index, owner)

        @pl.when(jnp.logical_not(here))
        def _():
            leave(step, owner, sub).start()

        @pl.when(here)
        def _():
            out_ref[me_nbhd] = stage[step]

        leaving.append((step, owner, sub, here))
    for nbhd in range(owners):
        @pl.when(jnp.logical_not(is_me(nbhd)))
        def _():
            pltpu.make_async_remote_copy(
                src_ref=stage.at[0], dst_ref=out_ref.at[nbhd], send_sem=send_out.at[0],
                recv_sem=recv_out.at[nbhd], device_id=(nbhd, me_sub), device_id_type=MESH,
            ).wait_recv()
    for step, owner, sub, here in leaving:
        @pl.when(jnp.logical_not(here))
        def _():
            leave(step, owner, sub).wait_send()
    for copies in sent:
        for copy in copies:
            copy.wait_send()
    drain()


def on_device(snap_init, channel_map, yface_vals, zface_vals, face_of, start_block, correlation):
    own, rows_all, depth, width = snap_init.shape[1:]
    modes = start_block.shape[2]
    members, owners = lax.axis_size("sub"), lax.axis_size("nbhd")
    both, rows = 2 * own, rows_all // 2
    cells = own * rows_all * depth
    chunk = width // members
    vmem = pl.BlockSpec(memory_space=pltpu.VMEM)
    f32, bf16 = jnp.float32, jnp.bfloat16
    dma = pltpu.SemaphoreType.DMA
    result = pl.pallas_call(
        functools.partial(
            whole_kernel, members=members, owners=owners, own=own, cell_count=float(cells * members)
        ),
        out_shape=jax.ShapeDtypeStruct((owners, modes, cells // owners), bf16),
        in_specs=[pl.BlockSpec(memory_space=pl.ANY)] + [vmem] * 5
        + [pl.BlockSpec(memory_space=pltpu.SMEM)],
        out_specs=vmem,
        scratch_shapes=[
            pltpu.VMEM((2, both + 2, rows + 2, depth + 16, width), f32),
            pltpu.VMEM((8, both, rows, depth, width), f32),
            pltpu.VMEM((8, both, rows_all, depth), f32),
            pltpu.VMEM((4 * rows, rows * width), bf16),
            pltpu.VMEM((both + 2, rows_all, depth), f32),
            pltpu.VMEM((2, rows_all, width), f32),
            pltpu.VMEM((SWEEPS - 1, both, rows, depth, width), bf16),
            pltpu.VMEM((own, rows + 1, depth, width), bf16),
            pltpu.VMEM((SWEEPS + 1, 2, rows, depth, width), bf16),
            pltpu.VMEM((SWEEPS, both, depth, width), bf16),
            pltpu.VMEM((max(both, rows), depth, 2 * width), bf16),
            pltpu.VMEM((own, rows_all, depth), jnp.int32),
            pltpu.VMEM((rows_all, depth), jnp.int32),
            pltpu.VMEM((rows_all, depth), jnp.int32),
            pltpu.VMEM((own, rows_all, depth, width), bf16),
            dma,
            dma((own,)),
            dma((own,)),
            dma((SWEEPS + 1, 2, 2)),
            dma((SWEEPS + 1, 2, 2)),
            dma((SWEEPS, 4)),
            dma((SWEEPS, 4)),
            dma((3,)),
            dma((3,)),
            pltpu.VMEM((both, rows, depth, width), bf16),
            pltpu.VMEM((width, width), f32),
            pltpu.VMEM((width, width), f32),
            pltpu.VMEM((2, members, chunk, width), f32),
            pltpu.VMEM((2, chunk, width), f32),
            pltpu.VMEM((width, width), f32),
            pltpu.VMEM((width, width), f32),
            pltpu.VMEM((owners, modes, cells // owners), bf16),
            dma((2, 4, members)),
            dma((owners,)),
            dma((owners,)),
        ],
        compiler_params=pltpu.CompilerParams(
            collective_id=0, has_side_effects=True, vmem_limit_bytes=60 << 20
        ),
    )(
        snap_init[0], channel_map[0], yface_vals[0], zface_vals[0], face_of, start_block[0].T,
        correlation,
    )
    return result[None, None]


def solution(mesh):
    return jax.shard_map(
        on_device,
        mesh=mesh,
        in_specs=(
            P("nbhd", "sub", None, None, None),
            P("nbhd", "sub", None, None),
            P("nbhd", None, None),
            P("nbhd", None, None),
            P("nbhd", None),
            P("nbhd", None, None),
            P(),
        ),
        out_specs=P("nbhd", "sub", None, None, None),
        check_vma=False,
    )
```

```python
import functools

import jax
import jax.numpy as jnp
from jax import lax
from jax.experimental import pallas as pl
from jax.experimental.pallas import tpu as pltpu
from jax.sharding import PartitionSpec as P

MESH = pl.DeviceIdType.MESH

SWEEPS = 3
ITERS = 4


def harmonic(left_k, right_k):
    return 2.0 * left_k * right_k / (left_k + right_k)


def relax_part(
    snap_ref, class_ref, yface_ref, zface_ref, face_ref, state_ref, mass_ref, stiff_ref,
    field, coef, compact, select, kappa, ghost_z, early, swap, zland, yland, rhs,
    class_pair, class_low, class_high, slab, slab_sem,
    swap_send, swap_recv, z_send, z_recv, y_send, y_recv, class_send, class_recv,
    members, stiff_ready,
):
    me_nbhd = lax.axis_index("nbhd")
    me = lax.axis_index("sub")
    half = lax.rem(me, 2)
    tower = me // 2
    towers = members // 2
    own, rows_all, depth, width = snap_ref.shape
    both = 2 * own
    rows = rows_all // 2
    top = both + 1
    base = 8
    inner = pl.ds(base, depth)

    def at(sub):
        return (me_nbhd, lax.rem(sub + members, members))

    partner = at(me + 1 - 2 * half)
    cross = at(me - 1 + 2 * half)
    lower = at(me - 2)
    upper = at(me + 2)

    def remote(src, dst, send, recv, device):
        return pltpu.make_async_remote_copy(
            src_ref=src, dst_ref=dst, send_sem=send, recv_sem=recv,
            device_id=device, device_id_type=MESH,
        )

    class_copies = [
        remote(class_ref, class_pair, class_send.at[0], class_recv.at[0], partner),
    ]
    class_copies[0].start()
    class_other = []

    def class_sends(plane, land, slot, devices):
        made = []
        for place, device in enumerate(devices):
            made.append(remote(
                class_ref.at[plane], land, class_send.at[1 + place], class_recv.at[slot], device
            ))
        return made

    @pl.when(half == 0)
    def _():
        for copy in class_sends(0, class_high, 2, (lower, cross)):
            copy.start()

    @pl.when(half == 1)
    def _():
        for copy in class_sends(own - 1, class_low, 1, (upper, cross)):
            copy.start()

    order = [0, 1] + list(range(own - 1, 1, -1))
    swaps = []
    for turn, q in enumerate(order):
        plane = q + half * (own - 1 - 2 * q)
        copy = remote(
            snap_ref.at[plane, pl.ds((rows - 1) * (1 - half), rows + 1)],
            swap.at[turn], swap_send.at[turn], swap_recv.at[turn], partner,
        )
        copy.start()
        swaps.append(copy)

    @pl.when(half == 0)
    def _():
        remote(
            snap_ref.at[0, pl.ds(0, rows)], zland.at[0, 1], z_send.at[0, 0, 0],
            z_recv.at[0, 1, 0], lower
        ).start()

    @pl.when(half == 1)
    def _():
        remote(
            snap_ref.at[own - 1, pl.ds(rows, rows)], zland.at[0, 0], z_send.at[0, 1, 0],
            z_recv.at[0, 0, 0], upper
        ).start()

    shift = 1 - half

    def fill_own(p, _):
        def fill(r, _):
            field[0, 1 + own * half + p, shift + r, inner, :] = slab[
                p, (rows - 1) * half + r
            ].astype(jnp.float32)
            return 0
        return lax.fori_loop(0, rows + 1, fill, 0)

    pltpu.make_async_copy(snap_ref, slab, slab_sem).wait()
    lax.fori_loop(0, own, fill_own, 0)

    face = face_ref[...]

    def pick(side):
        return jnp.where(face == side, 1.0, 0.0)

    side_y = jnp.where(half == 0, pick(0), pick(1))
    ghost_y = yface_ref[...].astype(jnp.float32) * side_y
    zface = zface_ref[...].astype(jnp.float32)
    ghost_z[0] = zface * pick(2)
    ghost_z[1] = zface * pick(3)

    def set_ghosts(p, _):
        for buf in range(2):
            field[buf, p + 1, (rows + 1) * half, inner, :] = ghost_y

            def one(y, _):
                field[buf, p + 1, y + 1, pl.ds(base - 1, 1), :] = ghost_z[0, pl.ds(rows * half + y, 1), :]
                field[buf, p + 1, y + 1, pl.ds(base + depth, 1), :] = ghost_z[1, pl.ds(rows * half + y, 1), :]
                return 0

            lax.fori_loop(0, rows, one, 0)
        return 0

    lax.fori_loop(0, both, set_ghosts, 0)

    def to_kappa(classes):
        return jnp.left_shift(1, 2 * classes).astype(jnp.float32)

    def land(slot, ref):
        remote(ref, ref, class_send.at[0], class_recv.at[slot], partner).wait_recv()

    land(0, class_pair)
    land(1, class_low)
    land(2, class_high)
    kappa[0] = to_kappa(class_low[...])
    kappa[top] = to_kappa(class_high[...])
    for p in range(own):
        kappa[1 + own * half + p] = to_kappa(class_ref[p])
        kappa[1 + own * (1 - half) + p] = to_kappa(class_pair[p])

    def coefficients(p, _):
        centre = kappa[p + 1]
        has_low = jnp.logical_or(tower > 0, p > 0)
        has_high = jnp.logical_or(tower < towers - 1, p < both - 1)
        face_low = harmonic(centre, kappa[p])
        face_high = harmonic(centre, kappa[p + 2])
        x_lower = jnp.where(has_low, face_low, centre)
        x_upper = jnp.where(has_high, face_high, centre)
        y_inner = harmonic(centre[1:], centre[:-1])
        y_lower = jnp.concatenate([centre[:1], y_inner], axis=0)
        y_upper = jnp.concatenate([y_inner, centre[-1:]], axis=0)
        z_inner = harmonic(centre[:, 1:], centre[:, :-1])
        z_lower = jnp.concatenate([centre[:, :1], z_inner], axis=1)
        z_upper = jnp.concatenate([z_inner, centre[:, -1:]], axis=1)
        denom = x_lower + x_upper + y_lower + y_upper + z_lower + z_upper
        inverse = 1.0 / denom
        compact[0, p] = jnp.where(has_low, face_low, 0.0) * inverse
        compact[1, p] = jnp.where(has_high, face_high, 0.0) * inverse
        compact[2, p] = y_lower * inverse
        compact[3, p] = y_upper * inverse
        compact[4, p] = z_lower * inverse
        compact[5, p] = z_upper * inverse
        compact[6, p] = denom
        compact[7, p] = centre * (1.0 / 16.0)
        return 0

    lax.fori_loop(0, both, coefficients, 0)
    taken = lax.broadcasted_iota(jnp.int32, select.shape, 0)
    given = lax.broadcasted_iota(jnp.int32, select.shape, 1)
    select[...] = jnp.where(lax.rem(taken, rows) == given // width, 1.0, 0.0).astype(jnp.bfloat16)

    def widen(kinds):
        def one(p, _):
            for kind in kinds:
                exact = compact[kind, p, pl.ds(pl.multiple_of(rows * half, rows), rows), :]
                terms = []
                for _ in range(3):
                    term = exact.astype(jnp.bfloat16).astype(jnp.float32)
                    terms.append(term)
                    exact = exact - term
                terms.append(jnp.zeros_like(exact))
                wide = lax.dot_general(
                    jnp.concatenate(terms, axis=0).astype(jnp.bfloat16), select[...],
                    (((0,), (0,)), ((), ())), preferred_element_type=jnp.float32,
                )
                for y in range(rows):
                    coef[kind, p, y] = wide[:, width * y:width * (y + 1)]
            return 0
        lax.fori_loop(0, both, one, 0)

    widen(range(3))
    swaps[0].wait_recv()

    @pl.when(half == 0)
    def _():
        remote(
            swap.at[0, pl.ds(0, rows)], zland.at[0, 0], z_send.at[0, 1, 0], z_recv.at[0, 0, 0],
            upper,
        ).start()

    @pl.when(half == 1)
    def _():
        remote(
            swap.at[0, pl.ds(1, rows)], zland.at[0, 1], z_send.at[0, 0, 0], z_recv.at[0, 1, 0],
            lower,
        ).start()

    widen(range(3, 6))

    def row(sweep, p, y):
        src, dst = (sweep + 1) % 2, sweep % 2
        c = [coef.at[kind, p - 1, y - 1] for kind in range(6)]
        value = c[0][...] * field[src, p - 1, y, inner, :]
        value += c[1][...] * field[src, p + 1, y, inner, :]
        value += c[2][...] * field[src, p, y - 1, inner, :]
        value += c[3][...] * field[src, p, y + 1, inner, :]
        value += c[4][...] * field[src, p, y, pl.ds(base - 1, depth), :]
        value += c[5][...] * field[src, p, y, pl.ds(base + 1, depth), :]
        low = value.astype(jnp.bfloat16)
        field[dst, p, y, inner, :] = low.astype(jnp.float32)
        if sweep < SWEEPS:
            early[sweep - 1, p - 1, y - 1] = low
        else:
            state_ref[p - 1, y - 1] = low
            field[dst, p, y, pl.ds(base + depth, 1), :] = jnp.zeros((1, width), jnp.float32)

    def line(sweep, p, first, count):
        def body(i, _):
            row(sweep, p, first + i)
            return 0
        lax.fori_loop(0, count, body, 0)

    chunk = rows // 2
    edge = rows - (rows - 1) * half

    def chunk_at(part):
        return chunk * half if part == 0 else chunk - chunk * half

    def held(sweep):
        return early.at[sweep - 1] if sweep < SWEEPS else state_ref

    def send_z(sweep, side, part):
        cells = pl.ds(chunk_at(part), chunk)
        remote(
            held(sweep).at[side * (both - 1), cells], zland.at[sweep, 1 - side, cells],
            z_send.at[sweep, side, part], z_recv.at[sweep, 1 - side, part], at(me - 2 + 4 * side),
        ).start()

    def send_y(sweep, part, first, count):
        planes = pl.ds(first, count)
        remote(
            held(sweep).at[planes, edge - 1], yland.at[sweep - 1, planes], y_send.at[sweep - 1, part],
            y_recv.at[sweep - 1, part], partner,
        ).start()

    def take_z(buf, sweep, side, part):
        cells = pl.ds(0, rows if sweep == 0 else chunk)
        remote(
            zland.at[sweep, side, cells], zland.at[sweep, side, cells], z_send.at[sweep, side, part],
            z_recv.at[sweep, side, part], lower,
        ).wait_recv()
        first = 0 if sweep == 0 else chunk_at(part)

        def fill(i, _):
            field[buf, top * side, first + i + 1, inner, :] = zland[sweep, side, first + i].astype(
                jnp.float32
            )
            return 0
        lax.fori_loop(0, rows if sweep == 0 else chunk, fill, 0)

    y_parts = ((1, own - 1), (own, own - 1), (0, 1), (both - 1, 1))

    def take_y(buf, sweep, part):
        first, count = y_parts[part]
        planes = pl.ds(first, count)
        remote(
            yland.at[sweep - 1, planes], yland.at[sweep - 1, planes], y_send.at[sweep - 1, part],
            y_recv.at[sweep - 1, part], partner,
        ).wait_recv()

        def fill(i, _):
            p = first + i
            field[buf, p + 1, (rows + 1) * (1 - half), inner, :] = yland[sweep - 1, p].astype(jnp.float32)
            return 0
        lax.fori_loop(0, count, fill, 0)

    def plane_of(e):
        return e + (1 - half) * (top - 2 * e)

    ahead = range(own + 2, both)
    for e in ahead:
        line(1, plane_of(e), 1, rows)
    for turn, q in enumerate(order):
        if turn:
            swaps[turn].wait_recv()
        plane = q + (1 - half) * (own - 1 - 2 * q)
        def fill(r, _):
            field[0, 1 + own * (1 - half) + plane, shift + r, inner, :] = swap[turn, r].astype(
                jnp.float32
            )
            return 0

        lax.fori_loop(0, rows + 1, fill, 0)
        if turn == 1:
            take_z(0, 0, 0, 0)
            take_z(0, 0, 1, 0)
            for e, side in ((both, half), (1, 1 - half)):
                line(1, plane_of(e), 1, rows)
                send_z(1, side, 0)
                send_z(1, side, 1)
                send_y(1, 2 + side, side * (both - 1), 1)
        if 2 <= turn < own - 1:
            line(1, plane_of(q + 2), 1, rows)
        if q == own - 1:
            send_y(1, half, 1 + (own - 1) * half, own - 1)
            widen((6, 7))
            for e in ahead:
                line(2, plane_of(e), 1 + half, rows - 1)
    for e in range(own, 1, -1):
        row(1, plane_of(e), edge)
    send_y(1, 1 - half, 1 + (own - 1) * (1 - half), own - 1)
    for e in range(own, 1, -1):
        line(1, plane_of(e), 1 + half, rows - 1)

    def only_if_last(sweep, action):
        if sweep < SWEEPS:
            action()
        else:
            pl.when(half == 1)(action)

    for sweep in range(2, SWEEPS + 1):
        src = (sweep + 1) % 2
        sides = (0, 1) if sweep < SWEEPS else (0,)

        def middle(i, _):
            line(sweep, plane_of(i + 2), 1 + half, rows - 1)
            return 0
        lax.fori_loop(0, both - 2 - (len(ahead) if sweep == 2 else 0), middle, 0)
        def border(part):
            take_y(src, sweep - 1, part)
            first, count = y_parts[part]

            def body(i, _):
                row(sweep, first + i + 1, edge)
                return 0
            lax.fori_loop(0, count, body, 0)
            only_if_last(sweep, lambda: send_y(sweep, part, first, count))

        for side in (0, 1):
            take_z(src, sweep - 1, side, 0)
            line(sweep, 1 + side * (both - 1), 1 + chunk_at(0), chunk)
            if side in sides:
                send_z(sweep, side, 0)
        border(0)
        border(1)
        for side in (0, 1):
            take_y(src, sweep - 1, 2 + side)
            take_z(src, sweep - 1, side, 1)
            line(sweep, 1 + side * (both - 1), 1 + chunk_at(1), chunk)
            if side in sides:
                send_z(sweep, side, 1)

            def last_part():
                send_y(sweep, 2 + side, *y_parts[2 + side])
            only_if_last(sweep, last_part)

    last = SWEEPS % 2

    def stiff_row(p, y, place):
        here = field[last, p, y, inner, :]
        ahead = coef[1, p - 1, y - 1] * field[last, p + 1, y, inner, :]
        ahead += coef[3, p - 1, y - 1] * field[last, p, y + 1, inner, :]
        ahead += coef[5, p - 1, y - 1] * field[last, p, y, pl.ds(base + 1, depth), :]
        value = coef[6, p - 1, y - 1] * (here - 2.0 * ahead)
        high = value.astype(jnp.bfloat16)
        rest = (value - high.astype(jnp.float32)).astype(jnp.bfloat16)
        rhs[place, :, pl.ds(0, width)] = high
        rhs[place, :, pl.ds(width, width)] = rest

    def gram(left, count, used):
        right = rhs[pl.ds(0, count), :, pl.ds(0, used)].reshape(count * depth, used)
        return lax.dot_general(
            left.reshape(count * depth, width), right, (((0,), (0,)), ((), ())),
            preferred_element_type=jnp.float32,
        )

    def add_stiff(left, count):
        terms = gram(left, count, 2 * width)
        stiff_ref[...] += terms[:, :width] + terms[:, width:]

    mass_ref[...] = jnp.zeros_like(mass_ref)
    stiff_ref[...] = jnp.zeros_like(stiff_ref)

    def weigh(p, _):
        def body(y, _):
            here = state_ref[p, y].astype(jnp.float32)
            rhs[y, :, pl.ds(0, width)] = (here * coef[7, p, y]).astype(jnp.bfloat16)
            return 0
        lax.fori_loop(0, rows, body, 0)
        mass_ref[...] += gram(state_ref[p], rows, width)
        return 0
    def inside(i, _):
        def body(y, _):
            stiff_row(i + 1, y + 1, y)
            return 0
        lax.fori_loop(0, rows - 1, body, 0)
        add_stiff(state_ref[i, pl.ds(0, rows - 1)], rows - 1)
        return 0
    lax.fori_loop(0, both - 1, inside, 0)
    lax.fori_loop(0, own - 1, weigh, 0)

    @pl.when(half == 0)
    def _():
        for part in range(4):
            take_y(last, SWEEPS, part)

    @pl.when(half == 1)
    def _():
        def clear(p, _):
            field[last, p + 1, rows + 1, inner, :] = jnp.zeros((depth, width), jnp.float32)
            return 0
        lax.fori_loop(0, both, clear, 0)

    def side(i, _):
        stiff_row(i + 1, rows, i)
        return 0
    lax.fori_loop(0, both - 1, side, 0)
    add_stiff(state_ref[pl.ds(0, both - 1), rows - 1], both - 1)
    take_z(last, SWEEPS, 1, 0)
    take_z(last, SWEEPS, 1, 1)

    def roof(y, _):
        stiff_row(both, y + 1, y)
        return 0
    lax.fori_loop(0, rows, roof, 0)
    add_stiff(state_ref[both - 1], rows)
    stiff_ready()
    lax.fori_loop(own - 1, both, weigh, 0)

    def drain():
        class_copies[0].wait_send()
        for place in range(2):
            remote(
                class_ref.at[0], class_low, class_send.at[1 + place], class_recv.at[1], partner
            ).wait_send()
        for copy in swaps:
            copy.wait_send()
        for side in range(2):
            remote(
                snap_ref.at[0, pl.ds(0, rows)], zland.at[0, 0], z_send.at[0, side, 0], z_recv.at[0, 0, 0], lower
            ).wait_send()

        def left_z(sweep, side, part):
            cells = pl.ds(0, chunk)
            remote(
                held(sweep).at[0, cells], zland.at[sweep, 0, cells], z_send.at[sweep, side, part],
                z_recv.at[sweep, 0, part], lower,
            ).wait_send()

        def left_y(sweep, part):
            planes = pl.ds(*y_parts[part])
            remote(
                held(sweep).at[planes, 0], yland.at[sweep - 1, planes], y_send.at[sweep - 1, part],
                y_recv.at[sweep - 1, part], partner,
            ).wait_send()

        for sweep in range(1, SWEEPS + 1):
            for side in range(2 if sweep < SWEEPS else 1):
                for part in range(2):
                    left_z(sweep, side, part)

            def all_y():
                for part in range(4):
                    left_y(sweep, part)
            only_if_last(sweep, all_y)

    return drain


TILE = 8


def spread(tile, col, width):
    return jnp.broadcast_to(tile[:, col:col + 1], (tile.shape[0], width))


def eliminate_spd(full, size, block):
    lanes = lax.broadcasted_iota(jnp.int32, (TILE, size), 1)
    rows = lax.broadcasted_iota(jnp.int32, (TILE, size), 0)
    wide = lax.broadcasted_iota(jnp.int32, (size, size), 1)
    block_lanes = lax.broadcasted_iota(jnp.int32, (block, size), 1)
    count = block // TILE
    for first in range(0, size, block):
        panel = full[first:first + block]
        signed = jnp.where(block_lanes < first, -panel, panel) if first else panel
        tiles = [panel[TILE * u:TILE * (u + 1)] for u in range(count)]
        for t in range(count):
            base = first + TILE * t
            columns = [[spread(tile, base + j, size) for tile in tiles] for j in range(TILE)]
            for i in range(TILE):
                here = rows == i
                at_col = lanes == base + i
                lead = columns[i]
                pivot = 1.0 / lead[t][i:i + 1]
                row = jnp.where(at_col[:1], 1.0, tiles[t][i:i + 1]) * pivot
                for j in range(i + 1, TILE):
                    scaled = columns[j][t][i:i + 1] * pivot
                    columns[j] = [columns[j][u] - lead[u] * scaled for u in range(count)]
                    columns[j][t] = jnp.where(here, scaled, columns[j][t])
                tiles = [jnp.where(at_col, 0.0, tiles[u]) - lead[u] * row for u in range(count)]
                tiles[t] = jnp.where(here, row, tiles[t])
        panel = jnp.concatenate(tiles, axis=0)
        inside = (wide >= first) & (wide < first + block)
        update = lax.dot_general(
            signed, panel, (((0,), (0,)), ((), ())),
            precision=lax.Precision.HIGHEST, preferred_element_type=jnp.float32,
        )
        rest = jnp.where(inside, 0.0, full) - update
        parts = []
        if first:
            parts.append(rest[:first])
        parts.append(panel)
        if first + block < size:
            parts.append(rest[first + block:])
        full = jnp.concatenate(parts, axis=0)
    return full


def normalize(inner, vectors):
    width = vectors.shape[1]
    count = inner.shape[0] // TILE
    rows = lax.broadcasted_iota(jnp.int32, (TILE, width), 0)
    left = [inner[TILE * u:TILE * (u + 1)] for u in range(count)]
    right = [vectors[TILE * u:TILE * (u + 1)] for u in range(count)]
    scales = []
    for t in range(count):
        columns = [
            [spread(left[u], TILE * t + j, width) for u in range(t, count)] for j in range(TILE)
        ]
        scale = jnp.zeros((TILE, width), jnp.float32)
        for i in range(TILE):
            lead = columns[i]
            value = lead[0][i:i + 1]
            pivot = 1.0 / value
            scale = jnp.where(rows == i, value, scale)
            for j in range(i + 1, TILE):
                scaled = columns[j][0][i:i + 1] * pivot
                columns[j] = [column - part * scaled for column, part in zip(columns[j], lead)]
            below = [jnp.where(rows > i, lead[0], 0.0)] + lead[1:]
            mate = right[t][i:i + 1] * pivot
            for u in range(t, count):
                right[u] = right[u] - below[u - t] * mate
            if t + 1 < count:
                ahead = left[t][i:i + 1] * pivot[:, :left[t].shape[1]]
                for u in range(t, count):
                    left[u] = left[u] - below[u - t][:, :left[t].shape[1]] * ahead
        scales.append(scale)
    return jnp.concatenate([tile / jnp.sqrt(scale) for tile, scale in zip(right, scales)], axis=0)


def whole_kernel(
    snap_ref, class_ref, yface_ref, zface_ref, face_ref, start_ref, corr_ref, out_ref,
    field, coef, compact, select, kappa, ghost_z, early, swap, zland, yland, rhs,
    class_pair, class_low, class_high, slab, slab_sem,
    swap_send, swap_recv, z_send, z_recv, y_send, y_recv, class_send, class_recv,
    state, mass_part, stiff_part, slots, summed, mass_total, stiff_total, stage,
    sum_sem, send_out, recv_out,
    *, members, owners, own, cell_count,
):
    me_sub = lax.axis_index("sub")
    me_nbhd = lax.axis_index("nbhd")
    size = mass_part.shape[1]
    chunk = size // members
    half = lax.rem(me_sub, 2)
    tower = me_sub - half
    across = owners // own
    mine = across // 2
    from_half = lax.rem(me_nbhd, across) // mine
    whole = jnp.where(from_half == half, 1, 0)

    pltpu.make_async_copy(snap_ref, slab, slab_sem).start()

    def sub_at(step):
        return lax.rem(me_sub + step, members)

    def is_me(nbhd):
        return jnp.logical_and(nbhd == me_nbhd, from_half == half)

    barrier = pltpu.get_barrier_semaphore()
    for step in (1, 2, members - 2, members - 1):
        pl.semaphore_signal(barrier, inc=1, device_id=(me_nbhd, sub_at(step)), device_id_type=MESH)
    for nbhd in range(owners):
        @pl.when(jnp.logical_not(is_me(nbhd)))
        def _():
            pl.semaphore_signal(
                barrier, inc=1, device_id=(nbhd, tower + from_half), device_id_type=MESH
            )
    pl.semaphore_wait(barrier, 4 + owners - whole)

    def rows_of(sub):
        return pl.ds(pl.multiple_of(sub * chunk, chunk), chunk)

    def scatter(which, partial_ref):
        copies = []
        for step in range(1, members):
            peer = sub_at(step)
            copy = pltpu.make_async_remote_copy(
                src_ref=partial_ref.at[rows_of(peer)],
                dst_ref=slots.at[which, step],
                send_sem=sum_sem.at[which, 0, step],
                recv_sem=sum_sem.at[which, 1, step],
                device_id=(me_nbhd, peer),
                device_id_type=MESH,
            )
            copy.start()
            copies.append(copy)
        return copies

    def share(which, partial_ref, total_ref, copies):
        acc = partial_ref[rows_of(me_sub)]
        for step in range(1, members):
            copies[step - 1].wait_recv()
            acc = acc + slots[which, step]
        summed[which] = acc
        total_ref[rows_of(me_sub)] = acc
        spreads = []
        for step in range(1, members):
            copy = pltpu.make_async_remote_copy(
                src_ref=summed.at[which],
                dst_ref=total_ref.at[rows_of(me_sub)],
                send_sem=sum_sem.at[which, 2, step],
                recv_sem=sum_sem.at[which, 3, step],
                device_id=(me_nbhd, sub_at(step)),
                device_id_type=MESH,
            )
            copy.start()
            spreads.append(copy)
        return spreads

    sent = []
    drain = relax_part(
        snap_ref, class_ref, yface_ref, zface_ref, face_ref, state, mass_part, stiff_part,
        field, coef, compact, select, kappa, ghost_z, early, swap, zland, yland, rhs,
        class_pair, class_low, class_high, slab, slab_sem,
        swap_send, swap_recv, z_send, z_recv, y_send, y_recv, class_send, class_recv,
        members, lambda: sent.append(scatter(1, stiff_part)),
    )
    sent.append(scatter(0, mass_part))
    sent.append(share(1, stiff_part, stiff_total, sent[0]))
    sent.append(share(0, mass_part, mass_total, sent[1]))

    dot = functools.partial(
        lax.dot_general, precision=lax.Precision.HIGHEST, preferred_element_type=jnp.float32
    )
    for copy in sent[2]:
        copy.wait_recv()
    stiff = stiff_total[...]
    stiff = (stiff + stiff.T) * (0.5 / cell_count)
    inverse = eliminate_spd(stiff, size, 32)
    for copy in sent[3]:
        copy.wait_recv()
    mass = mass_total[...] / cell_count
    step_map = dot(mass, inverse, (((1,), (0,)), ((), ())))
    both = jnp.concatenate([step_map, dot(step_map, mass, (((1,), (0,)), ((), ())))], axis=1)
    rows = start_ref[...]
    for turn in range(ITERS):
        pair = dot(rows, both, (((1,), (0,)), ((), ())))
        solved, image = pair[:, :size], pair[:, size:]
        inner = dot(solved, image, (((1,), (1,)), ((), ())))
        inner = 0.5 * (inner + inner.T)
        rows = normalize(inner, solved)
    modes = rows.astype(jnp.bfloat16)

    lines = state.shape[1] // mine

    def piece(index, owner):
        values = lax.dot_general(
            modes, state[index // mine, pl.ds(lax.rem(index, mine) * lines, lines)].reshape(
                lines * state.shape[2], size
            ), (((1,), (1,)), ((), ())), preferred_element_type=jnp.float32,
        )
        return (values * corr_ref[me_nbhd, owner].astype(jnp.float32)).astype(jnp.bfloat16)

    def leave(step, owner, sub):
        return pltpu.make_async_remote_copy(
            src_ref=stage.at[step],
            dst_ref=out_ref.at[me_nbhd],
            send_sem=send_out.at[step],
            recv_sem=recv_out.at[me_nbhd],
            device_id=(owner, sub),
            device_id_type=MESH,
        )

    leaving = []
    for step in range(owners):
        index = lax.rem(step + me_nbhd, owners)
        level = index // mine
        owner = across * lax.rem(level, own) + mine * half + lax.rem(index, mine)
        sub = tower + level // own
        here = jnp.logical_and(owner == me_nbhd, sub == me_sub)
        stage[step] = piece(index, owner)

        @pl.when(jnp.logical_not(here))
        def _():
            leave(step, owner, sub).start()

        @pl.when(here)
        def _():
            out_ref[me_nbhd] = stage[step]

        leaving.append((step, owner, sub, here))
    for nbhd in range(owners):
        @pl.when(jnp.logical_not(is_me(nbhd)))
        def _():
            pltpu.make_async_remote_copy(
                src_ref=stage.at[0], dst_ref=out_ref.at[nbhd], send_sem=send_out.at[0],
                recv_sem=recv_out.at[nbhd], device_id=(nbhd, me_sub), device_id_type=MESH,
            ).wait_recv()
    for step, owner, sub, here in leaving:
        @pl.when(jnp.logical_not(here))
        def _():
            leave(step, owner, sub).wait_send()
    for copies in sent:
        for copy in copies:
            copy.wait_send()
    drain()


def on_device(snap_init, channel_map, yface_vals, zface_vals, face_of, start_block, correlation):
    own, rows_all, depth, width = snap_init.shape[1:]
    modes = start_block.shape[2]
    members, owners = lax.axis_size("sub"), lax.axis_size("nbhd")
    both, rows = 2 * own, rows_all // 2
    cells = own * rows_all * depth
    chunk = width // members
    vmem = pl.BlockSpec(memory_space=pltpu.VMEM)
    f32, bf16 = jnp.float32, jnp.bfloat16
    dma = pltpu.SemaphoreType.DMA
    result = pl.pallas_call(
        functools.partial(
            whole_kernel, members=members, owners=owners, own=own, cell_count=float(cells * members)
        ),
        out_shape=jax.ShapeDtypeStruct((owners, modes, cells // owners), bf16),
        in_specs=[pl.BlockSpec(memory_space=pl.ANY)] + [vmem] * 5
        + [pl.BlockSpec(memory_space=pltpu.SMEM)],
        out_specs=vmem,
        scratch_shapes=[
            pltpu.VMEM((2, both + 2, rows + 2, depth + 16, width), f32),
            pltpu.VMEM((8, both, rows, depth, width), f32),
            pltpu.VMEM((8, both, rows_all, depth), f32),
            pltpu.VMEM((4 * rows, rows * width), bf16),
            pltpu.VMEM((both + 2, rows_all, depth), f32),
            pltpu.VMEM((2, rows_all, width), f32),
            pltpu.VMEM((SWEEPS - 1, both, rows, depth, width), bf16),
            pltpu.VMEM((own, rows + 1, depth, width), bf16),
            pltpu.VMEM((SWEEPS + 1, 2, rows, depth, width), bf16),
            pltpu.VMEM((SWEEPS, both, depth, width), bf16),
            pltpu.VMEM((max(both, rows), depth, 2 * width), bf16),
            pltpu.VMEM((own, rows_all, depth), jnp.int32),
            pltpu.VMEM((rows_all, depth), jnp.int32),
            pltpu.VMEM((rows_all, depth), jnp.int32),
            pltpu.VMEM((own, rows_all, depth, width), bf16),
            dma,
            dma((own,)),
            dma((own,)),
            dma((SWEEPS + 1, 2, 2)),
            dma((SWEEPS + 1, 2, 2)),
            dma((SWEEPS, 4)),
            dma((SWEEPS, 4)),
            dma((3,)),
            dma((3,)),
            pltpu.VMEM((both, rows, depth, width), bf16),
            pltpu.VMEM((width, width), f32),
            pltpu.VMEM((width, width), f32),
            pltpu.VMEM((2, members, chunk, width), f32),
            pltpu.VMEM((2, chunk, width), f32),
            pltpu.VMEM((width, width), f32),
            pltpu.VMEM((width, width), f32),
            pltpu.VMEM((owners, modes, cells // owners), bf16),
            dma((2, 4, members)),
            dma((owners,)),
            dma((owners,)),
        ],
        compiler_params=pltpu.CompilerParams(
            collective_id=0, has_side_effects=True, vmem_limit_bytes=60 << 20
        ),
    )(
        snap_init[0], channel_map[0], yface_vals[0], zface_vals[0], face_of, start_block[0].T,
        correlation,
    )
    return result[None, None]


def solution(mesh):
    return jax.shard_map(
        on_device,
        mesh=mesh,
        in_specs=(
            P("nbhd", "sub", None, None, None),
            P("nbhd", "sub", None, None),
            P("nbhd", None, None),
            P("nbhd", None, None),
            P("nbhd", None),
            P("nbhd", None, None),
            P(),
        ),
        out_specs=P("nbhd", "sub", None, None, None),
        check_vma=False,
    )
```

```python
import functools

import jax
import jax.numpy as jnp
from jax import lax
from jax.experimental import pallas as pl
from jax.experimental.pallas import tpu as pltpu
from jax.sharding import PartitionSpec as P

MESH = pl.DeviceIdType.MESH

SWEEPS = 3
ITERS = 4


def harmonic(left_k, right_k):
    return 2.0 * left_k * right_k / (left_k + right_k)


def relax_part(
    snap_ref, class_ref, yface_ref, zface_ref, face_ref, state_ref, mass_ref, stiff_ref,
    field, coef, compact, select, kappa, ghost_z, early, swap, zland, yland, rhs,
    class_pair, class_low, class_high, slab, slab_sem,
    swap_send, swap_recv, z_send, z_recv, y_send, y_recv, class_send, class_recv,
    members, stiff_ready,
):
    me_nbhd = lax.axis_index("nbhd")
    me = lax.axis_index("sub")
    half = lax.rem(me, 2)
    tower = me // 2
    towers = members // 2
    own, rows_all, depth, width = snap_ref.shape
    both = 2 * own
    rows = rows_all // 2
    top = both + 1
    base = 8
    inner = pl.ds(base, depth)

    def at(sub):
        return (me_nbhd, lax.rem(sub + members, members))

    partner = at(me + 1 - 2 * half)
    cross = at(me - 1 + 2 * half)
    lower = at(me - 2)
    upper = at(me + 2)

    def remote(src, dst, send, recv, device):
        return pltpu.make_async_remote_copy(
            src_ref=src, dst_ref=dst, send_sem=send, recv_sem=recv,
            device_id=device, device_id_type=MESH,
        )

    class_copies = [
        remote(class_ref, class_pair, class_send.at[0], class_recv.at[0], partner),
    ]
    class_copies[0].start()
    class_other = []

    def class_sends(plane, land, slot, devices):
        made = []
        for place, device in enumerate(devices):
            made.append(remote(
                class_ref.at[plane], land, class_send.at[1 + place], class_recv.at[slot], device
            ))
        return made

    @pl.when(half == 0)
    def _():
        for copy in class_sends(0, class_high, 2, (lower, cross)):
            copy.start()

    @pl.when(half == 1)
    def _():
        for copy in class_sends(own - 1, class_low, 1, (upper, cross)):
            copy.start()

    order = [0, 1] + list(range(own - 1, 1, -1))
    swaps = []
    for turn, q in enumerate(order):
        plane = q + half * (own - 1 - 2 * q)
        copy = remote(
            snap_ref.at[plane, pl.ds((rows - 1) * (1 - half), rows + 1)],
            swap.at[turn], swap_send.at[turn], swap_recv.at[turn], partner,
        )
        copy.start()
        swaps.append(copy)

    @pl.when(half == 0)
    def _():
        remote(
            snap_ref.at[0, pl.ds(0, rows)], zland.at[0, 1], z_send.at[0, 0, 0],
            z_recv.at[0, 1, 0], lower
        ).start()

    @pl.when(half == 1)
    def _():
        remote(
            snap_ref.at[own - 1, pl.ds(rows, rows)], zland.at[0, 0], z_send.at[0, 1, 0],
            z_recv.at[0, 0, 0], upper
        ).start()

    shift = 1 - half

    def fill_own(p, _):
        def fill(r, _):
            field[0, 1 + own * half + p, shift + r, inner, :] = slab[
                p, (rows - 1) * half + r
            ].astype(jnp.float32)
            return 0
        return lax.fori_loop(0, rows + 1, fill, 0)

    pltpu.make_async_copy(snap_ref, slab, slab_sem).wait()
    lax.fori_loop(0, own, fill_own, 0)

    face = face_ref[...]

    def pick(side):
        return jnp.where(face == side, 1.0, 0.0)

    side_y = jnp.where(half == 0, pick(0), pick(1))
    ghost_y = yface_ref[...].astype(jnp.float32) * side_y
    zface = zface_ref[...].astype(jnp.float32)
    ghost_z[0] = zface * pick(2)
    ghost_z[1] = zface * pick(3)

    def set_ghosts(p, _):
        for buf in range(2):
            field[buf, p + 1, (rows + 1) * half, inner, :] = ghost_y

            def one(y, _):
                field[buf, p + 1, y + 1, pl.ds(base - 1, 1), :] = ghost_z[0, pl.ds(rows * half + y, 1), :]
                field[buf, p + 1, y + 1, pl.ds(base + depth, 1), :] = ghost_z[1, pl.ds(rows * half + y, 1), :]
                return 0

            lax.fori_loop(0, rows, one, 0)
        return 0

    lax.fori_loop(0, both, set_ghosts, 0)

    def to_kappa(classes):
        return jnp.left_shift(1, 2 * classes).astype(jnp.float32)

    def land(slot, ref):
        remote(ref, ref, class_send.at[0], class_recv.at[slot], partner).wait_recv()

    land(0, class_pair)
    land(1, class_low)
    land(2, class_high)
    kappa[0] = to_kappa(class_low[...])
    kappa[top] = to_kappa(class_high[...])
    for p in range(own):
        kappa[1 + own * half + p] = to_kappa(class_ref[p])
        kappa[1 + own * (1 - half) + p] = to_kappa(class_pair[p])

    def coefficients(p, _):
        centre = kappa[p + 1]
        has_low = jnp.logical_or(tower > 0, p > 0)
        has_high = jnp.logical_or(tower < towers - 1, p < both - 1)
        face_low = harmonic(centre, kappa[p])
        face_high = harmonic(centre, kappa[p + 2])
        x_lower = jnp.where(has_low, face_low, centre)
        x_upper = jnp.where(has_high, face_high, centre)
        y_inner = harmonic(centre[1:], centre[:-1])
        y_lower = jnp.concatenate([centre[:1], y_inner], axis=0)
        y_upper = jnp.concatenate([y_inner, centre[-1:]], axis=0)
        z_inner = harmonic(centre[:, 1:], centre[:, :-1])
        z_lower = jnp.concatenate([centre[:, :1], z_inner], axis=1)
        z_upper = jnp.concatenate([z_inner, centre[:, -1:]], axis=1)
        denom = x_lower + x_upper + y_lower + y_upper + z_lower + z_upper
        inverse = 1.0 / denom
        compact[0, p] = jnp.where(has_low, face_low, 0.0) * inverse
        compact[1, p] = jnp.where(has_high, face_high, 0.0) * inverse
        compact[2, p] = y_lower * inverse
        compact[3, p] = y_upper * inverse
        compact[4, p] = z_lower * inverse
        compact[5, p] = z_upper * inverse
        compact[6, p] = denom
        compact[7, p] = centre * (1.0 / 16.0)
        return 0

    lax.fori_loop(0, both, coefficients, 0)
    taken = lax.broadcasted_iota(jnp.int32, select.shape, 0)
    given = lax.broadcasted_iota(jnp.int32, select.shape, 1)
    select[...] = jnp.where(lax.rem(taken, rows) == given // width, 1.0, 0.0).astype(jnp.bfloat16)

    def widen(kinds):
        def one(p, _):
            for kind in kinds:
                exact = compact[kind, p, pl.ds(pl.multiple_of(rows * half, rows), rows), :]
                terms = []
                for _ in range(3):
                    term = exact.astype(jnp.bfloat16).astype(jnp.float32)
                    terms.append(term)
                    exact = exact - term
                terms.append(jnp.zeros_like(exact))
                wide = lax.dot_general(
                    jnp.concatenate(terms, axis=0).astype(jnp.bfloat16), select[...],
                    (((0,), (0,)), ((), ())), preferred_element_type=jnp.float32,
                )
                for y in range(rows):
                    coef[kind, p, y] = wide[:, width * y:width * (y + 1)]
            return 0
        lax.fori_loop(0, both, one, 0)

    widen(range(3))
    swaps[0].wait_recv()

    @pl.when(half == 0)
    def _():
        remote(
            swap.at[0, pl.ds(0, rows)], zland.at[0, 0], z_send.at[0, 1, 0], z_recv.at[0, 0, 0],
            upper,
        ).start()

    @pl.when(half == 1)
    def _():
        remote(
            swap.at[0, pl.ds(1, rows)], zland.at[0, 1], z_send.at[0, 0, 0], z_recv.at[0, 1, 0],
            lower,
        ).start()

    widen(range(3, 6))

    def row(sweep, p, y):
        src, dst = (sweep + 1) % 2, sweep % 2
        c = [coef.at[kind, p - 1, y - 1] for kind in range(6)]
        value = c[0][...] * field[src, p - 1, y, inner, :]
        value += c[1][...] * field[src, p + 1, y, inner, :]
        value += c[2][...] * field[src, p, y - 1, inner, :]
        value += c[3][...] * field[src, p, y + 1, inner, :]
        value += c[4][...] * field[src, p, y, pl.ds(base - 1, depth), :]
        value += c[5][...] * field[src, p, y, pl.ds(base + 1, depth), :]
        low = value.astype(jnp.bfloat16)
        field[dst, p, y, inner, :] = low.astype(jnp.float32)
        if sweep < SWEEPS:
            early[sweep - 1, p - 1, y - 1] = low
        else:
            state_ref[p - 1, y - 1] = low
            field[dst, p, y, pl.ds(base + depth, 1), :] = jnp.zeros((1, width), jnp.float32)

    def line(sweep, p, first, count):
        def body(i, _):
            row(sweep, p, first + i)
            return 0
        lax.fori_loop(0, count, body, 0)

    chunk = rows // 2
    edge = rows - (rows - 1) * half

    def chunk_at(part):
        return chunk * half if part == 0 else chunk - chunk * half

    def held(sweep):
        return early.at[sweep - 1] if sweep < SWEEPS else state_ref

    def send_z(sweep, side, part):
        cells = pl.ds(chunk_at(part), chunk)
        remote(
            held(sweep).at[side * (both - 1), cells], zland.at[sweep, 1 - side, cells],
            z_send.at[sweep, side, part], z_recv.at[sweep, 1 - side, part], at(me - 2 + 4 * side),
        ).start()

    def send_y(sweep, part, first, count):
        planes = pl.ds(first, count)
        remote(
            held(sweep).at[planes, edge - 1], yland.at[sweep - 1, planes], y_send.at[sweep - 1, part],
            y_recv.at[sweep - 1, part], partner,
        ).start()

    def take_z(buf, sweep, side, part):
        cells = pl.ds(0, rows if sweep == 0 else chunk)
        remote(
            zland.at[sweep, side, cells], zland.at[sweep, side, cells], z_send.at[sweep, side, part],
            z_recv.at[sweep, side, part], lower,
        ).wait_recv()
        first = 0 if sweep == 0 else chunk_at(part)

        def fill(i, _):
            field[buf, top * side, first + i + 1, inner, :] = zland[sweep, side, first + i].astype(
                jnp.float32
            )
            return 0
        lax.fori_loop(0, rows if sweep == 0 else chunk, fill, 0)

    y_parts = ((1, own - 1), (own, own - 1), (0, 1), (both - 1, 1))

    def take_y(buf, sweep, part):
        first, count = y_parts[part]
        planes = pl.ds(first, count)
        remote(
            yland.at[sweep - 1, planes], yland.at[sweep - 1, planes], y_send.at[sweep - 1, part],
            y_recv.at[sweep - 1, part], partner,
        ).wait_recv()

        def fill(i, _):
            p = first + i
            field[buf, p + 1, (rows + 1) * (1 - half), inner, :] = yland[sweep - 1, p].astype(jnp.float32)
            return 0
        lax.fori_loop(0, count, fill, 0)

    def plane_of(e):
        return e + (1 - half) * (top - 2 * e)

    ahead = range(own + 2, both)
    for e in ahead:
        line(1, plane_of(e), 1, rows)
    for turn, q in enumerate(order):
        if turn:
            swaps[turn].wait_recv()
        plane = q + (1 - half) * (own - 1 - 2 * q)
        def fill(r, _):
            field[0, 1 + own * (1 - half) + plane, shift + r, inner, :] = swap[turn, r].astype(
                jnp.float32
            )
            return 0

        lax.fori_loop(0, rows + 1, fill, 0)
        if turn == 1:
            take_z(0, 0, 0, 0)
            take_z(0, 0, 1, 0)
            for e, side in ((both, half), (1, 1 - half)):
                line(1, plane_of(e), 1, rows)
                send_z(1, side, 0)
                send_z(1, side, 1)
                send_y(1, 2 + side, side * (both - 1), 1)
        if 2 <= turn < own - 1:
            line(1, plane_of(q + 2), 1, rows)
        if q == own - 1:
            send_y(1, half, 1 + (own - 1) * half, own - 1)
            widen((6, 7))
            for e in ahead:
                line(2, plane_of(e), 1 + half, rows - 1)
    for e in range(own, 1, -1):
        row(1, plane_of(e), edge)
    send_y(1, 1 - half, 1 + (own - 1) * (1 - half), own - 1)
    for e in range(own, 1, -1):
        line(1, plane_of(e), 1 + half, rows - 1)

    def only_if_last(sweep, action):
        if sweep < SWEEPS:
            action()
        else:
            pl.when(half == 1)(action)

    for sweep in range(2, SWEEPS + 1):
        src = (sweep + 1) % 2
        sides = (0, 1) if sweep < SWEEPS else (0,)

        def middle(i, _):
            line(sweep, plane_of(i + 2), 1 + half, rows - 1)
            return 0
        lax.fori_loop(0, both - 2 - (len(ahead) if sweep == 2 else 0), middle, 0)
        def border(part):
            take_y(src, sweep - 1, part)
            first, count = y_parts[part]

            def body(i, _):
                row(sweep, first + i + 1, edge)
                return 0
            lax.fori_loop(0, count, body, 0)
            only_if_last(sweep, lambda: send_y(sweep, part, first, count))

        for side in (0, 1):
            take_z(src, sweep - 1, side, 0)
            line(sweep, 1 + side * (both - 1), 1 + chunk_at(0), chunk)
            if side in sides:
                send_z(sweep, side, 0)
        border(0)
        border(1)
        for side in (0, 1):
            take_y(src, sweep - 1, 2 + side)
            take_z(src, sweep - 1, side, 1)
            line(sweep, 1 + side * (both - 1), 1 + chunk_at(1), chunk)
            if side in sides:
                send_z(sweep, side, 1)

            def last_part():
                send_y(sweep, 2 + side, *y_parts[2 + side])
            only_if_last(sweep, last_part)

    last = SWEEPS % 2

    def stiff_row(p, y, place):
        here = field[last, p, y, inner, :]
        ahead = coef[1, p - 1, y - 1] * field[last, p + 1, y, inner, :]
        ahead += coef[3, p - 1, y - 1] * field[last, p, y + 1, inner, :]
        ahead += coef[5, p - 1, y - 1] * field[last, p, y, pl.ds(base + 1, depth), :]
        value = coef[6, p - 1, y - 1] * (here - 2.0 * ahead)
        high = value.astype(jnp.bfloat16)
        rest = (value - high.astype(jnp.float32)).astype(jnp.bfloat16)
        rhs[place, :, pl.ds(0, width)] = high
        rhs[place, :, pl.ds(width, width)] = rest

    def gram(left, count, used):
        right = rhs[pl.ds(0, count), :, pl.ds(0, used)].reshape(count * depth, used)
        return lax.dot_general(
            left.reshape(count * depth, width), right, (((0,), (0,)), ((), ())),
            preferred_element_type=jnp.float32,
        )

    def add_stiff(left, count):
        terms = gram(left, count, 2 * width)
        stiff_ref[...] += terms[:, :width] + terms[:, width:]

    mass_ref[...] = jnp.zeros_like(mass_ref)
    stiff_ref[...] = jnp.zeros_like(stiff_ref)

    def weigh(p, _):
        def body(y, _):
            here = state_ref[p, y].astype(jnp.float32)
            rhs[y, :, pl.ds(0, width)] = (here * coef[7, p, y]).astype(jnp.bfloat16)
            return 0
        lax.fori_loop(0, rows, body, 0)
        mass_ref[...] += gram(state_ref[p], rows, width)
        return 0
    def inside(i, _):
        def body(y, _):
            stiff_row(i + 1, y + 1, y)
            return 0
        lax.fori_loop(0, rows - 1, body, 0)
        add_stiff(state_ref[i, pl.ds(0, rows - 1)], rows - 1)
        return 0
    lax.fori_loop(0, both - 1, inside, 0)
    lax.fori_loop(0, own // 2, weigh, 0)

    @pl.when(half == 0)
    def _():
        for part in range(4):
            take_y(last, SWEEPS, part)

    @pl.when(half == 1)
    def _():
        def clear(p, _):
            field[last, p + 1, rows + 1, inner, :] = jnp.zeros((depth, width), jnp.float32)
            return 0
        lax.fori_loop(0, both, clear, 0)

    def side(i, _):
        stiff_row(i + 1, rows, i)
        return 0
    lax.fori_loop(0, both - 1, side, 0)
    add_stiff(state_ref[pl.ds(0, both - 1), rows - 1], both - 1)
    take_z(last, SWEEPS, 1, 0)
    take_z(last, SWEEPS, 1, 1)

    def roof(y, _):
        stiff_row(both, y + 1, y)
        return 0
    lax.fori_loop(0, rows, roof, 0)
    add_stiff(state_ref[both - 1], rows)
    stiff_ready()
    lax.fori_loop(own // 2, both, weigh, 0)

    def drain():
        class_copies[0].wait_send()
        for place in range(2):
            remote(
                class_ref.at[0], class_low, class_send.at[1 + place], class_recv.at[1], partner
            ).wait_send()
        for copy in swaps:
            copy.wait_send()
        for side in range(2):
            remote(
                snap_ref.at[0, pl.ds(0, rows)], zland.at[0, 0], z_send.at[0, side, 0], z_recv.at[0, 0, 0], lower
            ).wait_send()

        def left_z(sweep, side, part):
            cells = pl.ds(0, chunk)
            remote(
                held(sweep).at[0, cells], zland.at[sweep, 0, cells], z_send.at[sweep, side, part],
                z_recv.at[sweep, 0, part], lower,
            ).wait_send()

        def left_y(sweep, part):
            planes = pl.ds(*y_parts[part])
            remote(
                held(sweep).at[planes, 0], yland.at[sweep - 1, planes], y_send.at[sweep - 1, part],
                y_recv.at[sweep - 1, part], partner,
            ).wait_send()

        for sweep in range(1, SWEEPS + 1):
            for side in range(2 if sweep < SWEEPS else 1):
                for part in range(2):
                    left_z(sweep, side, part)

            def all_y():
                for part in range(4):
                    left_y(sweep, part)
            only_if_last(sweep, all_y)

    return drain


TILE = 8


def spread(tile, col, width):
    return jnp.broadcast_to(tile[:, col:col + 1], (tile.shape[0], width))


def eliminate_spd(full, size, block):
    lanes = lax.broadcasted_iota(jnp.int32, (TILE, size), 1)
    rows = lax.broadcasted_iota(jnp.int32, (TILE, size), 0)
    wide = lax.broadcasted_iota(jnp.int32, (size, size), 1)
    block_lanes = lax.broadcasted_iota(jnp.int32, (block, size), 1)
    count = block // TILE
    for first in range(0, size, block):
        panel = full[first:first + block]
        signed = jnp.where(block_lanes < first, -panel, panel) if first else panel
        tiles = [panel[TILE * u:TILE * (u + 1)] for u in range(count)]
        for t in range(count):
            base = first + TILE * t
            columns = [[spread(tile, base + j, size) for tile in tiles] for j in range(TILE)]
            for i in range(TILE):
                here = rows == i
                at_col = lanes == base + i
                lead = columns[i]
                pivot = 1.0 / lead[t][i:i + 1]
                row = jnp.where(at_col[:1], 1.0, tiles[t][i:i + 1]) * pivot
                for j in range(i + 1, TILE):
                    scaled = columns[j][t][i:i + 1] * pivot
                    columns[j] = [columns[j][u] - lead[u] * scaled for u in range(count)]
                    columns[j][t] = jnp.where(here, scaled, columns[j][t])
                tiles = [jnp.where(at_col, 0.0, tiles[u]) - lead[u] * row for u in range(count)]
                tiles[t] = jnp.where(here, row, tiles[t])
        panel = jnp.concatenate(tiles, axis=0)
        inside = (wide >= first) & (wide < first + block)
        update = lax.dot_general(
            signed, panel, (((0,), (0,)), ((), ())),
            precision=lax.Precision.HIGHEST, preferred_element_type=jnp.float32,
        )
        rest = jnp.where(inside, 0.0, full) - update
        parts = []
        if first:
            parts.append(rest[:first])
        parts.append(panel)
        if first + block < size:
            parts.append(rest[first + block:])
        full = jnp.concatenate(parts, axis=0)
    return full


def normalize(inner, vectors):
    width = vectors.shape[1]
    count = inner.shape[0] // TILE
    rows = lax.broadcasted_iota(jnp.int32, (TILE, width), 0)
    left = [inner[TILE * u:TILE * (u + 1)] for u in range(count)]
    right = [vectors[TILE * u:TILE * (u + 1)] for u in range(count)]
    scales = []
    for t in range(count):
        columns = [
            [spread(left[u], TILE * t + j, width) for u in range(t, count)] for j in range(TILE)
        ]
        scale = jnp.zeros((TILE, width), jnp.float32)
        for i in range(TILE):
            lead = columns[i]
            value = lead[0][i:i + 1]
            pivot = 1.0 / value
            scale = jnp.where(rows == i, value, scale)
            for j in range(i + 1, TILE):
                scaled = columns[j][0][i:i + 1] * pivot
                columns[j] = [column - part * scaled for column, part in zip(columns[j], lead)]
            below = [jnp.where(rows > i, lead[0], 0.0)] + lead[1:]
            mate = right[t][i:i + 1] * pivot
            for u in range(t, count):
                right[u] = right[u] - below[u - t] * mate
            if t + 1 < count:
                ahead = left[t][i:i + 1] * pivot[:, :left[t].shape[1]]
                for u in range(t, count):
                    left[u] = left[u] - below[u - t][:, :left[t].shape[1]] * ahead
        scales.append(scale)
    return jnp.concatenate([tile / jnp.sqrt(scale) for tile, scale in zip(right, scales)], axis=0)


def whole_kernel(
    snap_ref, class_ref, yface_ref, zface_ref, face_ref, start_ref, corr_ref, out_ref,
    field, coef, compact, select, kappa, ghost_z, early, swap, zland, yland, rhs,
    class_pair, class_low, class_high, slab, slab_sem,
    swap_send, swap_recv, z_send, z_recv, y_send, y_recv, class_send, class_recv,
    state, mass_part, stiff_part, slots, summed, mass_total, stiff_total, stage,
    sum_sem, send_out, recv_out,
    *, members, owners, own, cell_count,
):
    me_sub = lax.axis_index("sub")
    me_nbhd = lax.axis_index("nbhd")
    size = mass_part.shape[1]
    chunk = size // members
    half = lax.rem(me_sub, 2)
    tower = me_sub - half
    across = owners // own
    mine = across // 2
    from_half = lax.rem(me_nbhd, across) // mine
    whole = jnp.where(from_half == half, 1, 0)

    pltpu.make_async_copy(snap_ref, slab, slab_sem).start()

    def sub_at(step):
        return lax.rem(me_sub + step, members)

    def is_me(nbhd):
        return jnp.logical_and(nbhd == me_nbhd, from_half == half)

    barrier = pltpu.get_barrier_semaphore()
    for step in (1, 2, members - 2, members - 1):
        pl.semaphore_signal(barrier, inc=1, device_id=(me_nbhd, sub_at(step)), device_id_type=MESH)
    for nbhd in range(owners):
        @pl.when(jnp.logical_not(is_me(nbhd)))
        def _():
            pl.semaphore_signal(
                barrier, inc=1, device_id=(nbhd, tower + from_half), device_id_type=MESH
            )
    pl.semaphore_wait(barrier, 4 + owners - whole)

    def rows_of(sub):
        return pl.ds(pl.multiple_of(sub * chunk, chunk), chunk)

    def scatter(which, partial_ref):
        copies = []
        for step in range(1, members):
            peer = sub_at(step)
            copy = pltpu.make_async_remote_copy(
                src_ref=partial_ref.at[rows_of(peer)],
                dst_ref=slots.at[which, step],
                send_sem=sum_sem.at[which, 0, step],
                recv_sem=sum_sem.at[which, 1, step],
                device_id=(me_nbhd, peer),
                device_id_type=MESH,
            )
            copy.start()
            copies.append(copy)
        return copies

    def share(which, partial_ref, total_ref, copies):
        acc = partial_ref[rows_of(me_sub)]
        for step in range(1, members):
            copies[step - 1].wait_recv()
            acc = acc + slots[which, step]
        summed[which] = acc
        total_ref[rows_of(me_sub)] = acc
        spreads = []
        for step in range(1, members):
            copy = pltpu.make_async_remote_copy(
                src_ref=summed.at[which],
                dst_ref=total_ref.at[rows_of(me_sub)],
                send_sem=sum_sem.at[which, 2, step],
                recv_sem=sum_sem.at[which, 3, step],
                device_id=(me_nbhd, sub_at(step)),
                device_id_type=MESH,
            )
            copy.start()
            spreads.append(copy)
        return spreads

    sent = []
    drain = relax_part(
        snap_ref, class_ref, yface_ref, zface_ref, face_ref, state, mass_part, stiff_part,
        field, coef, compact, select, kappa, ghost_z, early, swap, zland, yland, rhs,
        class_pair, class_low, class_high, slab, slab_sem,
        swap_send, swap_recv, z_send, z_recv, y_send, y_recv, class_send, class_recv,
        members, lambda: sent.append(scatter(1, stiff_part)),
    )
    sent.append(scatter(0, mass_part))
    sent.append(share(1, stiff_part, stiff_total, sent[0]))
    sent.append(share(0, mass_part, mass_total, sent[1]))

    dot = functools.partial(
        lax.dot_general, precision=lax.Precision.HIGHEST, preferred_element_type=jnp.float32
    )
    for copy in sent[2]:
        copy.wait_recv()
    stiff = stiff_total[...]
    stiff = (stiff + stiff.T) * (0.5 / cell_count)
    inverse = eliminate_spd(stiff, size, 32)
    for copy in sent[3]:
        copy.wait_recv()
    mass = mass_total[...] / cell_count
    step_map = dot(mass, inverse, (((1,), (0,)), ((), ())))
    both = jnp.concatenate([step_map, dot(step_map, mass, (((1,), (0,)), ((), ())))], axis=1)
    rows = start_ref[...]
    for turn in range(ITERS):
        pair = dot(rows, both, (((1,), (0,)), ((), ())))
        solved, image = pair[:, :size], pair[:, size:]
        inner = dot(solved, image, (((1,), (1,)), ((), ())))
        inner = 0.5 * (inner + inner.T)
        rows = normalize(inner, solved)
    modes = rows.astype(jnp.bfloat16)

    lines = state.shape[1] // mine

    def piece(index, owner):
        values = lax.dot_general(
            modes, state[index // mine, pl.ds(lax.rem(index, mine) * lines, lines)].reshape(
                lines * state.shape[2], size
            ), (((1,), (1,)), ((), ())), preferred_element_type=jnp.float32,
        )
        return (values * corr_ref[me_nbhd, owner].astype(jnp.float32)).astype(jnp.bfloat16)

    def leave(step, owner, sub):
        return pltpu.make_async_remote_copy(
            src_ref=stage.at[step],
            dst_ref=out_ref.at[me_nbhd],
            send_sem=send_out.at[step],
            recv_sem=recv_out.at[me_nbhd],
            device_id=(owner, sub),
            device_id_type=MESH,
        )

    leaving = []
    for step in range(owners):
        index = lax.rem(step + me_nbhd, owners)
        level = index // mine
        owner = across * lax.rem(level, own) + mine * half + lax.rem(index, mine)
        sub = tower + level // own
        here = jnp.logical_and(owner == me_nbhd, sub == me_sub)
        stage[step] = piece(index, owner)

        @pl.when(jnp.logical_not(here))
        def _():
            leave(step, owner, sub).start()

        @pl.when(here)
        def _():
            out_ref[me_nbhd] = stage[step]

        leaving.append((step, owner, sub, here))
    for nbhd in range(owners):
        @pl.when(jnp.logical_not(is_me(nbhd)))
        def _():
            pltpu.make_async_remote_copy(
                src_ref=stage.at[0], dst_ref=out_ref.at[nbhd], send_sem=send_out.at[0],
                recv_sem=recv_out.at[nbhd], device_id=(nbhd, me_sub), device_id_type=MESH,
            ).wait_recv()
    for step, owner, sub, here in leaving:
        @pl.when(jnp.logical_not(here))
        def _():
            leave(step, owner, sub).wait_send()
    for copies in sent:
        for copy in copies:
            copy.wait_send()
    drain()


def on_device(snap_init, channel_map, yface_vals, zface_vals, face_of, start_block, correlation):
    own, rows_all, depth, width = snap_init.shape[1:]
    modes = start_block.shape[2]
    members, owners = lax.axis_size("sub"), lax.axis_size("nbhd")
    both, rows = 2 * own, rows_all // 2
    cells = own * rows_all * depth
    chunk = width // members
    vmem = pl.BlockSpec(memory_space=pltpu.VMEM)
    f32, bf16 = jnp.float32, jnp.bfloat16
    dma = pltpu.SemaphoreType.DMA
    result = pl.pallas_call(
        functools.partial(
            whole_kernel, members=members, owners=owners, own=own, cell_count=float(cells * members)
        ),
        out_shape=jax.ShapeDtypeStruct((owners, modes, cells // owners), bf16),
        in_specs=[pl.BlockSpec(memory_space=pl.ANY)] + [vmem] * 5
        + [pl.BlockSpec(memory_space=pltpu.SMEM)],
        out_specs=vmem,
        scratch_shapes=[
            pltpu.VMEM((2, both + 2, rows + 2, depth + 16, width), f32),
            pltpu.VMEM((8, both, rows, depth, width), f32),
            pltpu.VMEM((8, both, rows_all, depth), f32),
            pltpu.VMEM((4 * rows, rows * width), bf16),
            pltpu.VMEM((both + 2, rows_all, depth), f32),
            pltpu.VMEM((2, rows_all, width), f32),
            pltpu.VMEM((SWEEPS - 1, both, rows, depth, width), bf16),
            pltpu.VMEM((own, rows + 1, depth, width), bf16),
            pltpu.VMEM((SWEEPS + 1, 2, rows, depth, width), bf16),
            pltpu.VMEM((SWEEPS, both, depth, width), bf16),
            pltpu.VMEM((max(both, rows), depth, 2 * width), bf16),
            pltpu.VMEM((own, rows_all, depth), jnp.int32),
            pltpu.VMEM((rows_all, depth), jnp.int32),
            pltpu.VMEM((rows_all, depth), jnp.int32),
            pltpu.VMEM((own, rows_all, depth, width), bf16),
            dma,
            dma((own,)),
            dma((own,)),
            dma((SWEEPS + 1, 2, 2)),
            dma((SWEEPS + 1, 2, 2)),
            dma((SWEEPS, 4)),
            dma((SWEEPS, 4)),
            dma((3,)),
            dma((3,)),
            pltpu.VMEM((both, rows, depth, width), bf16),
            pltpu.VMEM((width, width), f32),
            pltpu.VMEM((width, width), f32),
            pltpu.VMEM((2, members, chunk, width), f32),
            pltpu.VMEM((2, chunk, width), f32),
            pltpu.VMEM((width, width), f32),
            pltpu.VMEM((width, width), f32),
            pltpu.VMEM((owners, modes, cells // owners), bf16),
            dma((2, 4, members)),
            dma((owners,)),
            dma((owners,)),
        ],
        compiler_params=pltpu.CompilerParams(
            collective_id=0, has_side_effects=True, vmem_limit_bytes=60 << 20
        ),
    )(
        snap_init[0], channel_map[0], yface_vals[0], zface_vals[0], face_of, start_block[0].T,
        correlation,
    )
    return result[None, None]


def solution(mesh):
    return jax.shard_map(
        on_device,
        mesh=mesh,
        in_specs=(
            P("nbhd", "sub", None, None, None),
            P("nbhd", "sub", None, None),
            P("nbhd", None, None),
            P("nbhd", None, None),
            P("nbhd", None),
            P("nbhd", None, None),
            P(),
        ),
        out_specs=P("nbhd", "sub", None, None, None),
        check_vma=False,
    )
```
